32 devices in a mesh: dp: 8 (over y, x, core), tensor: 4 (over z).
Axes of the slice: x: 2, y: 2, z: 4, core: 2. Of those that a mesh axis runs over, the one named last changes fastest.
Arguments:
- tokens: bfloat16 [16, 2048, 768], P('dp', 'tensor'), may hold values from -6 to 6
- segments: int32 [16, 2048], P('dp'), may hold values from 0 to 3, never falling along the last dimension, each value on 1 to 800 neighbouring positions
- pairing: int32 [12, 4], P('tensor'), may hold values from 0 to 3, each once within a row
- qkv_weight: bfloat16 [768, 12, 192], P('dp', 'tensor'), may hold values from -0.3125 to 0.3125
- qv_bias: bfloat16 [12, 128], P('tensor'), may hold values from -3 to 3
- out_weight: bfloat16 [12, 64, 768], P('tensor', None, 'dp'), may hold values from -0.875 to 0.875
- out_bias: bfloat16 [768], replicated, may hold values from -3 to 3
- first_gain: bfloat16 [768], replicated, may hold values from 0.5 to 1.5
- first_shift: bfloat16 [768], replicated, may hold values from -2 to 2
- up_weight: bfloat16 [768, 3072], P('dp', 'tensor'), may hold values from -0.21875 to 0.21875
- up_bias: bfloat16 [3072], P('tensor'), may hold values from -3 to 3
- down_weight: bfloat16 [3072, 768], P('tensor', 'dp'), may hold values from -0.109375 to 0.109375
- down_bias: bfloat16 [768], replicated, may hold values from -3 to 3
- second_gain: bfloat16 [768], replicated, may hold values from 0.5 to 1.5
- second_shift: bfloat16 [768], replicated, may hold values from -2 to 2
- cotangent: bfloat16 [16, 2048, 768], P('dp', 'tensor'), may hold values from -6 to 6
Outputs:
- layer_out: bfloat16 [16, 2048, 768], P('dp', 'tensor')
- input_grad: bfloat16 [16, 2048, 768], P('dp', 'tensor')
- qkv_weight_grad: float32 [768, 12, 192], P('dp', 'tensor')
- qv_bias_grad: float32 [12, 128], P('tensor')
- out_weight_grad: float32 [12, 64, 768], P('tensor', None, 'dp')
- out_bias_grad: float32 [768], replicated
- first_gain_grad: float32 [768], replicated
- first_shift_grad: float32 [768], replicated
- up_weight_grad: float32 [768, 3072], P('dp', 'tensor')
- up_bias_grad: float32 [3072], P('tensor')
- down_weight_grad: float32 [3072, 768], P('tensor', 'dp')
- down_bias_grad: float32 [768], replicated
- second_gain_grad: float32 [768], replicated
- second_shift_grad: float32 [768], replicated
The draws below stay inside these ranges and needn't reach their ends.
Inputs may be any that keep to these rules, and one draw needn't show every extreme that they name: `segments`: along each sequence the numbers never fall; each number covers at most 800 positions of its sequence, and one covers exactly 800. `pairing`: each row holds every number from 0 to 3 once.
All inputs are finite; a program needn't handle non-finite values.
Results may differ from the reference program's by a relative error of at most 0.013.
Values may be sent and summed in bfloat16 or wider, within the bound.
No kernel may reach another device: no remote copies, remote signals or barrier semaphores. Data moves between devices by JAX's collectives and lax.ppermute only.
A program may use at most 192 MiB of HBM per device.

```python
import math
import jax
import jax.numpy as jnp
import numpy as np
from jax import lax

D = 768
HEADS = 12
HD = 64
FF = 3072
SEQ_LEN = 2048
NBLK = 4
BLOCK = 512
DOCS = 4
DOC_MOST = 800
SEQS = 16


def strengthened(result, own_key, source, target, shards_of, factor):
    def block_of(dim):
        return (jnp.arange(result.shape[dim]) // (result.shape[dim] // shards_of)).reshape((-1,) + (1,) * (result.ndim - 1 - dim))

    one_side = jax.random.permutation(own_key, shards_of)[block_of(target)]
    far = (block_of(target) + shards_of // 2) % shards_of
    return jnp.where((block_of(source) == one_side) | (block_of(source) == far), factor * result, result)


def level_of(rng, dims, cuts, low, high):
    def one(position, blocks):
        heights = jax.random.uniform(jax.random.fold_in(jax.random.fold_in(rng, 6), position), (blocks,), jnp.float32, low / len(cuts), high / len(cuts))
        return jnp.repeat(jnp.exp(heights), dims[position] // blocks).reshape((-1,) + (1,) * (len(dims) - position - 1))

    gain = one(*cuts[0])
    for cut in cuts[1:]:
        gain = gain * one(*cut)
    return gain


def split_up(count, total, reach, slope):
    loads = [(1 << 20) // math.isqrt(standing ** slope) + 1 for standing in range(2, count + 1)]
    rest, given = total - reach - (count - 1), [1] * (count - 1)
    while rest > 0:
        movable = [i for i in range(count - 1) if given[i] < reach]
        pool, budget = sum([loads[i] for i in movable]), rest
        for i in movable:
            more = min(reach - given[i], max(1, budget * loads[i] // pool), rest)
            given[i] = given[i] + more
            rest = rest - more
    return np.array([reach] + given)


def ragged(rng, count, total, reach, skew):
    if count == 2:
        one = jax.random.randint(rng, (), max(1, total - reach), min(reach, total - 1) + 1)
        return jnp.stack([one, total - one])
    lengths = jnp.asarray(split_up(count, total, reach, skew), jnp.int32)
    pairs = (count - 1) // 2
    donor, taker = lengths[1:1 + 2 * pairs:2], lengths[2:2 + 2 * pairs:2]
    margin = jnp.minimum(donor - 1, reach - taker)
    passed = jax.random.randint(jax.random.fold_in(rng, 1), (pairs,), 0, 1 << 20) % (margin + 1)
    lengths = lengths.at[1:1 + 2 * pairs:2].set(donor - passed).at[2:2 + 2 * pairs:2].set(taker + passed)
    return lengths[jax.random.permutation(jax.random.fold_in(rng, 2), count)]


def normal_values(key, shape, scale, reach, shards=(), kind=jnp.bfloat16):
    entries = jax.random.normal(key, shape, jnp.float32) * scale
    if len(shards) > 0:
        entries = level_of(key, shape, shards, -0.22, 0.18) * entries
    return jnp.clip(entries, min=-reach, max=reach).astype(kind)


def noise_with(own_key, extent, scale, limit, cuts, heavy, kind=jnp.bfloat16):
    entries = scale * jax.random.normal(own_key, extent, jnp.float32)
    if cuts:
        entries = entries * level_of(own_key, extent, cuts, -0.22, 0.18)
    return jnp.clip(strengthened(entries, jax.random.fold_in(own_key, 3), *heavy), -limit, limit).astype(kind)


def setup_inputs(seed: int = 0) -> dict:
    key_of = jax.random.split(jax.random.key(seed), 17)
    return {
        "tokens": normal_values(key_of[0], (SEQS, SEQ_LEN, D), 1.0, 6.0, ((0, 8), (1, 4))),
        "segments": jax.vmap(lambda own: jnp.searchsorted(jnp.cumsum(ragged(own, DOCS, SEQ_LEN, DOC_MOST, 1)), jnp.arange(SEQ_LEN), side="right"))(jax.random.split(key_of[1], SEQS)).reshape((SEQS, SEQ_LEN)).astype(jnp.int32),
        "pairing": jax.vmap(lambda own: jax.random.permutation(own, NBLK))(jax.random.split(key_of[2], HEADS)).reshape((HEADS, NBLK)).astype(jnp.int32),
        "qkv_weight": normal_values(key_of[3], (D, HEADS, 3 * HD), (D // 2) ** -0.5, 0.3125, ((0, 8), (1, 4))),
        "qv_bias": normal_values(key_of[4], (HEADS, 2 * HD), 0.5, 3.0, ((0, 4),)),
        "out_weight": normal_values(key_of[5], (HEADS, HD, D), (D // 16) ** -0.5, 0.875, ((0, 4), (2, 8))),
        "out_bias": normal_values(key_of[6], (D,), 0.5, 3.0),
        "first_gain": jnp.clip(1.0 + 0.1 * jax.random.normal(key_of[7], (D,), jnp.float32), 0.5, 1.5).astype(jnp.bfloat16),
        "first_shift": normal_values(key_of[8], (D,), 0.3, 2.0),
        "up_weight": normal_values(key_of[9], (D, FF), D ** -0.5, 0.21875, ((0, 8), (1, 4))),
        "up_bias": normal_values(key_of[10], (FF,), 0.5, 3.0, ((0, 4),)),
        "down_weight": normal_values(key_of[11], (FF, D), FF ** -0.5, 0.109375, ((0, 4), (1, 8))),
        "down_bias": normal_values(key_of[12], (D,), 0.5, 3.0),
        "second_gain": jnp.clip(1.0 + 0.1 * jax.random.normal(key_of[13], (D,), jnp.float32), 0.5, 1.5).astype(jnp.bfloat16),
        "second_shift": normal_values(key_of[14], (D,), 0.3, 2.0),
        "cotangent": noise_with(key_of[15], (SEQS, SEQ_LEN, D), 1.0, 6.0, ((0, 8), (1, 4)), (0, 2, 8, 2.0)),
    }


@jax.custom_vjp
def low(v):
    return lax.optimization_barrier(v.astype(jnp.bfloat16)).astype(jnp.float32)

@jax.custom_vjp
def low_back(v):
    return v

def low_keep(v):
    return (low(v), None)

def low_pass(kept, grad):
    return (grad,)

def back_keep(v):
    return (v, None)

def back_low(kept, grad):
    return (low(grad),)
low.defvjp(low_keep, low_pass)
low_back.defvjp(back_keep, back_low)
eps = 1e-06
highest = lax.Precision.HIGHEST

def norm_layer(values, norm_gain, norm_shift):
    center = lax.optimization_barrier(jnp.mean(values, axis=-1, keepdims=True))
    centred = values - center
    spread = lax.optimization_barrier(jnp.mean(centred * centred, axis=-1, keepdims=True))
    return centred * lax.rsqrt(spread + eps) * norm_gain + norm_shift

def attend_allowed(segment_row, pairing):
    places = jnp.arange(SEQ_LEN, dtype=jnp.int32)
    block_of = places // BLOCK
    same_doc = segment_row[:, None] == segment_row[None, :]
    target = pairing[:, block_of]
    paired = target[:, :, None] == block_of[None, None, :]
    itself = places[:, None] == places[None, :]
    return same_doc[None] & paired | itself[None]

def layer_forward(parameters, row_tokens, segment_row, pairing):
    qkv_weight, qv_bias, out_weight, out_bias, first_gain, first_shift, up_weight, up_bias, down_weight, down_bias, second_gain, second_shift = parameters
    length = row_tokens.shape[0]
    score_scale = HD ** (-0.5)
    projected = jnp.dot(row_tokens, qkv_weight.reshape(D, 3 * D), precision=highest)
    head_bias = jnp.concatenate([qv_bias[:, :HD], jnp.zeros((HEADS, HD), jnp.float32), qv_bias[:, HD:]], axis=1)
    packed = low(low_back(projected).reshape(length, HEADS, 3 * HD) + head_bias)
    query_rows = packed[:, :, :HD]
    key_rows = packed[:, :, HD:2 * HD]
    value_rows = packed[:, :, 2 * HD:]
    raw_scores = jnp.einsum('qhe,khe->hqk', query_rows, key_rows, precision=highest) * score_scale
    scores = low_back(raw_scores)
    allowed = attend_allowed(segment_row, pairing)
    softmax_out = jax.nn.softmax(jnp.where(allowed, scores, -jnp.inf), axis=-1)
    mixed_heads = jnp.einsum('hqk,khe->qhe', low(softmax_out), value_rows, precision=highest)
    mixed_heads = low(low_back(mixed_heads)).reshape(length, D)
    attn_rows = low_back(jnp.dot(mixed_heads, out_weight.reshape(D, D), precision=highest)) + out_bias
    middle = norm_layer(row_tokens + attn_rows, first_gain, first_shift)
    upper_pre = low_back(jnp.dot(low(middle), up_weight, precision=highest)) + up_bias
    active = low(jax.nn.gelu(upper_pre, approximate=False))
    branch = low_back(jnp.dot(active, down_weight, precision=highest)) + down_bias
    return norm_layer(middle + branch, second_gain, second_shift)

def reference(tokens, segments, pairing, qkv_weight, qv_bias, out_weight, out_bias, first_gain, first_shift, up_weight, up_bias, down_weight, down_bias, second_gain, second_shift, cotangent):
    parameters = tuple((weight_item.astype(jnp.float32) for weight_item in (qkv_weight, qv_bias, out_weight, out_bias, first_gain, first_shift, up_weight, up_bias, down_weight, down_bias, second_gain, second_shift)))
    inputs_float = tokens.astype(jnp.float32)

    def forward_all(inputs_now, parameters_now):

        def scan_step(running, sequence_item):
            row_tokens, segment_row = sequence_item
            return (running, jax.checkpoint(layer_forward)(parameters_now, row_tokens, segment_row, pairing))
        running_end, stacked = lax.scan(scan_step, jnp.zeros((), jnp.float32), (inputs_now, segments))
        return stacked
    outputs, pullback = jax.vjp(forward_all, inputs_float, parameters)
    input_grad, param_grads = pullback(cotangent.astype(jnp.float32))
    return (outputs.astype(jnp.bfloat16), input_grad.astype(jnp.bfloat16), param_grads[0], param_grads[1], param_grads[2], param_grads[3], param_grads[4], param_grads[5], param_grads[6], param_grads[7], param_grads[8], param_grads[9], param_grads[10], param_grads[11])
```

```python
import functools

import jax
import jax.numpy as jnp
from jax import lax
from jax.experimental import pallas as pl
from jax.experimental.pallas import tpu as pltpu
from jax.sharding import PartitionSpec as P

EPS = 1e-06
NEG = -1e30
BOTH = ("dp", "tensor")
F32 = jnp.float32
BF16 = jnp.bfloat16


def mm(left, right):
    return lax.dot_general(left, right, (((1,), (0,)), ((), ())), preferred_element_type=F32)


def mm_rt(left, right):
    return lax.dot_general(left, right, (((1,), (1,)), ((), ())), preferred_element_type=F32)


def mm_lt(left, right):
    return lax.dot_general(left, right, (((0,), (0,)), ((), ())), preferred_element_type=F32)


def head_lanes(shape, head, dim, head_size):
    place = lax.broadcasted_iota(jnp.int32, shape, dim)
    return (place < head_size) if head == 0 else (place >= head_size)


def attend_kernel(pair_ref, q_ref, k_ref, v_ref, segq_ref, segk_ref, o_ref, lse_ref, *, rows, hs):
    group, block = pl.program_id(0), pl.program_id(1)
    own = pl.ds(pl.multiple_of(block * rows, rows), rows)
    q2 = q_ref[...]
    own_raw = (q2.astype(F32) * k_ref[own, :].astype(F32)).T
    own_values = v_ref[own, :].astype(F32).T
    segq = segq_ref[...]
    total = jnp.zeros((2 * hs, rows), F32)
    for head in range(2):
        target = pair_ref[2 * group + head, block]
        there = pl.ds(pl.multiple_of(target * rows, rows), rows)
        keys, values = k_ref[there, :], v_ref[there, :]
        lanes = head_lanes(q2.shape, head, 1, hs)
        scores = mm_rt(keys, jnp.where(lanes, q2, jnp.zeros_like(q2)))
        scores = jnp.where(segk_ref[there, :] == segq, scores, NEG)
        raw = jnp.sum(own_raw[head * hs : (head + 1) * hs], axis=0, keepdims=True)
        raw = jnp.where(target != block, raw, NEG)
        peak = jnp.maximum(jnp.max(scores, axis=0, keepdims=True), raw)
        expo = jnp.exp(scores - peak)
        own_expo = jnp.exp(raw - peak)
        denom = jnp.sum(expo, axis=0, keepdims=True) + own_expo
        masked_values = jnp.where(lanes, values, jnp.zeros_like(values))
        part = mm_lt(masked_values, expo.astype(BF16))
        low = own_expo.astype(BF16).astype(F32)
        mine = head_lanes(part.shape, head, 0, hs)
        part = part + jnp.where(mine, own_values * low, 0.0)
        total = total + part * (1.0 / denom)
        lse_ref[0, head : head + 1, :] = peak + jnp.log(denom)
    o_ref[...] = total.T.astype(BF16)


def attend(pairs, packed, segq, segk, hs):
    seq, width = packed.shape
    heads, blocks = pairs.shape
    rows, groups = seq // blocks, heads // 2
    lanes = 2 * hs
    return pl.pallas_call(
        functools.partial(attend_kernel, rows=rows, hs=hs),
        grid_spec=pltpu.PrefetchScalarGridSpec(
            num_scalar_prefetch=1,
            grid=(groups, blocks),
            in_specs=[
                pl.BlockSpec((rows, lanes), lambda g, i, p: (i, g)),
                pl.BlockSpec((seq, lanes), lambda g, i, p: (0, groups + g)),
                pl.BlockSpec((seq, lanes), lambda g, i, p: (0, 2 * groups + g)),
                pl.BlockSpec((1, rows), lambda g, i, p: (0, i)),
                pl.BlockSpec((seq, 1), lambda g, i, p: (0, 0)),
            ],
            out_specs=[
                pl.BlockSpec((rows, lanes), lambda g, i, p: (i, g)),
                pl.BlockSpec((1, 8, rows), lambda g, i, p: (g, 0, i)),
            ],
        ),
        out_shape=[
            jax.ShapeDtypeStruct((seq, groups * lanes), BF16),
            jax.ShapeDtypeStruct((groups, 8, seq), F32),
        ],
        compiler_params=pltpu.CompilerParams(vmem_limit_bytes=48 << 20),
        name="attend",
    )(pairs, packed, packed, packed, segq, segk)


def attend_back_kernel(
    pair_ref, q_ref, k_ref, v_ref, do_ref, segq_ref, segk_ref, lse_ref,
    dq_ref, dk_ref, dv_ref, sums_ref, dk_acc, dv_acc, *, rows, hs, blocks,
):
    group, block = pl.program_id(0), pl.program_id(1)

    @pl.when(block == 0)
    def _():
        dk_acc[...] = jnp.zeros_like(dk_acc)
        dv_acc[...] = jnp.zeros_like(dv_acc)
        sums_ref[...] = jnp.zeros_like(sums_ref)

    own = pl.ds(pl.multiple_of(block * rows, rows), rows)
    q2, do2 = q_ref[...], do_ref[...]
    qt, dot = q2.astype(F32).T, do2.astype(F32).T
    own_keys, own_values = k_ref[own, :].astype(F32).T, v_ref[own, :].astype(F32).T
    own_raw, own_dp = qt * own_keys, dot * own_values
    segq = segq_ref[...]
    dq = jnp.zeros((2 * hs, rows), F32)
    own_ds, own_low = [], []
    for head in range(2):
        target = pair_ref[2 * group + head, block]
        there = pl.ds(pl.multiple_of(target * rows, rows), rows)
        keys, values = k_ref[there, :], v_ref[there, :]
        lanes = head_lanes(q2.shape, head, 1, hs)
        zero = jnp.zeros_like(q2)
        qm, dom = jnp.where(lanes, q2, zero), jnp.where(lanes, do2, zero)
        lse = lse_ref[0, head : head + 1, :]
        scores = mm_rt(keys, qm)
        probs = jnp.exp(jnp.where(segk_ref[there, :] == segq, scores - lse, NEG))
        raw = jnp.sum(own_raw[head * hs : (head + 1) * hs], axis=0, keepdims=True)
        self_prob = jnp.exp(jnp.where(target != block, raw - lse, NEG))
        self_dp = jnp.sum(own_dp[head * hs : (head + 1) * hs], axis=0, keepdims=True)
        dv_acc[there, :] += mm(probs.astype(BF16), dom)
        dprobs = mm_rt(values, dom)
        delta = jnp.sum(probs * dprobs, axis=0, keepdims=True) + self_prob * self_dp
        dscores = (probs * (dprobs - delta)).astype(BF16)
        dk_acc[there, :] += mm(dscores, qm)
        dq = dq + mm_lt(jnp.where(lanes, keys, jnp.zeros_like(keys)), dscores)
        own_ds.append((self_prob * (self_dp - delta)).astype(BF16).astype(F32))
        own_low.append(self_prob.astype(BF16).astype(F32))
    first = head_lanes(dq.shape, 0, 0, hs)
    ds_rows = jnp.where(first, own_ds[0], own_ds[1])
    low_rows = jnp.where(first, own_low[0], own_low[1])
    dq = ((dq + ds_rows * own_keys) * (hs**-0.5)).T
    dq_ref[...] = dq.astype(BF16)
    sums_ref[0, 0:1, :] += jnp.sum(dq, axis=0, keepdims=True)
    dk_acc[own, :] += (ds_rows * qt).T
    dv_acc[own, :] += (low_rows * dot).T

    @pl.when(block == blocks - 1)
    def _():
        dk_ref[...] = dk_acc[...].astype(BF16)
        dv = dv_acc[...]
        dv_ref[...] = dv.astype(BF16)
        sums_ref[0, 1:2, :] = jnp.sum(dv, axis=0, keepdims=True)


def attend_back(pairs, packed, grad_mixed, segq, segk, lse, hs):
    seq, width = packed.shape
    heads, blocks = pairs.shape
    rows, groups = seq // blocks, heads // 2
    lanes = 2 * hs
    grads = jax.ShapeDtypeStruct((seq, groups * lanes), BF16)
    return pl.pallas_call(
        functools.partial(attend_back_kernel, rows=rows, hs=hs, blocks=blocks),
        grid_spec=pltpu.PrefetchScalarGridSpec(
            num_scalar_prefetch=1,
            grid=(groups, blocks),
            in_specs=[
                pl.BlockSpec((rows, lanes), lambda g, i, p: (i, g)),
                pl.BlockSpec((seq, lanes), lambda g, i, p: (0, groups + g)),
                pl.BlockSpec((seq, lanes), lambda g, i, p: (0, 2 * groups + g)),
                pl.BlockSpec((rows, lanes), lambda g, i, p: (i, g)),
                pl.BlockSpec((1, rows), lambda g, i, p: (0, i)),
                pl.BlockSpec((seq, 1), lambda g, i, p: (0, 0)),
                pl.BlockSpec((1, 8, rows), lambda g, i, p: (g, 0, i)),
            ],
            out_specs=[
                pl.BlockSpec((rows, lanes), lambda g, i, p: (i, g)),
                pl.BlockSpec((seq, lanes), lambda g, i, p: (0, g)),
                pl.BlockSpec((seq, lanes), lambda g, i, p: (0, g)),
                pl.BlockSpec((1, 8, lanes), lambda g, i, p: (g, 0, 0)),
            ],
            scratch_shapes=[pltpu.VMEM((seq, lanes), F32), pltpu.VMEM((seq, lanes), F32)],
        ),
        out_shape=[grads, grads, grads, jax.ShapeDtypeStruct((groups, 8, lanes), F32)],
        compiler_params=pltpu.CompilerParams(vmem_limit_bytes=48 << 20),
        name="attend_back",
    )(pairs, packed, packed, packed, grad_mixed, segq, segk, lse)


def xor_order(stacked, index, dim=0):
    count = stacked.shape[dim]
    bit = 1
    while bit < count:
        shape = stacked.shape
        split = shape[:dim] + (count // (2 * bit), 2, bit) + shape[dim + 1 :]
        view = stacked.reshape(split)
        swapped = jnp.flip(view, dim + 1)
        stacked = jnp.where((index // bit) % 2 == 1, swapped, view).reshape(shape)
        bit *= 2
    return stacked


def per_device(
    tokens,
    segments,
    pairing,
    qkv_weight,
    qv_bias,
    out_weight,
    out_bias,
    first_gain,
    first_shift,
    up_weight,
    up_bias,
    down_weight,
    down_bias,
    second_gain,
    second_shift,
    cotangent,
):
    width = tokens.shape[2]
    rows = tokens.shape[1]
    lheads, blocks = pairing.shape
    hs = qv_bias.shape[1] // 2
    units = up_weight.shape[1]
    ndp, nt = lax.axis_size("dp"), lax.axis_size("tensor")
    drows = width // ndp
    dp, tensor = lax.axis_index("dp"), lax.axis_index("tensor")
    core, half, low = dp % 2, tensor // 2, tensor % 2
    slot_mask = 2 * core + low
    heads = 2 * lheads

    core_pairs = [(i, i ^ 1) for i in range(ndp)]

    def core_swap(x):
        return lax.ppermute(x, "dp", core_pairs)

    def z_step(x, k):
        return lax.ppermute(x, "tensor", [(i, i ^ k) for i in range(nt)])

    def chip_step(x, k):
        return lax.ppermute(x, "dp", [(i, i ^ (2 * k)) for i in range(ndp)])

    def column(k, back):
        steps = []
        for p in range(ndp // 2):
            for c in range(2):
                for a in range(2):
                    for b in range(2):
                        home = (2 * p + c) * nt + 2 * a + b
                        away = (2 * p + a) * nt + 2 * c + (b ^ k)
                        steps.append((away, home) if back else (home, away))
        return steps

    def to_sequence(x):
        return [
            lax.ppermute(lax.dynamic_index_in_dim(x, low ^ k, 0, keepdims=False), BOTH, column(k, False))
            for k in range(2)
        ]

    def to_home(parts):
        first, second = [lax.ppermute(parts[k], BOTH, column(k, True)) for k in range(2)]
        return jnp.stack([jnp.where(low == 0, first, second), jnp.where(low == 0, second, first)])

    def z_gather(x):
        parts = jnp.stack([x] + [z_step(x, k) for k in range(1, nt)])
        return xor_order(parts, tensor)

    def gather_weight(local, stacked):
        parts = [stacked] + [chip_step(stacked, k) for k in range(1, ndp // 2)]
        out = jnp.zeros((nt, width, local.shape[1]), BF16)
        for k, part in enumerate(parts):
            out = lax.dynamic_update_slice(out, part, (0, (dp ^ (2 * k)) * drows, 0))
        for k, part in enumerate(parts):
            out = lax.dynamic_update_slice(out, core_swap(part), (0, (dp ^ (2 * k) ^ 1) * drows, 0))
        return out

    small = jnp.concatenate([pairing.astype(BF16).reshape(-1), qv_bias.reshape(-1), up_bias])
    n_pair, n_qv = lheads * blocks, lheads * 2 * hs
    small = z_gather(small)
    all_pairs = small[:, :n_pair].astype(jnp.int32).reshape(2, heads, blocks)
    my_pairs = jnp.where(core == 0, all_pairs[0], all_pairs[1])
    pair_slots = xor_order(my_pairs, slot_mask, 1) ^ slot_mask
    all_qvb = small[:, n_pair : n_pair + n_qv].astype(F32).reshape(2, heads, 2 * hs)
    my_qvb = jnp.where(core == 0, all_qvb[0], all_qvb[1])
    up_bias_all = small[:, n_pair + n_qv :].astype(F32).reshape(nt * units)

    segs = jnp.where(half == core, segments, core_swap(segments))
    seg_row = xor_order(jnp.where(low == 0, segs[0], segs[1]).reshape(blocks, rows), slot_mask)
    seg_row = seg_row.reshape(1, blocks * rows)
    seg_col = seg_row.reshape(blocks * rows, 1)

    qkv_local = qkv_weight.reshape(drows, lheads, 3, hs).transpose(0, 2, 1, 3).reshape(drows, 3 * lheads * hs)
    qkv_z = z_gather(qkv_local)
    halves = qkv_z.reshape(2, 2, drows, 3 * lheads * hs)
    give = jnp.where(core == 0, halves[1], halves[0])
    keep = jnp.where(core == 0, halves[0], halves[1])
    keeps = [keep] + [chip_step(keep, k) for k in range(1, ndp // 2)]
    gives = [give] + [chip_step(give, k) for k in range(1, ndp // 2)]
    qkv_full = jnp.zeros((2, width, 3 * lheads * hs), BF16)
    for k in range(ndp // 2):
        qkv_full = lax.dynamic_update_slice(qkv_full, keeps[k], (0, (dp ^ (2 * k)) * drows, 0))
        qkv_full = lax.dynamic_update_slice(
            qkv_full, core_swap(gives[k]), (0, (dp ^ (2 * k) ^ 1) * drows, 0)
        )
    qkv_full = (
        qkv_full.reshape(2, width, 3, lheads * hs).transpose(1, 2, 0, 3).reshape(width, 3 * heads * hs)
    )

    mine = to_sequence(tokens)
    x_mine = jnp.concatenate(mine)
    x_all = jnp.concatenate(mine + [core_swap(part) for part in mine])

    def weight_of(local):
        return gather_weight(local, z_gather(local))

    out_full = weight_of(out_weight.reshape(lheads * hs, drows).T)
    up_full = weight_of(up_weight)
    down_full = weight_of(down_weight.T)
    upstream = jnp.concatenate(to_sequence(cotangent)).astype(F32)

    zeros = jnp.zeros((heads * hs,), F32)
    bias = jnp.concatenate([my_qvb[:, :hs].reshape(-1), zeros, my_qvb[:, hs:].reshape(-1)])
    packed = (mm(x_all, qkv_full) + bias).astype(BF16)
    scale = jnp.concatenate([jnp.full((heads * hs,), hs**-0.5, BF16), jnp.ones((2 * heads * hs,), BF16)])
    packed = packed * scale
    mixed, lse = attend(pair_slots, packed, seg_row, seg_col, hs)

    count = 2 * rows
    other = core_swap(mixed[count:])
    mixed_all = jnp.where(
        core == 0,
        jnp.concatenate([mixed[:count], other], axis=1),
        jnp.concatenate([other, mixed[:count]], axis=1),
    )

    def joined(weight):
        return weight.transpose(1, 0, 2).reshape(width, -1)

    out_t = joined(out_full)
    up_n = joined(up_full)
    down_t = joined(down_full)
    gain_one, shift_one = first_gain.astype(F32), first_shift.astype(F32)
    gain_two, shift_two = second_gain.astype(F32), second_shift.astype(F32)

    def norm(values):
        centred = values - jnp.mean(values, axis=-1, keepdims=True)
        scale = lax.rsqrt(jnp.mean(centred * centred, axis=-1, keepdims=True) + EPS)
        return centred * scale, scale

    def norm_back(grad, unit, scale, gain):
        q = grad * gain
        return scale * (
            q
            - jnp.mean(q, axis=-1, keepdims=True)
            - unit * jnp.mean(q * unit, axis=-1, keepdims=True)
        )

    resid_one = x_mine.astype(F32) + mm_rt(mixed_all, out_t) + out_bias.astype(F32)
    unit_one, scale_one = norm(resid_one)
    middle = unit_one * gain_one + shift_one
    middle_low = middle.astype(BF16)
    upper = mm(middle_low, up_n) + up_bias_all
    phi_sum = 0.5 * (1.0 + lax.erf(upper * 0.7071067811865476))
    slope = (phi_sum + upper * (jnp.exp(-0.5 * upper * upper) * 0.3989422804014327)).astype(BF16)
    active = (upper * phi_sum).astype(BF16)
    resid_two = middle + mm_rt(active, down_t) + down_bias.astype(F32)
    unit_two, scale_two = norm(resid_two)
    layer_mine = (unit_two * gain_two + shift_two).astype(BF16)
    gain_two_part = jnp.sum(upstream * unit_two, axis=0)
    shift_two_part = jnp.sum(upstream, axis=0)
    grad_two = norm_back(upstream, unit_two, scale_two, gain_two)
    downb_part = jnp.sum(grad_two, axis=0)
    grad_branch = grad_two.astype(BF16)
    grad_upper = mm(grad_branch, down_t) * slope.astype(F32)
    upb_part = jnp.sum(grad_upper, axis=0)
    grad_upper_low = grad_upper.astype(BF16)
    grad_mid = mm_rt(grad_upper_low, up_n) + grad_two
    gain_one_part = jnp.sum(grad_mid * unit_one, axis=0)
    shift_one_part = jnp.sum(grad_mid, axis=0)
    grad_one = norm_back(grad_mid, unit_one, scale_one, gain_one)
    outb_part = jnp.sum(grad_one, axis=0)
    grad_attn = grad_one.astype(BF16)
    grad_mixed = mm(grad_attn, out_t).astype(BF16)

    layer_out = to_home([layer_mine[:rows], layer_mine[rows:]])

    def reduce_chip(grad):
        cols = grad.shape[1]
        view = grad.reshape(ndp // 2, 2, drows, cols)
        theirs = lax.dynamic_index_in_dim(view, 1 - core, 1, keepdims=False).astype(BF16)
        ours = lax.dynamic_index_in_dim(view, core, 1, keepdims=False)
        return ours + core_swap(theirs).astype(F32)

    def reduce_plane(view):
        chip = dp // 2
        total = lax.dynamic_index_in_dim(view, chip, 0, keepdims=False)
        for k in range(1, ndp // 2):
            part = lax.dynamic_index_in_dim(view, chip ^ k, 0, keepdims=False).astype(BF16)
            total = total + chip_step(part, k).astype(F32)
        return total

    def reduce_z(grad):
        view = grad.reshape(drows, nt, grad.shape[1] // nt)
        total = lax.dynamic_index_in_dim(view, tensor, 1, keepdims=False)
        for k in range(1, nt):
            part = lax.dynamic_index_in_dim(view, tensor ^ k, 1, keepdims=False).astype(BF16)
            total = total + z_step(part, k).astype(F32)
        return total

    def reduce_weight(grad):
        return reduce_z(reduce_plane(reduce_chip(grad)))

    down_grad = reduce_weight(mm_lt(grad_branch, active)).T
    up_grad = reduce_weight(mm_lt(middle_low, grad_upper_low))
    out_grad = reduce_weight(mm_lt(grad_attn, mixed_all)).T.reshape(lheads, hs, drows)

    def all_sum(x):
        for bit in range(nt.bit_length() - 1):
            x = x + z_step(x, 1 << bit)
        for bit in range(ndp.bit_length() - 1):
            x = x + lax.ppermute(x, "dp", [(i, i ^ (1 << bit)) for i in range(ndp)])
        return x

    sums = all_sum(
        jnp.concatenate(
            [outb_part, gain_one_part, shift_one_part, downb_part, gain_two_part, shift_two_part, upb_part]
        )
    )
    outb_grad, gain_one_grad, shift_one_grad, downb_grad, gain_two_grad, shift_two_grad = [
        sums[i * width : (i + 1) * width] for i in range(6)
    ]
    upb_grad = lax.dynamic_slice(sums, (6 * width + tensor * units,), (units,))

    cols = heads * hs
    gm_first, gm_second = grad_mixed[:, :cols], grad_mixed[:, cols:]
    got = core_swap(jnp.where(core == 0, gm_second, gm_first))
    gm_all = jnp.concatenate([jnp.where(core == 0, gm_first, gm_second), got])
    dq, dk, dv, head_sums = attend_back(pair_slots, packed, gm_all, seg_row, seg_col, lse, hs)
    grad_packed = jnp.concatenate([dq, dk, dv], axis=1)

    in_part = mm_rt(grad_packed, qkv_full)
    in_sum = in_part[:count] + core_swap(in_part[count:].astype(BF16)).astype(F32) + grad_one
    in_low = in_sum.astype(BF16)
    input_grad = to_home([in_low[:rows], in_low[rows:]])

    qkv_part = mm_lt(x_all, grad_packed).reshape(ndp // 2, 2 * drows, 3 * cols)
    qkv_sum = reduce_plane(qkv_part)
    qkv_sum = qkv_sum.reshape(2, drows, 3, 2, lheads * hs).transpose(0, 1, 3, 2, 4)
    qkv_sum = qkv_sum.reshape(2, drows, 2, 3 * lheads * hs)
    got = core_swap(jnp.where(core == 0, qkv_sum[1], qkv_sum[0]).astype(BF16)).astype(F32)
    kept = jnp.where(core == 0, qkv_sum[0], qkv_sum[1])
    qkv_rows = jnp.where(
        core == 0,
        jnp.concatenate([kept, got], axis=1),
        jnp.concatenate([got, kept], axis=1),
    )
    qkv_grad = reduce_z(qkv_rows.reshape(drows, nt * 3 * lheads * hs))
    qkv_grad = qkv_grad.reshape(drows, 3, lheads, hs).transpose(0, 2, 1, 3)
    qkv_grad = qkv_grad.reshape(drows, lheads, 3 * hs)

    groups = heads // 2
    q_sum = head_sums[:, 0, :].reshape(heads, hs)
    v_sum = head_sums[:, 1, :].reshape(heads, hs)
    own_qvb = jnp.concatenate([q_sum, v_sum], axis=1)
    blank = jnp.zeros_like(own_qvb)
    both = jnp.concatenate([jnp.where(core == 0, own_qvb, blank), jnp.where(core == 0, blank, own_qvb)])
    both = all_sum(both)
    qvb_grad = lax.dynamic_slice(both, (tensor * lheads, 0), (lheads, 2 * hs))
    return (
        layer_out,
        input_grad,
        qkv_grad,
        qvb_grad,
        out_grad,
        outb_grad,
        gain_one_grad,
        shift_one_grad,
        up_grad,
        upb_grad,
        down_grad,
        downb_grad,
        gain_two_grad,
        shift_two_grad,
    )


def solution(mesh):
    return jax.shard_map(
        per_device,
        mesh=mesh,
        in_specs=(
            P("dp", "tensor", None),
            P("dp", None),
            P("tensor", None),
            P("dp", "tensor", None),
            P("tensor", None),
            P("tensor", None, "dp"),
            P(),
            P(),
            P(),
            P("dp", "tensor"),
            P("tensor"),
            P("tensor", "dp"),
            P(),
            P(),
            P(),
            P("dp", "tensor", None),
        ),
        out_specs=(
            P("dp", "tensor", None),
            P("dp", "tensor", None),
            P("dp", "tensor", None),
            P("tensor", None),
            P("tensor", None, "dp"),
            P(),
            P(),
            P(),
            P("dp", "tensor"),
            P("tensor"),
            P("tensor", "dp"),
            P(),
            P(),
            P(),
        ),
        check_vma=False,
    )
```

```python
import functools

import jax
import jax.numpy as jnp
from jax import lax
from jax.experimental import pallas as pl
from jax.experimental.pallas import tpu as pltpu
from jax.sharding import PartitionSpec as P

EPS = 1e-06
NEG = -1e30
BOTH = ("dp", "tensor")
F32 = jnp.float32
BF16 = jnp.bfloat16
ANY = pl.BlockSpec(memory_space=pl.ANY)
LIMIT = 58 << 20


def mm(left, right):
    return lax.dot_general(left, right, (((1,), (0,)), ((), ())), preferred_element_type=F32)


def mm_rt(left, right):
    return lax.dot_general(left, right, (((1,), (1,)), ((), ())), preferred_element_type=F32)


def mm_lt(left, right):
    return lax.dot_general(left, right, (((0,), (0,)), ((), ())), preferred_element_type=F32)


def head_lanes(shape, head, dim, head_size):
    place = lax.broadcasted_iota(jnp.int32, shape, dim)
    return (place < head_size) if head == 0 else (place >= head_size)


def fetches(pieces, offsets, target, dim, sems, first):
    copies = []
    for k, (piece, offset) in enumerate(zip(pieces, offsets)):
        count = piece.shape[dim]
        where = pl.ds(offset if isinstance(offset, int) else pl.multiple_of(offset, count), count)
        index = (slice(None),) * dim + (where,)
        copies.append(pltpu.make_async_copy(piece, target.at[index], sems.at[first + k]))
    return copies


def piece_rows(place, step, rows, count):
    if count == 1:
        return [0]
    return [(place ^ (k * step)) * rows for k in range(count)]


def attend_kernel(pair_ref, place_ref, *refs, rows, hs, blocks, n_w):
    x_refs, refs = refs[:blocks], refs[blocks:]
    w_refs, refs = refs[:n_w], refs[n_w:]
    bias_ref, segq_ref, segk_ref, q_out, k_out, v_out, o_ref, lse_ref, x_all, w_all, sems = refs
    group, block = pl.program_id(0), pl.program_id(1)
    lanes2 = 2 * hs

    @pl.when((group == 0) & (block == 0))
    def _():
        chip = place_ref[0] // 2
        copies = fetches(
            w_refs, piece_rows(chip, 1, w_refs[0].shape[1], n_w), w_all, 1, sems, 0
        ) + fetches(x_refs, [rows * k for k in range(blocks)], x_all, 0, sems, n_w)
        for copy in copies:
            copy.start()
        for copy in copies:
            copy.wait()

    @pl.when(block == 0)
    def _():
        weight = w_all[group]
        for k in range(blocks):
            part = pl.ds(k * rows, rows)
            out = (mm(x_all[part, :], weight) + bias_ref[0]).astype(BF16)
            q_out[part, :] = out[:, :lanes2] * (hs**-0.5)
            k_out[part, :] = out[:, lanes2 : 2 * lanes2]
            v_out[part, :] = out[:, 2 * lanes2 :]

    own = pl.ds(pl.multiple_of(block * rows, rows), rows)
    q2 = q_out[own, :]
    own_raw = (q2.astype(F32) * k_out[own, :].astype(F32)).T
    own_values = v_out[own, :].astype(F32).T
    segq = segq_ref[...]
    total = jnp.zeros((2 * hs, rows), F32)
    for head in range(2):
        target = pair_ref[2 * group + head, block]
        there = pl.ds(pl.multiple_of(target * rows, rows), rows)
        keys, values = k_out[there, :], v_out[there, :]
        lanes = head_lanes(q2.shape, head, 1, hs)
        scores = mm_rt(keys, jnp.where(lanes, q2, jnp.zeros_like(q2)))
        scores = jnp.where(segk_ref[there, :] == segq, scores, NEG)
        raw = jnp.sum(own_raw[head * hs : (head + 1) * hs], axis=0, keepdims=True)
        raw = jnp.where(target != block, raw, NEG)
        peak = jnp.maximum(jnp.max(scores, axis=0, keepdims=True), raw)
        expo = jnp.exp(scores - peak)
        own_expo = jnp.exp(raw - peak)
        denom = jnp.sum(expo, axis=0, keepdims=True) + own_expo
        masked_values = jnp.where(lanes, values, jnp.zeros_like(values))
        part = mm_lt(masked_values, expo.astype(BF16))
        low = own_expo.astype(BF16).astype(F32)
        mine = head_lanes(part.shape, head, 0, hs)
        part = part + jnp.where(mine, own_values * low, 0.0)
        total = total + part * (1.0 / denom)
        lse_ref[0, head : head + 1, :] = peak + jnp.log(denom)
    o_ref[...] = total.T.astype(BF16)


def attend(pairs, place, x_parts, w_pieces, bias, segq, segk, hs):
    heads, blocks = pairs.shape
    rows, width = x_parts[0].shape
    seq, groups, lanes = rows * blocks, heads // 2, 2 * hs
    kept = jax.ShapeDtypeStruct((seq, groups * lanes), BF16)
    flops = 2 * seq * width * 3 * groups * lanes + 4 * heads * seq * rows * 2 * lanes
    return pl.pallas_call(
        functools.partial(attend_kernel, rows=rows, hs=hs, blocks=blocks, n_w=len(w_pieces)),
        grid_spec=pltpu.PrefetchScalarGridSpec(
            num_scalar_prefetch=2,
            grid=(groups, blocks),
            in_specs=[ANY] * (blocks + len(w_pieces))
            + [
                pl.BlockSpec((1, 1, 3 * lanes), lambda g, i, p, q: (g, 0, 0)),
                pl.BlockSpec((1, rows), lambda g, i, p, q: (0, i)),
                pl.BlockSpec((seq, 1), lambda g, i, p, q: (0, 0)),
            ],
            out_specs=[pl.BlockSpec((seq, lanes), lambda g, i, p, q: (0, g))] * 3
            + [
                pl.BlockSpec((rows, lanes), lambda g, i, p, q: (i, g)),
                pl.BlockSpec((1, 8, rows), lambda g, i, p, q: (g, 0, i)),
            ],
            scratch_shapes=[
                pltpu.VMEM((seq, width), BF16),
                pltpu.VMEM((groups, width, 3 * lanes), BF16),
                pltpu.SemaphoreType.DMA((blocks + len(w_pieces),)),
            ],
        ),
        out_shape=[kept, kept, kept, kept, jax.ShapeDtypeStruct((groups, 8, seq), F32)],
        compiler_params=pltpu.CompilerParams(vmem_limit_bytes=LIMIT),
        cost_estimate=pl.CostEstimate(flops=flops, bytes_accessed=20 << 20, transcendentals=0),
        name="attend",
    )(pairs, place, *x_parts, *w_pieces, bias, segq, segk)


def attend_back_kernel(pair_ref, place_ref, *refs, rows, hs, blocks, groups, n_w):
    x_refs, refs = refs[:blocks], refs[blocks:]
    w_refs, refs = refs[:n_w], refs[n_w:]
    (
        q_ref, k_ref, v_ref, do_ref, segq_ref, segk_ref, lse_ref,
        dw_ref, in_mine, in_other, sums_ref,
        x_all, x_t, w_all, in_acc, dq_all, dk_acc, dv_acc, sems,
    ) = refs
    group, block = pl.program_id(0), pl.program_id(1)

    @pl.when((group == 0) & (block == 0))
    def _():
        chip = place_ref[0] // 2
        copies = fetches(
            w_refs, piece_rows(chip, 1, w_refs[0].shape[1], n_w), w_all, 1, sems, 0
        ) + fetches(x_refs, [rows * k for k in range(blocks)], x_all, 0, sems, n_w)
        for copy in copies:
            copy.start()
        for copy in copies:
            copy.wait()
        for k in range(blocks):
            x_t[:, rows * k : rows * (k + 1)] = x_all[rows * k : rows * (k + 1), :].T
        in_acc[...] = jnp.zeros_like(in_acc)

    @pl.when(block == 0)
    def _():
        dk_acc[...] = jnp.zeros_like(dk_acc)
        dv_acc[...] = jnp.zeros_like(dv_acc)
        sums_ref[...] = jnp.zeros_like(sums_ref)

    own = pl.ds(pl.multiple_of(block * rows, rows), rows)
    q2, do2 = q_ref[...], do_ref[...]
    qt, dot = q2.astype(F32).T, do2.astype(F32).T
    own_keys, own_values = k_ref[own, :].astype(F32).T, v_ref[own, :].astype(F32).T
    own_raw, own_dp = qt * own_keys, dot * own_values
    segq = segq_ref[...]
    dq = jnp.zeros((2 * hs, rows), F32)
    own_ds, own_low = [], []
    for head in range(2):
        target = pair_ref[2 * group + head, block]
        there = pl.ds(pl.multiple_of(target * rows, rows), rows)
        keys, values = k_ref[there, :], v_ref[there, :]
        lanes = head_lanes(q2.shape, head, 1, hs)
        zero = jnp.zeros_like(q2)
        qm, dom = jnp.where(lanes, q2, zero), jnp.where(lanes, do2, zero)
        lse = lse_ref[0, head : head + 1, :]
        scores = mm_rt(keys, qm)
        probs = jnp.exp(jnp.where(segk_ref[there, :] == segq, scores - lse, NEG))
        raw = jnp.sum(own_raw[head * hs : (head + 1) * hs], axis=0, keepdims=True)
        self_prob = jnp.exp(jnp.where(target != block, raw - lse, NEG))
        self_dp = jnp.sum(own_dp[head * hs : (head + 1) * hs], axis=0, keepdims=True)
        dv_acc[there, :] += mm(probs.astype(BF16), dom)
        dprobs = mm_rt(values, dom)
        delta = jnp.sum(probs * dprobs, axis=0, keepdims=True) + self_prob * self_dp
        dscores = (probs * (dprobs - delta)).astype(BF16)
        dk_acc[there, :] += mm(dscores, qm)
        dq = dq + mm_lt(jnp.where(lanes, keys, jnp.zeros_like(keys)), dscores)
        own_ds.append((self_prob * (self_dp - delta)).astype(BF16).astype(F32))
        own_low.append(self_prob.astype(BF16).astype(F32))
    first = head_lanes(dq.shape, 0, 0, hs)
    ds_rows = jnp.where(first, own_ds[0], own_ds[1])
    low_rows = jnp.where(first, own_low[0], own_low[1])
    dq = ((dq + ds_rows * own_keys) * (hs**-0.5)).T
    dq_all[own, :] = dq.astype(BF16)
    sums_ref[0, 0:1, :] += jnp.sum(dq, axis=0, keepdims=True)
    dk_acc[own, :] += (ds_rows * qt).T
    dv_acc[own, :] += (low_rows * dot).T

    @pl.when(block == blocks - 1)
    def _():
        dv = dv_acc[...]
        sums_ref[0, 1:2, :] = jnp.sum(dv, axis=0, keepdims=True)
        packed = jnp.concatenate([dq_all[...], dk_acc[...].astype(BF16), dv.astype(BF16)], axis=1)
        dw_ref[0] = mm(x_t[...], packed)
        in_acc[...] += mm_rt(packed, w_all[group])

    @pl.when((block == blocks - 1) & (group == groups - 1))
    def _():
        half = blocks // 2 * rows
        in_mine[...] = in_acc[:half, :]
        in_other[...] = in_acc[half:, :].astype(BF16)


def attend_back(pairs, place, x_parts, w_pieces, q, k, v, grad_mixed, segq, segk, lse, hs):
    heads, blocks = pairs.shape
    rows, width = x_parts[0].shape
    seq, groups, lanes = rows * blocks, heads // 2, 2 * hs
    half = blocks // 2 * rows
    flops = 4 * seq * width * 3 * groups * lanes + 10 * heads * seq * rows * 2 * lanes
    return pl.pallas_call(
        functools.partial(
            attend_back_kernel, rows=rows, hs=hs, blocks=blocks, groups=groups, n_w=len(w_pieces)
        ),
        grid_spec=pltpu.PrefetchScalarGridSpec(
            num_scalar_prefetch=2,
            grid=(groups, blocks),
            in_specs=[ANY] * (blocks + len(w_pieces))
            + [
                pl.BlockSpec((rows, lanes), lambda g, i, p, q: (i, g)),
                pl.BlockSpec((seq, lanes), lambda g, i, p, q: (0, g)),
                pl.BlockSpec((seq, lanes), lambda g, i, p, q: (0, g)),
                pl.BlockSpec((rows, lanes), lambda g, i, p, q: (i, g)),
                pl.BlockSpec((1, rows), lambda g, i, p, q: (0, i)),
                pl.BlockSpec((seq, 1), lambda g, i, p, q: (0, 0)),
                pl.BlockSpec((1, 8, rows), lambda g, i, p, q: (g, 0, i)),
            ],
            out_specs=[
                pl.BlockSpec((1, width, 3 * lanes), lambda g, i, p, q: (g, 0, 0)),
                pl.BlockSpec((half, width), lambda g, i, p, q: (0, 0)),
                pl.BlockSpec((half, width), lambda g, i, p, q: (0, 0)),
                pl.BlockSpec((1, 8, lanes), lambda g, i, p, q: (g, 0, 0)),
            ],
            scratch_shapes=[
                pltpu.VMEM((seq, width), BF16),
                pltpu.VMEM((width, seq), BF16),
                pltpu.VMEM((groups, width, 3 * lanes), BF16),
                pltpu.VMEM((seq, width), F32),
                pltpu.VMEM((seq, lanes), BF16),
                pltpu.VMEM((seq, lanes), F32),
                pltpu.VMEM((seq, lanes), F32),
                pltpu.SemaphoreType.DMA((blocks + len(w_pieces),)),
            ],
        ),
        out_shape=[
            jax.ShapeDtypeStruct((groups, width, 3 * lanes), F32),
            jax.ShapeDtypeStruct((half, width), F32),
            jax.ShapeDtypeStruct((half, width), BF16),
            jax.ShapeDtypeStruct((groups, 8, lanes), F32),
        ],
        compiler_params=pltpu.CompilerParams(vmem_limit_bytes=LIMIT),
        cost_estimate=pl.CostEstimate(flops=flops, bytes_accessed=30 << 20, transcendentals=0),
        name="attend_back",
    )(pairs, place, *x_parts, *w_pieces, q, k, v, grad_mixed, segq, segk, lse)


def norm(values):
    centred = values - jnp.mean(values, axis=-1, keepdims=True)
    scale = lax.rsqrt(jnp.mean(centred * centred, axis=-1, keepdims=True) + EPS)
    return centred * scale, scale


def norm_back(grad, unit, scale, gain):
    q = grad * gain
    mean_q = jnp.mean(q, axis=-1, keepdims=True)
    mean_qn = jnp.mean(q * unit, axis=-1, keepdims=True)
    return scale * (q - mean_q - unit * mean_qn)


def gelu_parts(u):
    dense = jnp.exp(-0.5 * u * u) * 0.3989422804014327
    t = 1.0 / (1.0 + 0.2316419 * jnp.abs(u))
    poly = t * (
        0.319381530
        + t * (-0.356563782 + t * (1.781477937 + t * (-1.821255978 + t * 1.330274429)))
    )
    tail = dense * poly
    phi = jnp.where(u >= 0, 1.0 - tail, tail)
    return u * phi, phi + u * dense


def dense_kernel(place_ref, *refs, n_o, n_w, chunks):
    o_refs, refs = refs[:n_o], refs[n_o:]
    w_refs, refs = refs[:n_w], refs[n_w:]
    (
        x_ref, mine_ref, other_ref, cot_ref, vec_ref, upb_ref,
        layer_ref, gm_mine, gm_other, act_ref, mlow_ref, gb_ref, gul_ref, ga_ref, gone_ref, sums_ref, upsum_ref,
        wo, ww, slope, acc, sems,
    ) = refs
    step = pl.program_id(0)
    core = place_ref[0] % 2
    cols = mine_ref.shape[1]
    width = x_ref.shape[1]
    units = ww.shape[2] // 2

    @pl.when(step == 0)
    def _():
        o_copies = fetches(o_refs, piece_rows(place_ref[0], 1, o_refs[0].shape[0], n_o), wo, 0, sems, 0)
        w_copies = fetches(w_refs, piece_rows(place_ref[0], 1, w_refs[0].shape[1], n_w), ww, 1, sems, n_o)
        for copy in o_copies + w_copies:
            copy.start()
        for copy in o_copies + w_copies:
            copy.wait()
        sums_ref[...] = jnp.zeros_like(sums_ref)
        upsum_ref[...] = jnp.zeros_like(upsum_ref)

    mine_cols = pl.ds(pl.multiple_of(core * cols, cols), cols)
    other_cols = pl.ds(pl.multiple_of((1 - core) * cols, cols), cols)
    attn = mm_rt(mine_ref[...], wo[:, mine_cols]) + mm_rt(other_ref[...], wo[:, other_cols])
    unit_one, scale_one = norm(x_ref[...].astype(F32) + attn + vec_ref[0:1, :])
    middle = unit_one * vec_ref[1:2, :] + vec_ref[2:3, :]
    mlow_ref[...] = middle.astype(BF16)
    acc[...] = middle + vec_ref[3:4, :]

    @pl.loop(0, chunks)
    def _(k):
        place = pl.ds(pl.multiple_of(k * units, units), units)
        upper = mm(mlow_ref[...], ww[k, :, :units]) + upb_ref[:, place]
        active, rise = gelu_parts(upper)
        active = active.astype(BF16)
        act_ref[:, place] = active
        slope[:, place] = rise.astype(BF16)
        acc[...] += mm_rt(active, ww[k, :, units:])

    unit_two, scale_two = norm(acc[...])
    gain_two = vec_ref[4:5, :]
    layer_ref[...] = (unit_two * gain_two + vec_ref[5:6, :]).astype(BF16)
    cot = cot_ref[...].astype(F32)
    grad_two = norm_back(cot, unit_two, scale_two, gain_two)
    sums_ref[4:5, :] += jnp.sum(cot * unit_two, axis=0, keepdims=True)
    sums_ref[5:6, :] += jnp.sum(cot, axis=0, keepdims=True)
    sums_ref[3:4, :] += jnp.sum(grad_two, axis=0, keepdims=True)
    gb_ref[...] = grad_two.astype(BF16)
    acc[...] = grad_two

    @pl.loop(0, chunks)
    def _(k):
        place = pl.ds(pl.multiple_of(k * units, units), units)
        grad_upper = mm(gb_ref[...], ww[k, :, units:]) * slope[:, place].astype(F32)
        upsum_ref[:, place] += jnp.sum(grad_upper, axis=0, keepdims=True)
        grad_low = grad_upper.astype(BF16)
        gul_ref[:, place] = grad_low
        acc[...] += mm_rt(grad_low, ww[k, :, :units])

    grad_mid = acc[...]
    sums_ref[1:2, :] += jnp.sum(grad_mid * unit_one, axis=0, keepdims=True)
    sums_ref[2:3, :] += jnp.sum(grad_mid, axis=0, keepdims=True)
    grad_one = norm_back(grad_mid, unit_one, scale_one, vec_ref[1:2, :])
    sums_ref[0:1, :] += jnp.sum(grad_one, axis=0, keepdims=True)
    gone_ref[...] = grad_one
    grad_attn = grad_one.astype(BF16)
    ga_ref[...] = grad_attn
    gm_mine[...] = mm(grad_attn, wo[:, mine_cols]).astype(BF16)
    gm_other[...] = mm(grad_attn, wo[:, other_cols]).astype(BF16)


def dense(place, o_pieces, w_pieces, x, mine, other, cot, vec, upb, tile):
    count, width = x.shape
    cols = other.shape[1]
    chunks, units = w_pieces[0].shape[0], w_pieces[0].shape[2] // 2
    rows = lambda n: pl.BlockSpec((tile, n), lambda i, p: (i, 0))
    fixed = lambda a, b: pl.BlockSpec((a, b), lambda i, p: (0, 0))
    full = chunks * units
    shapes = [
        ((count, width), BF16), ((count, cols), BF16), ((count, cols), BF16), ((count, full), BF16),
        ((count, width), BF16), ((count, width), BF16), ((count, full), BF16), ((count, width), BF16),
        ((count, width), F32), ((8, width), F32), ((1, full), F32),
    ]
    flops = 8 * count * width * full + 4 * count * width * 2 * cols
    return pl.pallas_call(
        functools.partial(dense_kernel, n_o=len(o_pieces), n_w=len(w_pieces), chunks=chunks),
        grid_spec=pltpu.PrefetchScalarGridSpec(
            num_scalar_prefetch=1,
            grid=(count // tile,),
            in_specs=[ANY] * (len(o_pieces) + len(w_pieces))
            + [rows(width), rows(cols), rows(cols), rows(width), fixed(8, width), fixed(1, full)],
            out_specs=[
                rows(width), rows(cols), rows(cols), rows(full), rows(width), rows(width), rows(full),
                rows(width), rows(width), fixed(8, width), fixed(1, full),
            ],
            scratch_shapes=[
                pltpu.VMEM((width, 2 * cols), BF16),
                pltpu.VMEM((chunks, width, 2 * units), BF16),
                pltpu.VMEM((tile, full), BF16),
                pltpu.VMEM((tile, width), F32),
                pltpu.SemaphoreType.DMA((len(o_pieces) + len(w_pieces),)),
            ],
        ),
        out_shape=[jax.ShapeDtypeStruct(*s) for s in shapes],
        compiler_params=pltpu.CompilerParams(vmem_limit_bytes=LIMIT),
        cost_estimate=pl.CostEstimate(flops=flops, bytes_accessed=40 << 20, transcendentals=0),
        name="dense",
    )(place, *o_pieces, *w_pieces, x, mine, other, cot, vec, upb)


def grad_kernel(place_ref, *refs, n_r, drows, pairs):
    left_ref, right_refs, (ours_ref, theirs_ref, left_t, acc) = refs[0], refs[1 : 1 + n_r], refs[1 + n_r :]
    core = place_ref[0] % 2

    @pl.when(pl.program_id(0) == 0)
    def _():
        left_t[...] = left_ref[...].T

    if n_r == 1:
        acc[...] = mm(left_t[...], right_refs[0][...])
    else:
        cols = right_refs[0].shape[1]
        mine_cols = pl.ds(pl.multiple_of(core * cols, cols), cols)
        other_cols = pl.ds(pl.multiple_of((1 - core) * cols, cols), cols)
        acc[:, mine_cols] = mm(left_t[...], right_refs[0][...])
        acc[:, other_cols] = mm(left_t[...], right_refs[1][...])
    for p in range(pairs):
        ours_ref[p] = acc[pl.ds(pl.multiple_of((2 * p + core) * drows, drows), drows), :]
        theirs_ref[p] = acc[pl.ds(pl.multiple_of((2 * p + 1 - core) * drows, drows), drows), :].astype(BF16)


def weight_grad(place, left, rights, drows, tile):
    width, pairs = left.shape[1], left.shape[1] // (2 * drows)
    count = left.shape[0]
    if drows % 8:
        right = rights[0]
        if len(rights) > 1:
            right = jnp.where(
                place[0] % 2 == 0,
                jnp.concatenate([rights[0][:count], rights[1]], axis=1),
                jnp.concatenate([rights[1], rights[0][:count]], axis=1),
            )
        view = mm_lt(left, right).reshape(pairs, 2, drows, right.shape[1])
        ours = lax.dynamic_index_in_dim(view, place[0] % 2, 1, keepdims=False)
        theirs = lax.dynamic_index_in_dim(view, 1 - place[0] % 2, 1, keepdims=False)
        return ours, theirs.astype(BF16)
    cols = sum(r.shape[1] for r in rights)
    if len(rights) > 1:
        tile = cols
    block = tile // len(rights)
    return pl.pallas_call(
        functools.partial(grad_kernel, n_r=len(rights), drows=drows, pairs=pairs),
        grid_spec=pltpu.PrefetchScalarGridSpec(
            num_scalar_prefetch=1,
            grid=(cols // tile,),
            in_specs=[pl.BlockSpec((count, width), lambda i, p: (0, 0))]
            + [pl.BlockSpec((count, block), lambda i, p: (0, i))] * len(rights),
            out_specs=[pl.BlockSpec((pairs, drows, tile), lambda i, p: (0, 0, i))] * 2,
            scratch_shapes=[pltpu.VMEM((width, count), BF16), pltpu.VMEM((width, tile), F32)],
        ),
        out_shape=[
            jax.ShapeDtypeStruct((pairs, drows, cols), F32),
            jax.ShapeDtypeStruct((pairs, drows, cols), BF16),
        ],
        compiler_params=pltpu.CompilerParams(vmem_limit_bytes=LIMIT),
        cost_estimate=pl.CostEstimate(
            flops=2 * count * width * cols, bytes_accessed=8 * width * cols, transcendentals=0
        ),
        name="weight_grad",
    )(place, left, *rights)


def xor_order(parts, index):
    parts = list(parts)
    bit = 1
    while bit < len(parts):
        odd = (index // bit) % 2 == 1
        parts = [jnp.where(odd, parts[k ^ bit], parts[k]) for k in range(len(parts))]
        bit *= 2
    return parts


def per_device(
    tokens,
    segments,
    pairing,
    qkv_weight,
    qv_bias,
    out_weight,
    out_bias,
    first_gain,
    first_shift,
    up_weight,
    up_bias,
    down_weight,
    down_bias,
    second_gain,
    second_shift,
    cotangent,
):
    width = tokens.shape[2]
    rows = tokens.shape[1]
    lheads, blocks = pairing.shape
    hs = qv_bias.shape[1] // 2
    lanes = 2 * hs
    units = up_weight.shape[1]
    ndp, nt = lax.axis_size("dp"), lax.axis_size("tensor")
    drows = width // ndp
    chips = ndp // 2
    dp, tensor = lax.axis_index("dp"), lax.axis_index("tensor")
    core, chip, half, low = dp % 2, dp // 2, tensor // 2, tensor % 2
    slot_mask = 2 * core + low
    heads = 2 * lheads
    cols = heads * hs
    aligned = drows % 8 == 0
    place = jnp.stack([dp, tensor]).astype(jnp.int32)
    order = [0, 1, 3, 4, 2, 5]

    core_pairs = [(i, i ^ 1) for i in range(ndp)]

    def core_swap(x):
        return lax.ppermute(x, "dp", core_pairs)

    def z_step(x, k):
        return lax.ppermute(x, "tensor", [(i, i ^ k) for i in range(nt)])

    def chip_step(x, k):
        return lax.ppermute(x, "dp", [(i, i ^ (2 * k)) for i in range(ndp)])

    def column(k, flip, back):
        steps = []
        for p in range(chips):
            for c in range(2):
                for a in range(2):
                    for b in range(2):
                        home = (2 * p + c) * nt + 2 * a + b
                        away = (2 * p + (a ^ flip)) * nt + 2 * c + (b ^ k)
                        steps.append((away, home) if back else (home, away))
        return steps

    def to_sequence(x):
        return [
            lax.ppermute(
                lax.dynamic_index_in_dim(x, low ^ k, 0, keepdims=False), BOTH, column(k, 0, False)
            )
            for k in range(2)
        ]

    def to_home(parts):
        first, second = [lax.ppermute(parts[k], BOTH, column(k, 0, True)) for k in range(2)]
        return jnp.stack([jnp.where(low == 0, first, second), jnp.where(low == 0, second, first)])

    def z_all(x):
        return [x] + [z_step(x, k) for k in range(1, nt)]

    def chip_all(x):
        return [x] + [chip_step(x, k) for k in range(1, chips)]

    small = jnp.concatenate([pairing.astype(BF16).reshape(-1), qv_bias.reshape(-1), up_bias])
    n_pair, n_qv = lheads * blocks, lheads * lanes
    small_rel = z_all(small)
    small = jnp.stack(xor_order(small_rel, tensor))
    all_pairs = small[:, :n_pair].astype(jnp.int32).reshape(2, heads, blocks)
    my_pairs = jnp.where(core == 0, all_pairs[0], all_pairs[1])
    pair_slots = jnp.stack(xor_order([my_pairs[:, k] for k in range(blocks)], slot_mask), axis=1) ^ slot_mask
    pair_slots = jnp.stack([pair_slots[h] for h in order])
    all_qvb = small[:, n_pair : n_pair + n_qv].astype(F32).reshape(2, heads, lanes)
    my_qvb = jnp.where(core == 0, all_qvb[0], all_qvb[1])
    my_qvb = jnp.stack([my_qvb[h] for h in order])
    up_bias_rel = jnp.concatenate([s[n_pair + n_qv :] for s in small_rel]).astype(F32)
    groups = heads // 2
    bias = jnp.concatenate(
        [
            my_qvb[:, :hs].reshape(groups, lanes),
            jnp.zeros((groups, lanes), F32),
            my_qvb[:, hs:].reshape(groups, lanes),
        ],
        axis=1,
    ).reshape(groups, 1, 3 * lanes)

    segs = jnp.where(half == core, segments, core_swap(segments))
    seg_rows = jnp.where(low == 0, segs[0], segs[1]).reshape(blocks, rows)
    seg_row = jnp.concatenate(xor_order([seg_rows[k] for k in range(blocks)], slot_mask))
    seg_col = seg_row.reshape(blocks * rows, 1)
    seg_row = seg_row.reshape(1, blocks * rows)

    qkv_local = qkv_weight.reshape(drows, lheads, 3, hs).transpose(0, 2, 1, 3)
    qkv_local = jnp.concatenate(
        [qkv_local[:, :, :2].reshape(drows, 3 * lanes), qkv_local[:, :, 2].reshape(drows, 3 * hs)], axis=1
    )
    qkv_abs = xor_order(z_all(qkv_local), tensor)

    def regroup(first, second):
        left, right = first[:, 3 * lanes :], second[:, 3 * lanes :]
        both = [part[:, hs * k : hs * (k + 1)] for k in range(3) for part in (left, right)]
        return jnp.stack([first[:, : 3 * lanes], second[:, : 3 * lanes], jnp.concatenate(both, axis=1)])

    zero_heads, one_heads = regroup(qkv_abs[0], qkv_abs[1]), regroup(qkv_abs[2], qkv_abs[3])
    keep = jnp.where(core == 0, zero_heads, one_heads)
    got = core_swap(jnp.where(core == 0, one_heads, zero_heads))
    chip_rows = jnp.where(
        core == 0, jnp.concatenate([keep, got], axis=1), jnp.concatenate([got, keep], axis=1)
    )
    qkv_pieces = chip_all(chip_rows)
    if not aligned:
        qkv_pieces = [jnp.concatenate(xor_order(qkv_pieces, chip), axis=1)]

    mine = to_sequence(tokens)
    x_parts = mine + [core_swap(part) for part in mine]
    x_mine = jnp.concatenate(mine)

    out_abs = xor_order(z_all(out_weight.reshape(lheads * hs, drows).T), tensor)
    out_cols = []
    for u in range(2):
        first, second = out_abs[2 * u], out_abs[2 * u + 1]
        out_cols += [first[:, :lanes], second[:, :lanes], first[:, lanes:], second[:, lanes:]]
    out_own = chip_all(jnp.concatenate(out_cols, axis=1))
    out_pieces = [part for own in out_own for part in (own, core_swap(own))]

    ff_own = chip_all(jnp.stack(z_all(jnp.concatenate([up_weight, down_weight.T], axis=1))))
    ff_pieces = [part for own in ff_own for part in (own, core_swap(own))]
    if not aligned:
        out_pieces = [jnp.concatenate(xor_order(out_pieces, dp))]
        ff_pieces = [jnp.concatenate(xor_order(ff_pieces, dp), axis=1)]
    upstream = jnp.concatenate(to_sequence(cotangent))

    q, k, v, mixed, lse = attend(pair_slots, place, x_parts, qkv_pieces, bias, seg_row, seg_col, hs)
    count = blocks // 2 * rows
    other = core_swap(mixed[count:])

    blank = jnp.zeros((width,), BF16)
    vec = jnp.stack(
        [out_bias, first_gain, first_shift, down_bias, second_gain, second_shift, blank, blank]
    ).astype(F32)
    (
        layer_mine, gm_mine, gm_other, active, middle_low, grad_branch, grad_upper, grad_attn, grad_one, sums, up_sums,
    ) = dense(
        place, out_pieces, ff_pieces, x_mine, mixed, other, upstream, vec, up_bias_rel.reshape(1, nt * units), 256
    )
    layer_out = to_home([layer_mine[:rows], layer_mine[rows:]])

    def reduce_plane(view):
        total = lax.dynamic_index_in_dim(view, chip, 0, keepdims=False)
        for k in range(1, chips):
            part = lax.dynamic_index_in_dim(view, chip ^ k, 0, keepdims=False).astype(BF16)
            total = total + chip_step(part, k).astype(F32)
        return total

    def reduce_weight(left, rights):
        ours, theirs = weight_grad(place, left, rights, drows, 512)
        return reduce_plane(ours + core_swap(theirs).astype(F32))

    def reduce_relative(grad):
        total = grad[:, :units]
        for k in range(1, nt):
            part = grad[:, units * k : units * (k + 1)].astype(BF16)
            total = total + z_step(part, k).astype(F32)
        return total

    down_grad = reduce_relative(reduce_weight(grad_branch, [active])).T
    up_grad = reduce_relative(reduce_weight(middle_low, [grad_upper]))
    out_sum = reduce_weight(grad_attn, [mixed, other])
    out_parts = []
    for u in range(2):
        base = u * cols
        for w in range(2):
            out_parts.append(
                jnp.concatenate(
                    [
                        out_sum[:, base + lanes * w : base + lanes * (w + 1)],
                        out_sum[:, base + 2 * lanes + hs * w : base + 2 * lanes + hs * (w + 1)],
                    ],
                    axis=1,
                )
            )
    out_rel = xor_order(out_parts, tensor)
    out_grad = out_rel[0]
    for step in range(1, nt):
        out_grad = out_grad + z_step(out_rel[step].astype(BF16), step).astype(F32)
    out_grad = out_grad.T.reshape(lheads, hs, drows)

    def all_sum(x):
        for bit in range(nt.bit_length() - 1):
            x = x + z_step(x, 1 << bit)
        for bit in range(ndp.bit_length() - 1):
            x = x + lax.ppermute(x, "dp", [(i, i ^ (1 << bit)) for i in range(ndp)])
        return x

    up_abs = xor_order([up_sums[0, units * k : units * (k + 1)] for k in range(nt)], tensor)
    sums = all_sum(jnp.concatenate([sums[:6].reshape(-1)] + up_abs))
    outb_grad, gain_one_grad, shift_one_grad, downb_grad, gain_two_grad, shift_two_grad = [
        sums[i * width : (i + 1) * width] for i in range(6)
    ]
    upb_grad = lax.dynamic_slice(sums, (6 * width + tensor * units,), (units,))

    gm_all = jnp.concatenate([gm_mine, core_swap(gm_other)])
    qkv_part, in_mine, in_other, head_sums = attend_back(
        pair_slots, place, x_parts, qkv_pieces, q, k, v, gm_all, seg_row, seg_col, lse, hs
    )
    in_low = (in_mine + core_swap(in_other).astype(F32) + grad_one).astype(BF16)
    input_grad = to_home([in_low[:rows], in_low[rows:]])

    view = qkv_part.reshape(groups, chips, 2 * drows, 3 * lanes).transpose(1, 0, 2, 3)
    qkv_sum = reduce_plane(view).reshape(groups, 2, drows, 3 * lanes)

    def share(c, u):
        third = [qkv_sum[2, c][:, lanes * k + hs * u : lanes * k + hs * (u + 1)] for k in range(3)]
        return jnp.concatenate([qkv_sum[u, c]] + third, axis=1)

    shares = [[share(c, u).astype(BF16) for u in range(2)] for c in range(2)]
    qkv_grad = jnp.zeros((drows, 3 * lheads * hs), F32)
    for flip in range(2):
        for step in range(2):
            by_core = [jnp.where((low ^ step) == 0, shares[c][0], shares[c][1]) for c in range(2)]
            sent = jnp.where((half ^ flip) == 0, by_core[0], by_core[1])
            qkv_grad = qkv_grad + lax.ppermute(sent, BOTH, column(step, flip, False)).astype(F32)
    pairs_part = qkv_grad[:, : 3 * lanes].reshape(drows, 3, 2, hs)
    third_part = qkv_grad[:, 3 * lanes :].reshape(drows, 3, 1, hs)
    qkv_grad = jnp.concatenate([pairs_part, third_part], axis=2).transpose(0, 2, 1, 3)
    qkv_grad = qkv_grad.reshape(drows, lheads, 3 * hs)

    q_sum = head_sums[:, 0, :].reshape(heads, hs)
    v_sum = head_sums[:, 1, :].reshape(heads, hs)
    own_qvb = jnp.concatenate([q_sum, v_sum], axis=1)
    own_qvb = jnp.stack([own_qvb[order.index(h)] for h in range(heads)])
    blank = jnp.zeros_like(own_qvb)
    both = jnp.concatenate([jnp.where(core == 0, own_qvb, blank), jnp.where(core == 0, blank, own_qvb)])
    both = all_sum(both)
    qvb_grad = lax.dynamic_slice(both, (tensor * lheads, 0), (lheads, lanes))
    return (
        layer_out,
        input_grad,
        qkv_grad,
        qvb_grad,
        out_grad,
        outb_grad,
        gain_one_grad,
        shift_one_grad,
        up_grad,
        upb_grad,
        down_grad,
        downb_grad,
        gain_two_grad,
        shift_two_grad,
    )


def solution(mesh):
    return jax.shard_map(
        per_device,
        mesh=mesh,
        in_specs=(
            P("dp", "tensor", None),
            P("dp", None),
            P("tensor", None),
            P("dp", "tensor", None),
            P("tensor", None),
            P("tensor", None, "dp"),
            P(),
            P(),
            P(),
            P("dp", "tensor"),
            P("tensor"),
            P("tensor", "dp"),
            P(),
            P(),
            P(),
            P("dp", "tensor", None),
        ),
        out_specs=(
            P("dp", "tensor", None),
            P("dp", "tensor", None),
            P("dp", "tensor", None),
            P("tensor", None),
            P("tensor", None, "dp"),
            P(),
            P(),
            P(),
            P("dp", "tensor"),
            P("tensor"),
            P("tensor", "dp"),
            P(),
            P(),
            P(),
        ),
        check_vma=False,
    )
```

```python
import functools

import jax
import jax.numpy as jnp
from jax import lax
from jax.experimental import pallas as pl
from jax.experimental.pallas import tpu as pltpu
from jax.sharding import PartitionSpec as P

EPS = 1e-06
NEG = -1e30
BOTH = ("dp", "tensor")
F32 = jnp.float32
BF16 = jnp.bfloat16
ANY = pl.BlockSpec(memory_space=pl.ANY)
LIMIT = 58 << 20


def mm(left, right):
    return lax.dot_general(left, right, (((1,), (0,)), ((), ())), preferred_element_type=F32)


def mm_rt(left, right):
    return lax.dot_general(left, right, (((1,), (1,)), ((), ())), preferred_element_type=F32)


def mm_lt(left, right):
    return lax.dot_general(left, right, (((0,), (0,)), ((), ())), preferred_element_type=F32)


def head_lanes(shape, head, dim, head_size):
    place = lax.broadcasted_iota(jnp.int32, shape, dim)
    return (place < head_size) if head == 0 else (place >= head_size)


def fetches(pieces, offsets, target, dim, sems, first):
    copies = []
    for k, (piece, offset) in enumerate(zip(pieces, offsets)):
        count = piece.shape[dim]
        where = pl.ds(offset if isinstance(offset, int) else pl.multiple_of(offset, count), count)
        index = (slice(None),) * dim + (where,)
        copies.append(pltpu.make_async_copy(piece, target.at[index], sems.at[first + k]))
    return copies


def piece_rows(place, step, rows, count):
    if count == 1:
        return [0]
    return [(place ^ (k * step)) * rows for k in range(count)]


def attend_kernel(pair_ref, place_ref, *refs, rows, hs, blocks, n_w):
    x_refs, refs = refs[:2], refs[2:]
    w_refs, refs = refs[:n_w], refs[n_w:]
    bias_ref, segq_ref, segk_ref, q_out, k_out, v_out, o_mine, o_other, lse_ref, w_all, x_all, sems = refs
    group, block = pl.program_id(0), pl.program_id(1)
    lanes2 = 2 * hs

    @pl.when((group == 0) & (block == 0))
    def _():
        chip = place_ref[0] // 2
        w_parts = [piece.at[: w_all.shape[0]] for piece in w_refs]
        copies = fetches(
            w_parts, piece_rows(chip, 1, w_refs[0].shape[1], n_w), w_all, 1, sems, 0
        ) + fetches(x_refs, [0, x_refs[0].shape[0]], x_all, 0, sems, n_w)
        for copy in copies:
            copy.start()
        for copy in copies:
            copy.wait()

    @pl.when(block == 0)
    def _():
        weight = w_all[group]
        for k in range(blocks):
            part = pl.ds(k * rows, rows)
            out = (mm(x_all[part, :], weight) + bias_ref[0]).astype(BF16)
            q_out[part, :] = out[:, :lanes2] * (hs**-0.5)
            k_out[part, :] = out[:, lanes2 : 2 * lanes2]
            v_out[part, :] = out[:, 2 * lanes2 :]

    own = pl.ds(pl.multiple_of(block * rows, rows), rows)
    q2 = q_out[own, :]
    own_raw = (q2.astype(F32) * k_out[own, :].astype(F32)).T
    own_values = v_out[own, :].astype(F32).T
    segq = segq_ref[...]
    total = jnp.zeros((2 * hs, rows), F32)
    for head in range(2):
        target = pair_ref[2 * group + head, block]
        there = pl.ds(pl.multiple_of(target * rows, rows), rows)
        keys, values = k_out[there, :], v_out[there, :]
        lanes = head_lanes(q2.shape, head, 1, hs)
        scores = mm_rt(keys, jnp.where(lanes, q2, jnp.zeros_like(q2)))
        scores = jnp.where(segk_ref[there, :] == segq, scores, NEG)
        raw = jnp.sum(own_raw[head * hs : (head + 1) * hs], axis=0, keepdims=True)
        raw = jnp.where(target != block, raw, NEG)
        peak = jnp.maximum(jnp.max(scores, axis=0, keepdims=True), raw)
        expo = jnp.exp(scores - peak)
        own_expo = jnp.exp(raw - peak)
        denom = jnp.sum(expo, axis=0, keepdims=True) + own_expo
        masked_values = jnp.where(lanes, values, jnp.zeros_like(values))
        part = mm_lt(masked_values, expo.astype(BF16))
        low = own_expo.astype(BF16).astype(F32)
        mine = head_lanes(part.shape, head, 0, hs)
        part = part + jnp.where(mine, own_values * low, 0.0)
        total = total + part * (1.0 / denom)
        lse_ref[0, head : head + 1, :] = peak + jnp.log(denom)
    mixed = total.T.astype(BF16)

    @pl.when(block < blocks // 2)
    def _():
        o_mine[pl.ds(pl.multiple_of(block * rows, rows), rows), :] = mixed

    @pl.when(block >= blocks // 2)
    def _():
        o_other[pl.ds(pl.multiple_of((block - blocks // 2) * rows, rows), rows), :] = mixed


def attend(pairs, place, x_parts, w_pieces, bias, segq, segk, hs):
    heads, blocks = pairs.shape
    width = x_parts[0].shape[1]
    seq, groups, lanes = 2 * x_parts[0].shape[0], heads // 2, 2 * hs
    rows = seq // blocks
    kept = jax.ShapeDtypeStruct((seq, groups * lanes), BF16)
    flops = 2 * seq * width * 3 * groups * lanes + 4 * heads * seq * rows * 2 * lanes
    return pl.pallas_call(
        functools.partial(attend_kernel, rows=rows, hs=hs, blocks=blocks, n_w=len(w_pieces)),
        grid_spec=pltpu.PrefetchScalarGridSpec(
            num_scalar_prefetch=2,
            grid=(groups, blocks),
            in_specs=[ANY] * (2 + len(w_pieces))
            + [
                pl.BlockSpec((1, 1, 3 * lanes), lambda g, i, p, q: (g, 0, 0)),
                pl.BlockSpec((1, rows), lambda g, i, p, q: (0, i)),
                pl.BlockSpec((seq, 1), lambda g, i, p, q: (0, 0)),
            ],
            out_specs=[pl.BlockSpec((seq, lanes), lambda g, i, p, q: (0, g))] * 3
            + [
                pl.BlockSpec((seq // 2, lanes), lambda g, i, p, q: (0, g)),
                pl.BlockSpec((seq // 2, lanes), lambda g, i, p, q: (0, g)),
                pl.BlockSpec((1, 8, rows), lambda g, i, p, q: (g, 0, i)),
                pl.BlockSpec((groups, width, 3 * lanes), lambda g, i, p, q: (0, 0, 0)),
            ],
            scratch_shapes=[
                pltpu.VMEM((seq, width), BF16),
                pltpu.SemaphoreType.DMA((2 + len(w_pieces),)),
            ],
        ),
        out_shape=[kept] * 3
        + [jax.ShapeDtypeStruct((seq // 2, groups * lanes), BF16)] * 2
        + [
            jax.ShapeDtypeStruct((groups, 8, seq), F32),
            jax.ShapeDtypeStruct((groups, width, 3 * lanes), BF16),
        ],
        compiler_params=pltpu.CompilerParams(vmem_limit_bytes=LIMIT),
        cost_estimate=pl.CostEstimate(flops=flops, bytes_accessed=20 << 20, transcendentals=0),
        name="attend",
    )(pairs, place, *x_parts, *w_pieces, bias, segq, segk)


def attend_back_kernel(
    pair_ref, group_ref, q_ref, k_ref, v_ref, do_a, do_b, segq_ref, segk_ref, lse_ref,
    packed_ref, sums_ref, dq_all, dk_acc, dv_acc, *, rows, hs, blocks,
):
    block = pl.program_id(0)

    @pl.when(block == 0)
    def _():
        dk_acc[...] = jnp.zeros_like(dk_acc)
        dv_acc[...] = jnp.zeros_like(dv_acc)
        sums_ref[...] = jnp.zeros_like(sums_ref)

    own = pl.ds(pl.multiple_of(block * rows, rows), rows)
    q2, do2 = q_ref[...], jnp.where(block < blocks // 2, do_a[...], do_b[...])
    qt, dot = q2.astype(F32).T, do2.astype(F32).T
    own_keys, own_values = k_ref[own, :].astype(F32).T, v_ref[own, :].astype(F32).T
    own_raw, own_dp = qt * own_keys, dot * own_values
    segq = segq_ref[...]
    dq = jnp.zeros((2 * hs, rows), F32)
    own_ds, own_low = [], []
    for head in range(2):
        target = pair_ref[2 * group_ref[0] + head, block]
        there = pl.ds(pl.multiple_of(target * rows, rows), rows)
        keys, values = k_ref[there, :], v_ref[there, :]
        lanes = head_lanes(q2.shape, head, 1, hs)
        zero = jnp.zeros_like(q2)
        qm, dom = jnp.where(lanes, q2, zero), jnp.where(lanes, do2, zero)
        lse = lse_ref[0, head : head + 1, :]
        scores = mm_rt(keys, qm)
        probs = jnp.exp(jnp.where(segk_ref[there, :] == segq, scores - lse, NEG))
        raw = jnp.sum(own_raw[head * hs : (head + 1) * hs], axis=0, keepdims=True)
        self_prob = jnp.exp(jnp.where(target != block, raw - lse, NEG))
        self_dp = jnp.sum(own_dp[head * hs : (head + 1) * hs], axis=0, keepdims=True)
        dv_acc[there, :] += mm(probs.astype(BF16), dom)
        dprobs = mm_rt(values, dom)
        delta = jnp.sum(probs * dprobs, axis=0, keepdims=True) + self_prob * self_dp
        dscores = (probs * (dprobs - delta)).astype(BF16)
        dk_acc[there, :] += mm(dscores, qm)
        dq = dq + mm_lt(jnp.where(lanes, keys, jnp.zeros_like(keys)), dscores)
        own_ds.append((self_prob * (self_dp - delta)).astype(BF16).astype(F32))
        own_low.append(self_prob.astype(BF16).astype(F32))
    first = head_lanes(dq.shape, 0, 0, hs)
    ds_rows = jnp.where(first, own_ds[0], own_ds[1])
    low_rows = jnp.where(first, own_low[0], own_low[1])
    dq = ((dq + ds_rows * own_keys) * (hs**-0.5)).T
    dq_all[own, :] = dq.astype(BF16)
    sums_ref[0:1, :] += jnp.sum(dq, axis=0, keepdims=True)
    dk_acc[own, :] += (ds_rows * qt).T
    dv_acc[own, :] += (low_rows * dot).T

    @pl.when(block == blocks - 1)
    def _():
        dv = dv_acc[...]
        sums_ref[1:2, :] = jnp.sum(dv, axis=0, keepdims=True)
        packed_ref[...] = jnp.concatenate(
            [dq_all[...], dk_acc[...].astype(BF16), dv.astype(BF16)], axis=1
        )


def attend_back(pairs, group, q, k, v, grad_a, grad_b, segq, segk, lse, hs):
    heads, blocks = pairs.shape
    seq, lanes = q.shape[0], 2 * hs
    rows, half = seq // blocks, blocks // 2
    return pl.pallas_call(
        functools.partial(attend_back_kernel, rows=rows, hs=hs, blocks=blocks),
        grid_spec=pltpu.PrefetchScalarGridSpec(
            num_scalar_prefetch=2,
            grid=(blocks,),
            in_specs=[
                pl.BlockSpec((rows, lanes), lambda i, p, g: (i, g[0])),
                pl.BlockSpec((seq, lanes), lambda i, p, g: (0, g[0])),
                pl.BlockSpec((seq, lanes), lambda i, p, g: (0, g[0])),
                pl.BlockSpec((rows, lanes), lambda i, p, g: (jnp.minimum(i, half - 1), g[0])),
                pl.BlockSpec((rows, lanes), lambda i, p, g: (jnp.maximum(i - half, 0), g[0])),
                pl.BlockSpec((1, rows), lambda i, p, g: (0, i)),
                pl.BlockSpec((seq, 1), lambda i, p, g: (0, 0)),
                pl.BlockSpec((1, 8, rows), lambda i, p, g: (g[0], 0, i)),
            ],
            out_specs=[
                pl.BlockSpec((seq, 3 * lanes), lambda i, p, g: (0, 0)),
                pl.BlockSpec((8, lanes), lambda i, p, g: (0, 0)),
            ],
            scratch_shapes=[
                pltpu.VMEM((seq, lanes), BF16),
                pltpu.VMEM((seq, lanes), F32),
                pltpu.VMEM((seq, lanes), F32),
            ],
        ),
        out_shape=[
            jax.ShapeDtypeStruct((seq, 3 * lanes), BF16),
            jax.ShapeDtypeStruct((8, lanes), F32),
        ],
        compiler_params=pltpu.CompilerParams(vmem_limit_bytes=LIMIT),
        cost_estimate=pl.CostEstimate(
            flops=10 * 2 * seq * rows * 2 * lanes, bytes_accessed=6 << 20, transcendentals=0
        ),
        name="attend_back",
    )(pairs, jnp.full((1,), group, jnp.int32), q, k, v, grad_a, grad_b, segq, segk, lse)


def qkv_grad_kernel(place_ref, xa_ref, xb_ref, p0_ref, p1_ref, p2_ref, keep_ref, send_ref, acc):
    half = xa_ref.shape[0]
    chip = place_ref[0] // 2
    rows = keep_ref.shape[2]
    for j, packed in enumerate((p0_ref, p2_ref, p1_ref)):
        acc[...] = mm_lt(xa_ref[...], packed[:half, :]) + mm_lt(xb_ref[...], packed[half:, :])
        for k, away in enumerate(away_of(j == 2)):
            ours = acc[pl.ds(pl.multiple_of((chip ^ away) * rows, rows), rows), :]
            if k < 2:
                keep_ref[j, k] = ours
            else:
                send_ref[j, k - 2] = ours.astype(BF16)


def qkv_grads(place, x_parts, packed, rows):
    half, width = x_parts[0].shape
    cols = packed[0].shape[1]
    whole = lambda a, b: pl.BlockSpec((a, b), lambda i, p: (0, 0))
    part = pl.BlockSpec((3, 2, rows, cols), lambda i, p: (0, 0, 0, 0))
    return pl.pallas_call(
        qkv_grad_kernel,
        grid_spec=pltpu.PrefetchScalarGridSpec(
            num_scalar_prefetch=1,
            grid=(1,),
            in_specs=[whole(half, width)] * 2 + [whole(2 * half, cols)] * 3,
            out_specs=[part, part],
            scratch_shapes=[pltpu.VMEM((width, cols), F32)],
        ),
        out_shape=[
            jax.ShapeDtypeStruct((3, 2, rows, cols), F32),
            jax.ShapeDtypeStruct((3, 2, rows, cols), BF16),
        ],
        compiler_params=pltpu.CompilerParams(vmem_limit_bytes=LIMIT),
        cost_estimate=pl.CostEstimate(
            flops=12 * half * width * cols, bytes_accessed=12 << 20, transcendentals=0
        ),
        name="qkv_grads",
    )(place, *x_parts, *packed)


def in_grad_kernel(*refs, n, adds):
    packed, w_ref = refs[:n], refs[n]
    total = mm_rt(packed[0][...], w_ref[0])
    for g in range(1, n):
        total = total + mm_rt(packed[g][...], w_ref[g])
    for extra in refs[n + 1 : n + 1 + adds]:
        total = total + extra[...].astype(F32)
    outs = refs[n + 1 + adds :]
    if len(outs) == 1:
        outs[0][...] = total.astype(BF16)
        return
    for k, out in enumerate(outs):

        @pl.when(pl.program_id(0) == k)
        def _(out=out):
            out[...] = total.astype(BF16)


def in_grad(packed, weight, second, extras):
    seq, cols = packed[0].shape
    n, width = weight.shape[:2]
    tile = seq // 4
    first = 2 if second else 0
    return pl.pallas_call(
        functools.partial(in_grad_kernel, n=n, adds=len(extras)),
        grid=(2,),
        in_specs=[pl.BlockSpec((tile, cols), lambda i: (first + i, 0))] * n
        + [pl.BlockSpec((n, width, cols), lambda i: (0, 0, 0))]
        + [pl.BlockSpec((tile, width), lambda i: (i, 0))] * len(extras),
        out_specs=[pl.BlockSpec((tile, width), lambda i: (i, 0))]
        if second
        else [pl.BlockSpec((tile, width), lambda i: (0, 0))] * 2,
        out_shape=[jax.ShapeDtypeStruct((seq // 2, width), BF16)]
        if second
        else [jax.ShapeDtypeStruct((tile, width), BF16)] * 2,
        compiler_params=pltpu.CompilerParams(vmem_limit_bytes=LIMIT),
        cost_estimate=pl.CostEstimate(
            flops=seq * width * cols * n, bytes_accessed=8 << 20, transcendentals=0
        ),
        name="in_grad",
    )(*packed, weight, *extras)


def norm(values):
    centred = values - jnp.mean(values, axis=-1, keepdims=True)
    scale = lax.rsqrt(jnp.mean(centred * centred, axis=-1, keepdims=True) + EPS)
    return centred * scale, scale


def norm_back(grad, unit, scale, gain):
    q = grad * gain
    mean_q = jnp.mean(q, axis=-1, keepdims=True)
    mean_qn = jnp.mean(q * unit, axis=-1, keepdims=True)
    return scale * (q - mean_q - unit * mean_qn)


def gelu_parts(u):
    dense = jnp.exp(-0.5 * u * u) * 0.3989422804014327
    t = 1.0 / (1.0 + 0.2316419 * jnp.abs(u))
    poly = t * (
        0.319381530
        + t * (-0.356563782 + t * (1.781477937 + t * (-1.821255978 + t * 1.330274429)))
    )
    tail = dense * poly
    phi = jnp.where(u >= 0, 1.0 - tail, tail)
    return u * phi, phi + u * dense


def dense_copies(place, pieces, wo, ww, sems):
    copies = []

    def add(source, target):
        copies.append(pltpu.make_async_copy(source, target, sems.at[len(copies)]))

    if len(pieces) == 2:
        add(pieces[0], wo)
        add(pieces[1], ww)
        return copies
    core, chip = place % 2, place // 2
    chips, rows, cols = pieces[0].shape
    for side in range(2):
        lanes = pl.ds(pl.multiple_of((core ^ side) * cols, cols), cols)
        for k in range(chips):
            add(pieces[side].at[k], wo.at[pl.ds(pl.multiple_of((chip ^ k) * rows, rows), rows), lanes])
    half, rows = pieces[2].shape[1:3]
    for k, piece in enumerate(pieces[2:]):
        away = ((0, 1), (0, 2), (2, 3), (1, 3))[k % 4]
        for j in range(2):
            base = (place ^ (2 * away[j] + k // 4)) * rows
            add(piece.at[j], ww.at[pl.ds((k % 2) * half, half), pl.ds(pl.multiple_of(base, rows), rows), :])
    return copies


def dense_kernel(place_ref, *refs, n_w, chunks):
    w_refs, refs = refs[:n_w], refs[n_w:]
    (
        x_ref, mine_ref, other_ref, cot_a, cot_b, vec_ref, upb_ref,
        layer_a, layer_b, gm_mine, gm_other, act_ref, mlow_ref, gb_ref, gul_ref, ga_ref, gone_ref, sums_ref,
        wo, ww, slope, acc, sems,
    ) = refs
    step = pl.program_id(0)
    core = place_ref[0] % 2
    cols = mine_ref.shape[1]
    width = x_ref.shape[1]
    units = ww.shape[2] // 2

    @pl.when(step == 0)
    def _():
        copies = dense_copies(place_ref[0], w_refs, wo, ww, sems)
        for copy in copies:
            copy.start()
        for copy in copies:
            copy.wait()
        sums_ref[...] = jnp.zeros_like(sums_ref)

    mine_cols = pl.ds(pl.multiple_of(core * cols, cols), cols)
    other_cols = pl.ds(pl.multiple_of((1 - core) * cols, cols), cols)
    attn = mm_rt(mine_ref[...], wo[:, mine_cols]) + mm_rt(other_ref[...], wo[:, other_cols])
    unit_one, scale_one = norm(x_ref[...].astype(F32) + attn + vec_ref[0:1, :])
    middle = unit_one * vec_ref[1:2, :] + vec_ref[2:3, :]
    mlow_ref[...] = middle.astype(BF16)
    acc[...] = middle + vec_ref[3:4, :]

    @pl.loop(0, chunks)
    def _(k):
        place = pl.ds(pl.multiple_of(k * units, units), units)
        upper = mm(mlow_ref[...], ww[k, :, :units]) + upb_ref[:, place]
        active, rise = gelu_parts(upper)
        active = active.astype(BF16)
        act_ref[:, place] = active
        slope[:, place] = rise.astype(BF16)
        acc[...] += mm_rt(active, ww[k, :, units:])

    unit_two, scale_two = norm(acc[...])
    gain_two = vec_ref[4:5, :]
    layer = (unit_two * gain_two + vec_ref[5:6, :]).astype(BF16)

    @pl.when(step < pl.num_programs(0) // 2)
    def _():
        layer_a[...] = layer

    @pl.when(step >= pl.num_programs(0) // 2)
    def _():
        layer_b[...] = layer

    cot = jnp.where(step < pl.num_programs(0) // 2, cot_a[...], cot_b[...]).astype(F32)
    grad_two = norm_back(cot, unit_two, scale_two, gain_two)
    sums_ref[4:5, :] += jnp.sum(cot * unit_two, axis=0, keepdims=True)
    sums_ref[5:6, :] += jnp.sum(cot, axis=0, keepdims=True)
    sums_ref[3:4, :] += jnp.sum(grad_two, axis=0, keepdims=True)
    gb_ref[...] = grad_two.astype(BF16)
    acc[...] = grad_two

    @pl.loop(0, chunks)
    def _(k):
        place = pl.ds(pl.multiple_of(k * units, units), units)
        grad_upper = mm(gb_ref[...], ww[k, :, units:]) * slope[:, place].astype(F32)
        sums_ref[pl.ds(8 + (k ^ place_ref[1]), 1), :] += jnp.sum(grad_upper, axis=0, keepdims=True)
        grad_low = grad_upper.astype(BF16)
        gul_ref[:, place] = grad_low
        acc[...] += mm_rt(grad_low, ww[k, :, :units])

    grad_mid = acc[...]
    sums_ref[1:2, :] += jnp.sum(grad_mid * unit_one, axis=0, keepdims=True)
    sums_ref[2:3, :] += jnp.sum(grad_mid, axis=0, keepdims=True)
    grad_one = norm_back(grad_mid, unit_one, scale_one, vec_ref[1:2, :])
    sums_ref[0:1, :] += jnp.sum(grad_one, axis=0, keepdims=True)
    gone_ref[...] = grad_one
    grad_attn = grad_one.astype(BF16)
    ga_ref[...] = grad_attn
    gm_mine[...] = mm(grad_attn, wo[:, mine_cols]).astype(BF16)
    gm_other[...] = mm(grad_attn, wo[:, other_cols]).astype(BF16)


def dense(place, w_pieces, x, mine, other, cot_a, cot_b, vec, upb, tile):
    count, width = x.shape
    cols = other.shape[1]
    units = w_pieces[-1].shape[-1] // 2
    chunks = upb.shape[1] // units
    steps = count // tile
    half = steps // 2
    n_copies = 2 if len(w_pieces) == 2 else 2 * w_pieces[0].shape[0] + 2 * (len(w_pieces) - 2)
    rows = lambda n: pl.BlockSpec((tile, n), lambda i, p: (i, 0))
    fixed = lambda a, b: pl.BlockSpec((a, b), lambda i, p: (0, 0))
    full = chunks * units
    shapes = [
        ((count // 2, width), BF16), ((count // 2, width), BF16),
        ((count, cols), BF16), ((count, cols), BF16), ((count, full), BF16),
        ((count, width), BF16), ((count, width), BF16), ((count, full), BF16), ((count, width), BF16),
        ((count, width), F32), ((16, width), F32),
    ]
    flops = 8 * count * width * full + 4 * count * width * 2 * cols
    return pl.pallas_call(
        functools.partial(dense_kernel, n_w=len(w_pieces), chunks=chunks),
        grid_spec=pltpu.PrefetchScalarGridSpec(
            num_scalar_prefetch=1,
            grid=(count // tile,),
            in_specs=[ANY] * len(w_pieces)
            + [rows(width), rows(cols), rows(cols)]
            + [
                pl.BlockSpec((tile, width), lambda i, p: (jnp.minimum(i, half - 1), 0)),
                pl.BlockSpec((tile, width), lambda i, p: (jnp.maximum(i - half, 0), 0)),
                fixed(8, width),
                fixed(1, full),
            ],
            out_specs=[
                pl.BlockSpec((tile, width), lambda i, p: (jnp.minimum(i, half - 1), 0)),
                pl.BlockSpec((tile, width), lambda i, p: (jnp.maximum(i - half, 0), 0)),
                rows(cols), rows(cols), rows(full), rows(width), rows(width), rows(full),
                rows(width), rows(width), fixed(16, width),
            ],
            scratch_shapes=[
                pltpu.VMEM((width, 2 * cols), BF16),
                pltpu.VMEM((chunks, width, 2 * units), BF16),
                pltpu.VMEM((tile, full), BF16),
                pltpu.VMEM((tile, width), F32),
                pltpu.SemaphoreType.DMA((n_copies,)),
            ],
        ),
        out_shape=[jax.ShapeDtypeStruct(*s) for s in shapes],
        compiler_params=pltpu.CompilerParams(vmem_limit_bytes=LIMIT),
        cost_estimate=pl.CostEstimate(flops=flops, bytes_accessed=40 << 20, transcendentals=0),
        name="dense",
    )(place, *w_pieces, x, mine, other, cot_a, cot_b, vec, upb)


def away_of(second):
    return [0, jnp.where(second, 1, 2), jnp.where(second, 2, 1), 3]


def grad_kernel(place_ref, *refs, n, steps, drows, first):
    left_ref, right_ref, refs = refs[0], refs[1], refs[2:]
    extra, (keep_ref, send_ref, theirs_ref, left_t, acc) = refs[: n - 2], refs[n - 2 :]
    core, chip = place_ref[0] % 2, place_ref[0] // 2
    step = pl.program_id(0)

    @pl.when(step == 0)
    def _():
        left_t[...] = left_ref[...].T

    @pl.when(step >= steps)
    def _():
        acc[...] = mm(left_t[...], right_ref[...])

    if extra:

        @pl.when(step < steps)
        def _():
            cols = extra[1].shape[1]
            mine_cols = pl.ds(pl.multiple_of(core * cols, cols), cols)
            other_cols = pl.ds(pl.multiple_of((1 - core) * cols, cols), cols)
            acc[:, mine_cols] = mm_lt(extra[0][...], extra[1][...])
            acc[:, other_cols] = mm_lt(extra[0][...], extra[2][...])

    for k, away in enumerate(away_of(step >= first)):
        base = 2 * (chip ^ away)
        ours = acc[pl.ds(pl.multiple_of((base + core) * drows, drows), drows), :]
        if k < 2:
            keep_ref[0, k] = ours
        else:
            send_ref[0, k - 2] = ours.astype(BF16)
        theirs_ref[0, k] = acc[pl.ds(pl.multiple_of((base + 1 - core) * drows, drows), drows), :].astype(BF16)


def weight_grad(place, left, right, extra, drows, first):
    count, width = left.shape
    tile = width
    steps = 1 if extra else 0
    chunks = right.shape[1] // tile + steps
    whole = lambda a, b: pl.BlockSpec((a, b), lambda i, p: (0, 0))
    shapes = [((chunks, 2, drows, tile), F32), ((chunks, 2, drows, tile), BF16), ((chunks, 4, drows, tile), BF16)]
    return pl.pallas_call(
        functools.partial(grad_kernel, n=2 + len(extra), steps=steps, drows=drows, first=first),
        grid_spec=pltpu.PrefetchScalarGridSpec(
            num_scalar_prefetch=1,
            grid=(chunks,),
            in_specs=[
                whole(count, width),
                pl.BlockSpec((count, tile), lambda i, p: (0, jnp.maximum(i - steps, 0))),
            ]
            + [whole(count, e.shape[1]) for e in extra],
            out_specs=[pl.BlockSpec((1,) + shape[1:], lambda i, p: (i, 0, 0, 0)) for shape, _ in shapes],
            scratch_shapes=[pltpu.VMEM((width, count), BF16), pltpu.VMEM((width, tile), F32)],
        ),
        out_shape=[jax.ShapeDtypeStruct(*shape) for shape in shapes],
        compiler_params=pltpu.CompilerParams(vmem_limit_bytes=LIMIT),
        cost_estimate=pl.CostEstimate(
            flops=2 * count * width * chunks * tile, bytes_accessed=6 * chunks * width * tile, transcendentals=0
        ),
        name="weight_grad",
    )(place, left, right, *extra)


def xor_order(parts, index):
    parts = list(parts)
    bit = 1
    while bit < len(parts):
        odd = (index // bit) % 2 == 1
        parts = [jnp.where(odd, parts[k ^ bit], parts[k]) for k in range(len(parts))]
        bit *= 2
    return parts


def per_device(
    tokens,
    segments,
    pairing,
    qkv_weight,
    qv_bias,
    out_weight,
    out_bias,
    first_gain,
    first_shift,
    up_weight,
    up_bias,
    down_weight,
    down_bias,
    second_gain,
    second_shift,
    cotangent,
):
    width = tokens.shape[2]
    rows = tokens.shape[1]
    lheads, blocks = pairing.shape
    hs = qv_bias.shape[1] // 2
    lanes = 2 * hs
    units = up_weight.shape[1]
    ndp, nt = lax.axis_size("dp"), lax.axis_size("tensor")
    drows = width // ndp
    chips = ndp // 2
    dp, tensor = lax.axis_index("dp"), lax.axis_index("tensor")
    core, chip, half, low = dp % 2, dp // 2, tensor // 2, tensor % 2
    slot_mask = 2 * core + low
    heads = 2 * lheads
    cols = heads * hs
    aligned = drows % 8 == 0
    place = jnp.stack([dp, tensor]).astype(jnp.int32)
    order = [0, 1, 3, 4, 2, 5]

    core_pairs = [(i, i ^ 1) for i in range(ndp)]

    def core_swap(x):
        return lax.ppermute(x, "dp", core_pairs)

    def z_step(x, k):
        return lax.ppermute(x, "tensor", [(i, i ^ k) for i in range(nt)])

    def chip_step(x, k):
        return lax.ppermute(x, "dp", [(i, i ^ (2 * k)) for i in range(ndp)])

    def column(k, flip, back):
        steps = []
        for p in range(chips):
            for c in range(2):
                for a in range(2):
                    for b in range(2):
                        home = (2 * p + c) * nt + 2 * a + b
                        away = (2 * p + (a ^ flip)) * nt + 2 * c + (b ^ k)
                        steps.append((away, home) if back else (home, away))
        return steps

    def to_sequence(x):
        return [
            lax.ppermute(
                lax.dynamic_index_in_dim(x, low ^ k, 0, keepdims=False), BOTH, column(k, 0, False)
            )
            for k in range(2)
        ]

    def at_home(first, second):
        return jnp.stack([jnp.where(low == 0, first, second), jnp.where(low == 0, second, first)])

    def z_all(x):
        return [x] + [z_step(x, k) for k in range(1, nt)]

    def chip_all(x):
        return [x] + [chip_step(x, k) for k in range(1, chips)]

    gate = lambda *trees: lax.optimization_barrier(trees)

    qkv_local = qkv_weight.reshape(drows, lheads, 3, hs).transpose(0, 2, 1, 3)
    qkv_local = jnp.concatenate(
        [
            qkv_local[:, :, :2].reshape(drows, 3 * lanes),
            qkv_local[:, :, 2].reshape(drows, 3 * hs),
            out_weight.reshape(lheads * hs, drows).T,
        ],
        axis=1,
    )
    small = jnp.concatenate([pairing.astype(BF16).reshape(-1), qv_bias.reshape(-1), up_bias])
    n_pair, n_qv = lheads * blocks, lheads * lanes
    extra_rows = 8
    small = jnp.pad(small, (0, extra_rows * qkv_local.shape[1] - small.shape[0]))
    first_z = z_all(jnp.concatenate([qkv_local, small.reshape(extra_rows, -1)]))
    segs = jnp.where(half == core, segments, core_swap(segments))
    ff_local = jnp.concatenate([up_weight, down_weight.T], axis=1)
    ff_local, first_z = gate(ff_local, first_z)
    ff_one = z_step(ff_local, 1)

    abs_z = xor_order([part[:drows] for part in first_z], tensor)
    qkv_cols = 3 * lheads * hs

    def regroup(first, second):
        left, right = first[:, 3 * lanes : qkv_cols], second[:, 3 * lanes : qkv_cols]
        both = [part[:, hs * k : hs * (k + 1)] for k in range(3) for part in (left, right)]
        return jnp.stack([first[:, : 3 * lanes], second[:, : 3 * lanes], jnp.concatenate(both, axis=1)])

    def with_out(first, second):
        left, right = first[:, qkv_cols:], second[:, qkv_cols:]
        out = jnp.concatenate([left[:, :lanes], right[:, :lanes], left[:, lanes:], right[:, lanes:]], axis=1)
        return jnp.concatenate([regroup(first, second), out[None]])

    zero_heads, one_heads = with_out(abs_z[0], abs_z[1]), with_out(abs_z[2], abs_z[3])
    keep = jnp.where(core == 0, zero_heads, one_heads)
    got = core_swap(jnp.where(core == 0, one_heads, zero_heads))
    chip_rows = jnp.where(
        core == 0, jnp.concatenate([keep, got], axis=1), jnp.concatenate([got, keep], axis=1)
    )
    ff_pair = jnp.stack([ff_local, ff_one])
    chip_rows, ff_pair = gate(chip_rows, ff_pair)
    qkv_pieces = chip_all(chip_rows)
    ff_other = z_step(ff_pair, 2)

    tokens, ff_other = gate(tokens, ff_other)
    moved = to_sequence(tokens)
    qkv_pieces, ff_pair, ff_other = gate(qkv_pieces, ff_pair, ff_other)
    out_mine = jnp.stack([piece[3] for piece in qkv_pieces])
    if aligned:
        firsts = [chip_step(ff_pair, 1), chip_step(ff_other, 2)]
        out_other = core_swap(out_mine)
        x_mine = jnp.concatenate(moved)
        x_mine, firsts, out_other = gate(x_mine, firsts, out_other)
        twos = [jnp.stack([ff_pair, firsts[0]]), jnp.stack([ff_other, firsts[1]])]
        x_other = core_swap(x_mine)
        twos_swapped = [core_swap(two) for two in twos]
        fours = [chip_step(twos[0], 2), chip_step(twos[1], 1)]
        cotangent, x_mine, x_other, twos_swapped = gate(cotangent, x_mine, x_other, twos_swapped)
        cot_a, cot_b = to_sequence(cotangent)
    else:
        x_mine = jnp.concatenate(moved)
        x_other = core_swap(x_mine)
        cot_a, cot_b = to_sequence(cotangent)
        out_other = core_swap(out_mine)
        ff_own = chip_all(jnp.concatenate([ff_pair, ff_other]))
        ff_all = [part for piece in ff_own for part in (piece, core_swap(piece))]
        qkv_pieces = [jnp.concatenate(xor_order(qkv_pieces, chip), axis=1)]
        out_both = [jnp.concatenate(xor_order(list(o), chip)) for o in (out_mine, out_other)]
        dense_pieces = [
            jnp.concatenate(
                [jnp.where(core == 0, out_both[0], out_both[1]), jnp.where(core == 0, out_both[1], out_both[0])],
                axis=1,
            ),
            jnp.concatenate(xor_order(ff_all, dp), axis=1),
        ]

    small_rel = [part[drows:].reshape(-1) for part in first_z]
    small = jnp.stack(xor_order(small_rel, tensor))
    all_pairs = small[:, :n_pair].astype(jnp.int32).reshape(2, heads, blocks)
    my_pairs = jnp.where(core == 0, all_pairs[0], all_pairs[1])
    pair_slots = jnp.stack(xor_order([my_pairs[:, k] for k in range(blocks)], slot_mask), axis=1) ^ slot_mask
    pair_slots = jnp.stack([pair_slots[h] for h in order])
    all_qvb = small[:, n_pair : n_pair + n_qv].astype(F32).reshape(2, heads, lanes)
    my_qvb = jnp.where(core == 0, all_qvb[0], all_qvb[1])
    my_qvb = jnp.stack([my_qvb[h] for h in order])
    up_bias_rel = jnp.concatenate([s[n_pair + n_qv :][:units] for s in small_rel]).astype(F32)
    groups = heads // 2
    bias = jnp.concatenate(
        [
            my_qvb[:, :hs].reshape(groups, lanes),
            jnp.zeros((groups, lanes), F32),
            my_qvb[:, hs:].reshape(groups, lanes),
        ],
        axis=1,
    ).reshape(groups, 1, 3 * lanes)

    seg_rows = jnp.where(low == 0, segs[0], segs[1]).reshape(blocks, rows)
    seg_row = jnp.concatenate(xor_order([seg_rows[k] for k in range(blocks)], slot_mask))
    seg_col = seg_row.reshape(blocks * rows, 1)
    seg_row = seg_row.reshape(1, blocks * rows)

    x_parts = [x_mine, x_other]
    q, k, v, mixed, mixed_other, lse, w_all = attend(pair_slots, place, x_parts, qkv_pieces, bias, seg_row, seg_col, hs)
    if aligned:
        q, k, v, mixed, mixed_other, lse, w_all, fours, cot_a, cot_b = gate(
            q, k, v, mixed, mixed_other, lse, w_all, fours, cot_a, cot_b
        )
        dense_pieces = [out_mine, out_other] + twos + fours + twos_swapped + [core_swap(four) for four in fours]
    other = core_swap(mixed_other)

    blank = jnp.zeros((width,), BF16)
    vec = jnp.stack(
        [out_bias, first_gain, first_shift, down_bias, second_gain, second_shift, blank, blank]
    ).astype(F32)
    (
        layer_a, layer_b, gm_mine, gm_other, active, middle_low, grad_branch, grad_upper, grad_attn, grad_one, sums,
    ) = dense(
        place, dense_pieces, x_mine, mixed, other, cot_a, cot_b, vec, up_bias_rel.reshape(1, nt * units), 256
    )
    gm_got = core_swap(gm_other)
    home_0 = lax.ppermute(layer_a, BOTH, column(0, 0, True))

    def total_of(parts):
        total = parts[0].astype(F32)
        for part in parts[1:]:
            total = total + part.astype(F32)
        return total

    class Plane:
        def __init__(self, first, keep, send, got=None):
            self.first, self.got = first, got
            self.keep, self.send = self.split(keep), self.split(send)

        def split(self, x):
            return [x[: self.first], x[self.first :]]

        def first_sends(self):
            if self.got is None:
                return self.send
            got = self.split(self.got)
            self.keep = [[keep, g[:, :2]] for keep, g in zip(self.keep, got)]
            return [total_of([send, g[:, 2:]]).astype(BF16) for send, g in zip(self.send, got)]

        def first_moves(self, sends):
            return [chip_step(sends[0], 1), chip_step(sends[1], 2)]

        def second_sends(self, moves):
            keep = [k if isinstance(k, list) else [k] for k in self.keep]
            own = [total_of([part[:, 0] for part in k] + [m[:, 0]]) for k, m in zip(keep, moves)]
            sends = [total_of([part[:, 1] for part in k] + [m[:, 1]]).astype(BF16) for k, m in zip(keep, moves)]
            return own, sends

        def second_moves(self, sends):
            return [chip_step(sends[0], 2), chip_step(sends[1], 1)]

        def sums(self, own, moves):
            return [total_of([o, m]) for o, m in zip(own, moves)]

    class SlowPlane(Plane):
        def __init__(self, first, keep, send, got=None):
            self.first, self.view = first, keep if got is None else keep + got.astype(F32)

        def first_sends(self):
            return []

        def first_moves(self, sends):
            return []

        def second_sends(self, moves):
            return [], []

        def second_moves(self, sends):
            return []

        def sums(self, own, moves):
            pick = lambda step: lax.dynamic_index_in_dim(self.view, chip ^ step, 0, keepdims=False)
            total = total_of([pick(0)] + [chip_step(pick(step).astype(BF16), step) for step in range(1, chips)])
            return self.split(total.transpose(1, 0, 2))

    fast = chips == 4 and aligned

    def grads_of(left, right, extra, first):
        if fast:
            return weight_grad(place, left, right, extra, drows, first)
        grads = mm_lt(left, right)
        if extra:
            near, far = mm_lt(extra[0], extra[1]), mm_lt(extra[0], extra[2])
            head = [jnp.where(core == 0, near, far), jnp.where(core == 0, far, near)]
            grads = jnp.concatenate(head + [grads], axis=1)
        view = grads.reshape(chips, 2, drows, grads.shape[1] // width, width)
        ours = lax.dynamic_index_in_dim(view, core, 1, keepdims=False)
        theirs = lax.dynamic_index_in_dim(view, 1 - core, 1, keepdims=False).astype(BF16)
        return ours, theirs, theirs

    plane_of = Plane if fast else SlowPlane
    down_keep, down_send, down_theirs = grads_of(grad_branch, active, [], 2)
    down_got = core_swap(down_theirs)
    middle_low, down_keep, down_send, down_theirs, gm_got = gate(
        middle_low, down_keep, down_send, down_theirs, gm_got
    )
    up_keep, up_send, up_theirs = grads_of(middle_low, grad_upper, [grad_attn, mixed, other], 3)
    up_got = core_swap(up_theirs)

    down = plane_of(2, down_keep, down_send, down_got)
    d_sends = down.first_sends()
    pairs_0, gm_got, d_sends = gate(pair_slots, gm_got, d_sends)
    d_moves = down.first_moves(d_sends)
    packed_0, sums_0 = attend_back(pairs_0, 0, q, k, v, gm_mine, gm_got, seg_row, seg_col, lse, hs)
    packed_0, sums_0, d_moves, up_got, home_0 = gate(packed_0, sums_0, d_moves, up_got, home_0)
    d_own, d_sends = down.second_sends(d_moves)
    up = plane_of(3, up_keep, up_send, up_got)
    u_sends = up.first_sends()
    pairs_1, d_own, d_sends, u_sends = gate(pair_slots, d_own, d_sends, u_sends)
    d_moves = down.second_moves(d_sends)
    u_moves = up.first_moves(u_sends)
    packed_1, sums_1 = attend_back(pairs_1, 1, q, k, v, gm_mine, gm_got, seg_row, seg_col, lse, hs)
    packed_1, sums_1, d_moves, u_moves, layer_b = gate(packed_1, sums_1, d_moves, u_moves, layer_b)
    home_1 = lax.ppermute(layer_b, BOTH, column(1, 0, True))
    d_first, d_second = down.sums(d_own, d_moves)
    u_own, u_sends = up.second_sends(u_moves)
    d_second = d_second.astype(BF16)
    pair_slots, packed_1, d_first, d_second, u_own, u_sends = gate(
        pair_slots, packed_1, d_first, d_second, u_own, u_sends
    )
    d_second = z_step(d_second, 2)
    u_moves = up.second_moves(u_sends)
    packed_2, sums_2 = attend_back(pair_slots, 2, q, k, v, gm_mine, gm_got, seg_row, seg_col, lse, hs)
    packed_2, sums_2, u_moves, d_second = gate(packed_2, sums_2, u_moves, d_second)
    d_keep = total_of([d_first[0], d_second[0]])
    d_give = total_of([d_first[1], d_second[1]]).astype(BF16)
    u_first, u_second = up.sums(u_own, u_moves)
    out_near = jnp.where(half == 0, u_first[0, :, :cols], u_first[0, :, cols:])
    out_far = jnp.where(half == 0, u_first[0, :, cols:], u_first[0, :, :cols])
    u_first = u_first[1:]
    u_second, out_far = u_second.astype(BF16), out_far.astype(BF16)
    out_far = jnp.pad(out_far, ((0, 0), (0, width - cols)))
    u_second = jnp.concatenate([u_second, out_far[None]])

    head_sums = jnp.concatenate([part[row] for row in range(2) for part in (sums_0, sums_1, sums_2)])[None]
    blank = jnp.zeros_like(head_sums)
    sums = jnp.concatenate(
        [
            sums[:12],
            jnp.where(core == 0, head_sums, blank),
            jnp.where(core == 0, blank, head_sums),
            jnp.zeros((2, width), F32),
        ]
    )
    packed_2, d_keep, d_give, u_first, u_second, sums, out_near = gate(
        packed_2, d_keep, d_give, u_first, u_second, sums, out_near
    )
    packed = [packed_0, packed_1, packed_2]
    d_give = z_step(d_give, 1)
    u_second = z_step(u_second, 2)
    sums_got = z_step(sums, 1)
    (in_other,) = in_grad(packed, w_all, True, [])
    in_other, d_give, u_second, sums_got, packed_0, home_1 = gate(
        in_other, d_give, u_second, sums_got, packed_0, home_1
    )
    layer_out = at_home(home_0, home_1)
    down_grad = (d_keep + d_give.astype(F32)).T
    sums = sums + sums_got
    u_keep, u_give = [total_of([u_first[j], u_second[j]]) for j in range(2)]
    out_near = total_of([out_near, u_second[2, :, :cols]])

    def out_unit(wanted_low):
        parts = [
            jnp.concatenate(
                [out_near[:, lanes * w : lanes * (w + 1)], out_near[:, 2 * lanes + hs * w : 2 * lanes + hs * (w + 1)]],
                axis=1,
            )
            for w in range(2)
        ]
        return jnp.where(wanted_low == 0, parts[0], parts[1])

    u_give = jnp.concatenate([u_give, out_unit(1 - low)], axis=1).astype(BF16)
    out_near = out_unit(low)
    in_other, u_keep, u_give, sums, packed_0 = gate(in_other, u_keep, u_give, sums, packed_0)
    in_got = core_swap(in_other)
    u_give = z_step(u_give, 1)
    sums_got = z_step(sums, 2)
    if fast:
        qkv_keep, qkv_send = qkv_grads(place, x_parts, packed, 2 * drows)
    else:
        parts = [mm_lt(jnp.concatenate(x_parts), packed[g]).reshape(chips, 2 * drows, 3 * lanes) for g in (0, 2, 1)]
        qkv_keep = qkv_send = jnp.stack(parts, axis=2)
    qkv_keep, qkv_send, in_got, u_give, sums_got = gate(qkv_keep, qkv_send, in_got, u_give, sums_got)
    sums = sums + sums_got
    qkv = plane_of(2, qkv_keep, qkv_send)
    a_sends = qkv.first_sends()
    in_got, a_sends, sums = gate(in_got, a_sends, sums)
    a_moves = qkv.first_moves(a_sends)
    sums_got = core_swap(sums)
    in_low = in_grad(packed, w_all, False, [in_got, grad_one])
    in_low, a_moves, sums_got = gate(in_low, a_moves, sums_got)
    homes = [lax.ppermute(in_low[k], BOTH, column(k, 0, True)) for k in range(2)]
    a_own, a_sends = qkv.second_sends(a_moves)
    a_moves = qkv.second_moves(a_sends)
    sums = sums + sums_got
    up_grad = total_of([u_keep, u_give[:, :units]])
    out_grad = total_of([out_near, u_give[:, units:]]).T.reshape(lheads, hs, drows)
    for bit in range(chips.bit_length() - 1):
        sums = sums + chip_step(sums, 1 << bit)
    outb_grad, gain_one_grad, shift_one_grad, downb_grad, gain_two_grad, shift_two_grad = [
        sums[row] for row in range(6)
    ]
    upb_grad = lax.dynamic_index_in_dim(sums, 8 + tensor, 0, keepdims=False)
    head_row = jnp.where(half == 0, sums[12], sums[13]).reshape(2, 6, hs)
    qvb_grad = jnp.where(low == 0, head_row[:, [0, 1, 4]], head_row[:, [2, 3, 5]])
    qvb_grad = jnp.concatenate([qvb_grad[0], qvb_grad[1]], axis=1)

    homes, a_moves = gate(homes, a_moves)
    input_grad = at_home(*homes)
    sum_a, sum_b = qkv.sums(a_own, a_moves)
    sum_0, sum_2, sum_1 = [part.reshape(2, drows, 3 * lanes) for part in (sum_a[0], sum_a[1], sum_b[0])]
    sum_01 = [sum_0, sum_1]

    def share(c, u):
        third = [sum_2[c][:, lanes * k + hs * u : lanes * k + hs * (u + 1)] for k in range(3)]
        return jnp.concatenate([sum_01[u][c]] + third, axis=1)

    shares = [[share(c, u).astype(BF16) for u in range(2)] for c in range(2)]
    qkv_grad = jnp.zeros((drows, 3 * lheads * hs), F32)
    for flip in range(2):
        for step in range(2):
            by_core = [jnp.where((low ^ step) == 0, shares[c][0], shares[c][1]) for c in range(2)]
            sent = jnp.where((half ^ flip) == 0, by_core[0], by_core[1])
            qkv_grad = qkv_grad + lax.ppermute(sent, BOTH, column(step, flip, False)).astype(F32)
    pairs_part = qkv_grad[:, : 3 * lanes].reshape(drows, 3, 2, hs)
    third_part = qkv_grad[:, 3 * lanes :].reshape(drows, 3, 1, hs)
    qkv_grad = jnp.concatenate([pairs_part, third_part], axis=2).transpose(0, 2, 1, 3)
    qkv_grad = qkv_grad.reshape(drows, lheads, 3 * hs)
    return (
        layer_out,
        input_grad,
        qkv_grad,
        qvb_grad,
        out_grad,
        outb_grad,
        gain_one_grad,
        shift_one_grad,
        up_grad,
        upb_grad,
        down_grad,
        downb_grad,
        gain_two_grad,
        shift_two_grad,
    )


def solution(mesh):
    return jax.shard_map(
        per_device,
        mesh=mesh,
        in_specs=(
            P("dp", "tensor", None),
            P("dp", None),
            P("tensor", None),
            P("dp", "tensor", None),
            P("tensor", None),
            P("tensor", None, "dp"),
            P(),
            P(),
            P(),
            P("dp", "tensor"),
            P("tensor"),
            P("tensor", "dp"),
            P(),
            P(),
            P(),
            P("dp", "tensor", None),
        ),
        out_specs=(
            P("dp", "tensor", None),
            P("dp", "tensor", None),
            P("dp", "tensor", None),
            P("tensor", None),
            P("tensor", None, "dp"),
            P(),
            P(),
            P(),
            P("dp", "tensor"),
            P("tensor"),
            P("tensor", "dp"),
            P(),
            P(),
            P(),
        ),
        check_vma=False,
    )
```

```python
import functools

import jax
import jax.numpy as jnp
from jax import lax
from jax.experimental import pallas as pl
from jax.experimental.pallas import tpu as pltpu
from jax.sharding import PartitionSpec as P

EPS = 1e-06
NEG = -1e30
BOTH = ("dp", "tensor")
F32 = jnp.float32
BF16 = jnp.bfloat16
ANY = pl.BlockSpec(memory_space=pl.ANY)
LIMIT = 58 << 20
COST = pl.CostEstimate(flops=10**9, bytes_accessed=1 << 16, transcendentals=0)


def mm(left, right):
    return lax.dot_general(left, right, (((1,), (0,)), ((), ())), preferred_element_type=F32)


def mm_rt(left, right):
    return lax.dot_general(left, right, (((1,), (1,)), ((), ())), preferred_element_type=F32)


def mm_lt(left, right):
    return lax.dot_general(left, right, (((0,), (0,)), ((), ())), preferred_element_type=F32)


def head_lanes(shape, head, dim, head_size):
    place = lax.broadcasted_iota(jnp.int32, shape, dim)
    return (place < head_size) if head == 0 else (place >= head_size)


def fetches(pieces, offsets, target, dim, sems, first):
    copies = []
    for k, (piece, offset) in enumerate(zip(pieces, offsets)):
        count = piece.shape[dim]
        where = pl.ds(offset if isinstance(offset, int) else pl.multiple_of(offset, count), count)
        index = (slice(None),) * dim + (where,)
        copies.append(pltpu.make_async_copy(piece, target.at[index], sems.at[first + k]))
    return copies


def piece_rows(place, step, rows, count):
    if count == 1:
        return [0]
    return [(place ^ (k * step)) * rows for k in range(count)]


def attend_kernel(pair_ref, place_ref, *refs, rows, hs, blocks, n_w):
    x_refs, refs = refs[:2], refs[2:]
    w_refs, refs = refs[:n_w], refs[n_w:]
    bias_ref, segq_ref, segk_ref, q_out, k_out, v_out, o_mine, o_other, lse_ref, w_all, x_all, sems = refs
    group, block = pl.program_id(0), pl.program_id(1)
    lanes2 = 2 * hs

    @pl.when((group == 0) & (block == 0))
    def _():
        chip = place_ref[0] // 2
        w_parts = [piece.at[: w_all.shape[0]] for piece in w_refs]
        copies = fetches(
            w_parts, piece_rows(chip, 1, w_refs[0].shape[1], n_w), w_all, 1, sems, 0
        ) + fetches(x_refs, [0, x_refs[0].shape[0]], x_all, 0, sems, n_w)
        for copy in copies:
            copy.start()
        for copy in copies:
            copy.wait()

    @pl.when(block == 0)
    def _():
        weight = w_all[group]
        for k in range(blocks):
            part = pl.ds(k * rows, rows)
            out = (mm(x_all[part, :], weight) + bias_ref[0]).astype(BF16)
            q_out[part, :] = out[:, :lanes2] * (hs**-0.5)
            k_out[part, :] = out[:, lanes2 : 2 * lanes2]
            v_out[part, :] = out[:, 2 * lanes2 :]

    own = pl.ds(pl.multiple_of(block * rows, rows), rows)
    q2 = q_out[own, :]
    own_raw = (q2.astype(F32) * k_out[own, :].astype(F32)).T
    own_values = v_out[own, :].astype(F32).T
    segq = segq_ref[...]
    total = jnp.zeros((2 * hs, rows), F32)
    for head in range(2):
        target = pair_ref[2 * group + head, block]
        there = pl.ds(pl.multiple_of(target * rows, rows), rows)
        keys, values = k_out[there, :], v_out[there, :]
        lanes = head_lanes(q2.shape, head, 1, hs)
        scores = mm_rt(keys, jnp.where(lanes, q2, jnp.zeros_like(q2)))
        scores = jnp.where(segk_ref[there, :] == segq, scores, NEG)
        raw = jnp.sum(own_raw[head * hs : (head + 1) * hs], axis=0, keepdims=True)
        raw = jnp.where(target != block, raw, NEG)
        peak = jnp.maximum(jnp.max(scores, axis=0, keepdims=True), raw)
        expo = jnp.exp(scores - peak)
        own_expo = jnp.exp(raw - peak)
        denom = jnp.sum(expo, axis=0, keepdims=True) + own_expo
        masked_values = jnp.where(lanes, values, jnp.zeros_like(values))
        part = mm_lt(masked_values, expo.astype(BF16))
        low = own_expo.astype(BF16).astype(F32)
        mine = head_lanes(part.shape, head, 0, hs)
        part = part + jnp.where(mine, own_values * low, 0.0)
        total = total + part * (1.0 / denom)
        lse_ref[0, head : head + 1, :] = peak + jnp.log(denom)
    mixed = total.T.astype(BF16)

    @pl.when(block < blocks // 2)
    def _():
        o_mine[pl.ds(pl.multiple_of(block * rows, rows), rows), :] = mixed

    @pl.when(block >= blocks // 2)
    def _():
        o_other[pl.ds(pl.multiple_of((block - blocks // 2) * rows, rows), rows), :] = mixed


def attend(pairs, place, x_parts, w_pieces, bias, segq, segk, hs):
    heads, blocks = pairs.shape
    width = x_parts[0].shape[1]
    seq, groups, lanes = 2 * x_parts[0].shape[0], heads // 2, 2 * hs
    rows = seq // blocks
    kept = jax.ShapeDtypeStruct((seq, groups * lanes), BF16)
    flops = 2 * seq * width * 3 * groups * lanes + 4 * heads * seq * rows * 2 * lanes
    return pl.pallas_call(
        functools.partial(attend_kernel, rows=rows, hs=hs, blocks=blocks, n_w=len(w_pieces)),
        grid_spec=pltpu.PrefetchScalarGridSpec(
            num_scalar_prefetch=2,
            grid=(groups, blocks),
            in_specs=[ANY] * (2 + len(w_pieces))
            + [
                pl.BlockSpec((1, 1, 3 * lanes), lambda g, i, p, q: (g, 0, 0)),
                pl.BlockSpec((1, rows), lambda g, i, p, q: (0, i)),
                pl.BlockSpec((seq, 1), lambda g, i, p, q: (0, 0)),
            ],
            out_specs=[pl.BlockSpec((seq, lanes), lambda g, i, p, q: (0, g))] * 3
            + [
                pl.BlockSpec((seq // 2, lanes), lambda g, i, p, q: (0, g)),
                pl.BlockSpec((seq // 2, lanes), lambda g, i, p, q: (0, g)),
                pl.BlockSpec((1, 8, rows), lambda g, i, p, q: (g, 0, i)),
                pl.BlockSpec((groups, width, 3 * lanes), lambda g, i, p, q: (0, 0, 0)),
            ],
            scratch_shapes=[
                pltpu.VMEM((seq, width), BF16),
                pltpu.SemaphoreType.DMA((2 + len(w_pieces),)),
            ],
        ),
        out_shape=[kept] * 3
        + [jax.ShapeDtypeStruct((seq // 2, groups * lanes), BF16)] * 2
        + [
            jax.ShapeDtypeStruct((groups, 8, seq), F32),
            jax.ShapeDtypeStruct((groups, width, 3 * lanes), BF16),
        ],
        compiler_params=pltpu.CompilerParams(vmem_limit_bytes=LIMIT),
        cost_estimate=COST,
        name="attend",
    )(pairs, place, *x_parts, *w_pieces, bias, segq, segk)


def attend_back_kernel(
    pair_ref, group_ref, q_ref, k_ref, v_ref, do_a, do_b, segq_ref, segk_ref, lse_ref,
    packed_ref, sums_ref, dq_all, dk_acc, dv_acc, *, rows, hs, blocks,
):
    block = pl.program_id(0)

    @pl.when(block == 0)
    def _():
        dk_acc[...] = jnp.zeros_like(dk_acc)
        dv_acc[...] = jnp.zeros_like(dv_acc)
        sums_ref[...] = jnp.zeros_like(sums_ref)

    own = pl.ds(pl.multiple_of(block * rows, rows), rows)
    q2, do2 = q_ref[...], jnp.where(block < blocks // 2, do_a[...], do_b[...])
    qt, dot = q2.astype(F32).T, do2.astype(F32).T
    own_keys, own_values = k_ref[own, :].astype(F32).T, v_ref[own, :].astype(F32).T
    own_raw, own_dp = qt * own_keys, dot * own_values
    segq = segq_ref[...]
    dq = jnp.zeros((2 * hs, rows), F32)
    own_ds, own_low = [], []
    for head in range(2):
        target = pair_ref[2 * group_ref[0] + head, block]
        there = pl.ds(pl.multiple_of(target * rows, rows), rows)
        keys, values = k_ref[there, :], v_ref[there, :]
        lanes = head_lanes(q2.shape, head, 1, hs)
        zero = jnp.zeros_like(q2)
        qm, dom = jnp.where(lanes, q2, zero), jnp.where(lanes, do2, zero)
        lse = lse_ref[0, head : head + 1, :]
        scores = mm_rt(keys, qm)
        probs = jnp.exp(jnp.where(segk_ref[there, :] == segq, scores - lse, NEG))
        raw = jnp.sum(own_raw[head * hs : (head + 1) * hs], axis=0, keepdims=True)
        self_prob = jnp.exp(jnp.where(target != block, raw - lse, NEG))
        self_dp = jnp.sum(own_dp[head * hs : (head + 1) * hs], axis=0, keepdims=True)
        dv_acc[there, :] += mm(probs.astype(BF16), dom)
        dprobs = mm_rt(values, dom)
        delta = jnp.sum(probs * dprobs, axis=0, keepdims=True) + self_prob * self_dp
        dscores = (probs * (dprobs - delta)).astype(BF16)
        dk_acc[there, :] += mm(dscores, qm)
        dq = dq + mm_lt(jnp.where(lanes, keys, jnp.zeros_like(keys)), dscores)
        own_ds.append((self_prob * (self_dp - delta)).astype(BF16).astype(F32))
        own_low.append(self_prob.astype(BF16).astype(F32))
    first = head_lanes(dq.shape, 0, 0, hs)
    ds_rows = jnp.where(first, own_ds[0], own_ds[1])
    low_rows = jnp.where(first, own_low[0], own_low[1])
    dq = ((dq + ds_rows * own_keys) * (hs**-0.5)).T
    dq_all[own, :] = dq.astype(BF16)
    sums_ref[0:1, :] += jnp.sum(dq, axis=0, keepdims=True)
    dk_acc[own, :] += (ds_rows * qt).T
    dv_acc[own, :] += (low_rows * dot).T

    @pl.when(block == blocks - 1)
    def _():
        dv = dv_acc[...]
        sums_ref[1:2, :] = jnp.sum(dv, axis=0, keepdims=True)
        packed_ref[...] = jnp.concatenate(
            [dq_all[...], dk_acc[...].astype(BF16), dv.astype(BF16)], axis=1
        )


def attend_back(pairs, group, q, k, v, grad_a, grad_b, segq, segk, lse, hs):
    heads, blocks = pairs.shape
    seq, lanes = q.shape[0], 2 * hs
    rows, half = seq // blocks, blocks // 2
    return pl.pallas_call(
        functools.partial(attend_back_kernel, rows=rows, hs=hs, blocks=blocks),
        grid_spec=pltpu.PrefetchScalarGridSpec(
            num_scalar_prefetch=2,
            grid=(blocks,),
            in_specs=[
                pl.BlockSpec((rows, lanes), lambda i, p, g: (i, g[0])),
                pl.BlockSpec((seq, lanes), lambda i, p, g: (0, g[0])),
                pl.BlockSpec((seq, lanes), lambda i, p, g: (0, g[0])),
                pl.BlockSpec((rows, lanes), lambda i, p, g: (jnp.minimum(i, half - 1), g[0])),
                pl.BlockSpec((rows, lanes), lambda i, p, g: (jnp.maximum(i - half, 0), g[0])),
                pl.BlockSpec((1, rows), lambda i, p, g: (0, i)),
                pl.BlockSpec((seq, 1), lambda i, p, g: (0, 0)),
                pl.BlockSpec((1, 8, rows), lambda i, p, g: (g[0], 0, i)),
            ],
            out_specs=[
                pl.BlockSpec((seq, 3 * lanes), lambda i, p, g: (0, 0)),
                pl.BlockSpec((8, lanes), lambda i, p, g: (0, 0)),
            ],
            scratch_shapes=[
                pltpu.VMEM((seq, lanes), BF16),
                pltpu.VMEM((seq, lanes), F32),
                pltpu.VMEM((seq, lanes), F32),
            ],
        ),
        out_shape=[
            jax.ShapeDtypeStruct((seq, 3 * lanes), BF16),
            jax.ShapeDtypeStruct((8, lanes), F32),
        ],
        compiler_params=pltpu.CompilerParams(vmem_limit_bytes=LIMIT),
        cost_estimate=COST,
        name="attend_back",
    )(pairs, jnp.full((1,), group, jnp.int32), q, k, v, grad_a, grad_b, segq, segk, lse)


def qkv_grad_kernel(place_ref, xa_ref, xb_ref, p0_ref, p1_ref, p2_ref, keep_ref, send_ref, acc):
    half = xa_ref.shape[0]
    chip = place_ref[0] // 2
    rows = keep_ref.shape[2]
    for j, packed in enumerate((p0_ref, p2_ref, p1_ref)):
        acc[...] = mm_lt(xa_ref[...], packed[:half, :]) + mm_lt(xb_ref[...], packed[half:, :])
        for k, away in enumerate(away_of(j == 2)):
            ours = acc[pl.ds(pl.multiple_of((chip ^ away) * rows, rows), rows), :]
            if k < 2:
                keep_ref[j, k] = ours
            else:
                send_ref[j, k - 2] = ours.astype(BF16)


def qkv_grads(place, x_parts, packed, rows):
    half, width = x_parts[0].shape
    cols = packed[0].shape[1]
    whole = lambda a, b: pl.BlockSpec((a, b), lambda i, p: (0, 0))
    part = pl.BlockSpec((3, 2, rows, cols), lambda i, p: (0, 0, 0, 0))
    return pl.pallas_call(
        qkv_grad_kernel,
        grid_spec=pltpu.PrefetchScalarGridSpec(
            num_scalar_prefetch=1,
            grid=(1,),
            in_specs=[whole(half, width)] * 2 + [whole(2 * half, cols)] * 3,
            out_specs=[part, part],
            scratch_shapes=[pltpu.VMEM((width, cols), F32)],
        ),
        out_shape=[
            jax.ShapeDtypeStruct((3, 2, rows, cols), F32),
            jax.ShapeDtypeStruct((3, 2, rows, cols), BF16),
        ],
        compiler_params=pltpu.CompilerParams(vmem_limit_bytes=LIMIT),
        cost_estimate=COST,
        name="qkv_grads",
    )(place, *x_parts, *packed)


def in_grad_kernel(*refs, n, adds):
    packed, w_ref = refs[:n], refs[n]
    total = mm_rt(packed[0][...], w_ref[0])
    for g in range(1, n):
        total = total + mm_rt(packed[g][...], w_ref[g])
    for extra in refs[n + 1 : n + 1 + adds]:
        total = total + extra[...].astype(F32)
    refs[-1][...] = total.astype(BF16)


def in_grad(packed, weight, second, extras, quarter=0):
    seq, cols = packed[0].shape
    n, width = weight.shape[:2]
    tile = seq // 4
    first = 2 if second else quarter
    steps = 2 if second else 1
    return pl.pallas_call(
        functools.partial(in_grad_kernel, n=n, adds=len(extras)),
        grid=(steps,),
        in_specs=[pl.BlockSpec((tile, cols), lambda i: (first + i, 0))] * n
        + [pl.BlockSpec((n, width, cols), lambda i: (0, 0, 0))]
        + [pl.BlockSpec((tile, width), lambda i: (quarter + i, 0))] * len(extras),
        out_specs=pl.BlockSpec((tile, width), lambda i: (i, 0)),
        out_shape=jax.ShapeDtypeStruct((steps * tile, width), BF16),
        compiler_params=pltpu.CompilerParams(vmem_limit_bytes=LIMIT),
        cost_estimate=COST,
        name="in_grad",
    )(*packed, weight, *extras)


def norm(values):
    centred = values - jnp.mean(values, axis=-1, keepdims=True)
    scale = lax.rsqrt(jnp.mean(centred * centred, axis=-1, keepdims=True) + EPS)
    return centred * scale, scale


def norm_back(grad, unit, scale, gain):
    q = grad * gain
    mean_q = jnp.mean(q, axis=-1, keepdims=True)
    mean_qn = jnp.mean(q * unit, axis=-1, keepdims=True)
    return scale * (q - mean_q - unit * mean_qn)


def gelu_parts(u):
    dense = jnp.exp(-0.5 * u * u) * 0.3989422804014327
    t = 1.0 / (1.0 + 0.2316419 * jnp.abs(u))
    poly = t * (
        0.319381530
        + t * (-0.356563782 + t * (1.781477937 + t * (-1.821255978 + t * 1.330274429)))
    )
    tail = dense * poly
    phi = jnp.where(u >= 0, 1.0 - tail, tail)
    return u * phi, phi + u * dense


def dense_copies(place, pieces, wo, ww, sems):
    copies = []

    def add(source, target):
        copies.append(pltpu.make_async_copy(source, target, sems.at[len(copies)]))

    if len(pieces) == 2:
        add(pieces[0], wo)
        add(pieces[1], ww)
        return copies
    core, chip = place % 2, place // 2
    chips, rows, cols = pieces[0].shape
    for side in range(2):
        lanes = pl.ds(pl.multiple_of((core ^ side) * cols, cols), cols)
        for k in range(chips):
            add(pieces[side].at[k], wo.at[pl.ds(pl.multiple_of((chip ^ k) * rows, rows), rows), lanes])
    half, rows = pieces[2].shape[1:3]
    for k, piece in enumerate(pieces[2:]):
        away = ((0, 1), (0, 2), (2, 3), (1, 3))[k % 4]
        for j in range(2):
            base = (place ^ (2 * away[j] + k // 4)) * rows
            add(piece.at[j], ww.at[pl.ds((k % 2) * half, half), pl.ds(pl.multiple_of(base, rows), rows), :])
    return copies


def dense_kernel(place_ref, *refs, n_w, chunks):
    w_refs, refs = refs[:n_w], refs[n_w:]
    (
        x_ref, mine_ref, other_ref, cot_a, cot_b, vec_ref, upb_ref,
        layer_a, layer_b, gm_mine, gm_other, act_ref, mlow_ref, gb_ref, gul_ref, ga_ref, gone_ref, sums_ref,
        wo, ww, slope, layer, sems,
    ) = refs
    step = pl.program_id(0)
    core = place_ref[0] % 2
    cols = mine_ref.shape[1]
    width = x_ref.shape[1]
    units = ww.shape[2] // 2
    copies = dense_copies(place_ref[0], w_refs, wo, ww, sems)
    n_wo = 1 if len(w_refs) == 2 else 2 * w_refs[0].shape[0]

    @pl.when(step == 0)
    def _():
        for copy in copies:
            copy.start()
        for copy in copies[:n_wo]:
            copy.wait()
        sums_ref[...] = jnp.zeros_like(sums_ref)

    mine_cols = pl.ds(pl.multiple_of(core * cols, cols), cols)
    other_cols = pl.ds(pl.multiple_of((1 - core) * cols, cols), cols)
    early = step < pl.num_programs(0) // 2

    def add_sum(row, values):
        sums_ref[pl.ds(row, 1), :] += jnp.sum(values, axis=0, keepdims=True)

    def advance(at):
        attn = mm_rt(mine_ref[at, :], wo[:, mine_cols]) + mm_rt(other_ref[at, :], wo[:, other_cols])
        yield
        unit_one, scale_one = norm(x_ref[at, :].astype(F32) + attn + vec_ref[0:1, :])
        middle = unit_one * vec_ref[1:2, :] + vec_ref[2:3, :]
        low = middle.astype(BF16)
        mlow_ref[at, :] = low
        total = middle + vec_ref[3:4, :]

        @pl.when(step == 0)
        def _():
            for copy in copies[n_wo:]:
                copy.wait()

        yield
        for k in range(chunks):
            place = slice(k * units, (k + 1) * units)
            upper = mm(low, ww[k, :, :units]) + upb_ref[:, place]
            active, rise = gelu_parts(upper)
            active = active.astype(BF16)
            act_ref[at, place] = active
            slope[at, place] = rise.astype(BF16)
            total = total + mm_rt(active, ww[k, :, units:])
            yield
        unit_two, scale_two = norm(total)
        gain_two = vec_ref[4:5, :]
        layer[at, :] = (unit_two * gain_two + vec_ref[5:6, :]).astype(BF16)
        cot = jnp.where(early, cot_a[at, :], cot_b[at, :]).astype(F32)
        grad_two = norm_back(cot, unit_two, scale_two, gain_two)
        add_sum(4, cot * unit_two)
        add_sum(5, cot)
        add_sum(3, grad_two)
        low = grad_two.astype(BF16)
        gb_ref[at, :] = low
        total = grad_two
        yield
        for k in range(chunks):
            place = slice(k * units, (k + 1) * units)
            grad_upper = mm(low, ww[k, :, units:]) * slope[at, place].astype(F32)
            add_sum(8 + (k ^ place_ref[1]), grad_upper)
            grad_low = grad_upper.astype(BF16)
            gul_ref[at, place] = grad_low
            total = total + mm_rt(grad_low, ww[k, :, :units])
            yield
        add_sum(1, total * unit_one)
        add_sum(2, total)
        grad_one = norm_back(total, unit_one, scale_one, vec_ref[1:2, :])
        add_sum(0, grad_one)
        gone_ref[at, :] = grad_one
        grad_attn = grad_one.astype(BF16)
        ga_ref[at, :] = grad_attn
        yield
        gm_mine[at, :] = mm(grad_attn, wo[:, mine_cols]).astype(BF16)
        gm_other[at, :] = mm(grad_attn, wo[:, other_cols]).astype(BF16)
        yield

    part = x_ref.shape[0] // 1
    for _ in zip(*[advance(slice(part * k, part * (k + 1))) for k in range(1)]):
        pass

    @pl.when(early)
    def _():
        layer_a[...] = layer[...]

    @pl.when(jnp.logical_not(early))
    def _():
        layer_b[...] = layer[...]


def dense(place, w_pieces, x, mine, other, cot_a, cot_b, vec, upb, tile):
    count, width = x.shape
    cols = other.shape[1]
    units = w_pieces[-1].shape[-1] // 2
    chunks = upb.shape[1] // units
    steps = count // tile
    half = steps // 2
    n_copies = 2 if len(w_pieces) == 2 else 2 * w_pieces[0].shape[0] + 2 * (len(w_pieces) - 2)
    rows = lambda n: pl.BlockSpec((tile, n), lambda i, p: (i, 0))
    fixed = lambda a, b: pl.BlockSpec((a, b), lambda i, p: (0, 0))
    full = chunks * units
    shapes = [
        ((count // 2, width), BF16), ((count // 2, width), BF16),
        ((count, cols), BF16), ((count, cols), BF16), ((count, full), BF16),
        ((count, width), BF16), ((count, width), BF16), ((count, full), BF16), ((count, width), BF16),
        ((count, width), F32), ((16, width), F32),
    ]
    flops = 8 * count * width * full + 4 * count * width * 2 * cols
    return pl.pallas_call(
        functools.partial(dense_kernel, n_w=len(w_pieces), chunks=chunks),
        grid_spec=pltpu.PrefetchScalarGridSpec(
            num_scalar_prefetch=1,
            grid=(count // tile,),
            in_specs=[ANY] * len(w_pieces)
            + [rows(width), rows(cols), rows(cols)]
            + [
                pl.BlockSpec((tile, width), lambda i, p: (jnp.minimum(i, half - 1), 0)),
                pl.BlockSpec((tile, width), lambda i, p: (jnp.maximum(i - half, 0), 0)),
                fixed(8, width),
                fixed(1, full),
            ],
            out_specs=[
                pl.BlockSpec((tile, width), lambda i, p: (jnp.minimum(i, half - 1), 0)),
                pl.BlockSpec((tile, width), lambda i, p: (jnp.maximum(i - half, 0), 0)),
                rows(cols), rows(cols), rows(full), rows(width), rows(width), rows(full),
                rows(width), rows(width), fixed(16, width),
            ],
            scratch_shapes=[
                pltpu.VMEM((width, 2 * cols), BF16),
                pltpu.VMEM((chunks, width, 2 * units), BF16),
                pltpu.VMEM((tile, full), BF16),
                pltpu.VMEM((tile, width), BF16),
                pltpu.SemaphoreType.DMA((n_copies,)),
            ],
        ),
        out_shape=[jax.ShapeDtypeStruct(*s) for s in shapes],
        compiler_params=pltpu.CompilerParams(vmem_limit_bytes=LIMIT),
        cost_estimate=COST,
        name="dense",
    )(place, *w_pieces, x, mine, other, cot_a, cot_b, vec, upb)


def away_of(second):
    return [0, jnp.where(second, 1, 2), jnp.where(second, 2, 1), 3]


def grad_kernel(place_ref, *refs, n, steps, drows, first):
    left_ref, right_ref, refs = refs[0], refs[1], refs[2:]
    extra, (keep_ref, send_ref, theirs_ref, left_t, acc) = refs[: n - 2], refs[n - 2 :]
    core, chip = place_ref[0] % 2, place_ref[0] // 2
    step = pl.program_id(0)

    @pl.when(step == 0)
    def _():
        left_t[...] = left_ref[...].T

    @pl.when(step >= steps)
    def _():
        acc[...] = mm(left_t[...], right_ref[...])

    if extra:

        @pl.when(step < steps)
        def _():
            cols = extra[1].shape[1]
            mine_cols = pl.ds(pl.multiple_of(core * cols, cols), cols)
            other_cols = pl.ds(pl.multiple_of((1 - core) * cols, cols), cols)
            acc[:, mine_cols] = mm_lt(extra[0][...], extra[1][...])
            acc[:, other_cols] = mm_lt(extra[0][...], extra[2][...])

    for k, away in enumerate(away_of(step >= first)):
        base = 2 * (chip ^ away)
        ours = acc[pl.ds(pl.multiple_of((base + core) * drows, drows), drows), :]
        if k < 2:
            keep_ref[0, k] = ours
        else:
            send_ref[0, k - 2] = ours.astype(BF16)
        theirs_ref[0, k] = acc[pl.ds(pl.multiple_of((base + 1 - core) * drows, drows), drows), :].astype(BF16)


def weight_grad(place, left, right, extra, drows, first):
    count, width = left.shape
    tile = width
    steps = 1 if extra else 0
    chunks = right.shape[1] // tile + steps
    whole = lambda a, b: pl.BlockSpec((a, b), lambda i, p: (0, 0))
    shapes = [((chunks, 2, drows, tile), F32), ((chunks, 2, drows, tile), BF16), ((chunks, 4, drows, tile), BF16)]
    return pl.pallas_call(
        functools.partial(grad_kernel, n=2 + len(extra), steps=steps, drows=drows, first=first),
        grid_spec=pltpu.PrefetchScalarGridSpec(
            num_scalar_prefetch=1,
            grid=(chunks,),
            in_specs=[
                whole(count, width),
                pl.BlockSpec((count, tile), lambda i, p: (0, jnp.maximum(i - steps, 0))),
            ]
            + [whole(count, e.shape[1]) for e in extra],
            out_specs=[pl.BlockSpec((1,) + shape[1:], lambda i, p: (i, 0, 0, 0)) for shape, _ in shapes],
            scratch_shapes=[pltpu.VMEM((width, count), BF16), pltpu.VMEM((width, tile), F32)],
        ),
        out_shape=[jax.ShapeDtypeStruct(*shape) for shape in shapes],
        compiler_params=pltpu.CompilerParams(vmem_limit_bytes=LIMIT),
        cost_estimate=COST,
        name="weight_grad",
    )(place, left, right, *extra)


def xor_order(parts, index):
    parts = list(parts)
    bit = 1
    while bit < len(parts):
        odd = (index // bit) % 2 == 1
        parts = [jnp.where(odd, parts[k ^ bit], parts[k]) for k in range(len(parts))]
        bit *= 2
    return parts


def per_device(
    tokens,
    segments,
    pairing,
    qkv_weight,
    qv_bias,
    out_weight,
    out_bias,
    first_gain,
    first_shift,
    up_weight,
    up_bias,
    down_weight,
    down_bias,
    second_gain,
    second_shift,
    cotangent,
):
    width = tokens.shape[2]
    rows = tokens.shape[1]
    lheads, blocks = pairing.shape
    hs = qv_bias.shape[1] // 2
    lanes = 2 * hs
    units = up_weight.shape[1]
    ndp, nt = lax.axis_size("dp"), lax.axis_size("tensor")
    drows = width // ndp
    chips = ndp // 2
    dp, tensor = lax.axis_index("dp"), lax.axis_index("tensor")
    core, chip, half, low = dp % 2, dp // 2, tensor // 2, tensor % 2
    slot_mask = 2 * core + low
    heads = 2 * lheads
    cols = heads * hs
    aligned = drows % 8 == 0
    place = jnp.stack([dp, tensor]).astype(jnp.int32)
    order = [0, 1, 3, 4, 2, 5]

    core_pairs = [(i, i ^ 1) for i in range(ndp)]

    def core_swap(x):
        return lax.ppermute(x, "dp", core_pairs)

    def z_step(x, k):
        return lax.ppermute(x, "tensor", [(i, i ^ k) for i in range(nt)])

    def chip_step(x, k):
        return lax.ppermute(x, "dp", [(i, i ^ (2 * k)) for i in range(ndp)])

    def column(k, flip, back):
        steps = []
        for p in range(chips):
            for c in range(2):
                for a in range(2):
                    for b in range(2):
                        home = (2 * p + c) * nt + 2 * a + b
                        away = (2 * p + (a ^ flip)) * nt + 2 * c + (b ^ k)
                        steps.append((away, home) if back else (home, away))
        return steps

    def to_sequence(x):
        return [
            lax.ppermute(
                lax.dynamic_index_in_dim(x, low ^ k, 0, keepdims=False), BOTH, column(k, 0, False)
            )
            for k in range(2)
        ]

    def at_home(first, second):
        return jnp.stack([jnp.where(low == 0, first, second), jnp.where(low == 0, second, first)])

    def z_all(x):
        return [x] + [z_step(x, k) for k in range(1, nt)]

    def chip_all(x):
        return [x] + [chip_step(x, k) for k in range(1, chips)]

    gate = lambda *trees: lax.optimization_barrier(trees)

    qkv_local = qkv_weight.reshape(drows, lheads, 3, hs).transpose(0, 2, 1, 3)
    qkv_local = jnp.concatenate(
        [
            qkv_local[:, :, :2].reshape(drows, 3 * lanes),
            qkv_local[:, :, 2].reshape(drows, 3 * hs),
            out_weight.reshape(lheads * hs, drows).T,
        ],
        axis=1,
    )
    small = jnp.concatenate([pairing.astype(BF16).reshape(-1), qv_bias.reshape(-1), up_bias])
    n_pair, n_qv = lheads * blocks, lheads * lanes
    extra_rows = 8
    small = jnp.pad(small, (0, extra_rows * qkv_local.shape[1] - small.shape[0]))
    first_z = z_all(jnp.concatenate([qkv_local, small.reshape(extra_rows, -1)]))
    segs = jnp.where(half == core, segments, core_swap(segments))
    ff_local = jnp.concatenate([up_weight, down_weight.T], axis=1)
    ff_local, first_z = gate(ff_local, first_z)
    ff_one = z_step(ff_local, 1)

    abs_z = xor_order([part[:drows] for part in first_z], tensor)
    qkv_cols = 3 * lheads * hs

    def regroup(first, second):
        left, right = first[:, 3 * lanes : qkv_cols], second[:, 3 * lanes : qkv_cols]
        both = [part[:, hs * k : hs * (k + 1)] for k in range(3) for part in (left, right)]
        return jnp.stack([first[:, : 3 * lanes], second[:, : 3 * lanes], jnp.concatenate(both, axis=1)])

    def with_out(first, second):
        left, right = first[:, qkv_cols:], second[:, qkv_cols:]
        out = jnp.concatenate([left[:, :lanes], right[:, :lanes], left[:, lanes:], right[:, lanes:]], axis=1)
        return jnp.concatenate([regroup(first, second), out[None]])

    zero_heads, one_heads = with_out(abs_z[0], abs_z[1]), with_out(abs_z[2], abs_z[3])
    keep = jnp.where(core == 0, zero_heads, one_heads)
    got = core_swap(jnp.where(core == 0, one_heads, zero_heads))
    chip_rows = jnp.where(
        core == 0, jnp.concatenate([keep, got], axis=1), jnp.concatenate([got, keep], axis=1)
    )
    ff_pair = jnp.stack([ff_local, ff_one])
    chip_rows, ff_pair = gate(chip_rows, ff_pair)
    qkv_pieces = chip_all(chip_rows)
    ff_middle = lax.ppermute(ff_pair, "tensor", [(1, 2), (2, 1)])

    tokens, ff_middle = gate(tokens, ff_middle)
    ff_end = lax.ppermute(ff_middle, "tensor", [(1, 0), (2, 3)])
    moved = to_sequence(tokens)
    inner = (tensor == 1) | (tensor == 2)
    ff_other = jnp.where(inner, ff_middle[::-1], ff_end)
    qkv_pieces, ff_pair, ff_other, moved[0] = gate(qkv_pieces, ff_pair, ff_other, moved[0])
    out_mine = jnp.stack([piece[3] for piece in qkv_pieces])
    if aligned:
        firsts = [chip_step(ff_pair, 1), chip_step(ff_other, 2)]
        twos = [jnp.stack([ff_pair, firsts[0]]), jnp.stack([ff_other, firsts[1]])]
        twos, moved = gate(twos, moved)
        fours = [chip_step(twos[0], 2), chip_step(twos[1], 1)]
        x_mine = jnp.concatenate(moved)
        x_other = core_swap(x_mine)
        twos_swapped = [core_swap(two) for two in twos]
        cotangent, x_mine, x_other, twos_swapped = gate(cotangent, x_mine, x_other, twos_swapped)
        cot_a, cot_b = to_sequence(cotangent)
    else:
        x_mine = jnp.concatenate(moved)
        x_other = core_swap(x_mine)
        cot_a, cot_b = to_sequence(cotangent)
        out_other = core_swap(out_mine)
        ff_own = chip_all(jnp.concatenate([ff_pair, ff_other]))
        ff_all = [part for piece in ff_own for part in (piece, core_swap(piece))]
        qkv_pieces = [jnp.concatenate(xor_order(qkv_pieces, chip), axis=1)]
        out_both = [jnp.concatenate(xor_order(list(o), chip)) for o in (out_mine, out_other)]
        dense_pieces = [
            jnp.concatenate(
                [jnp.where(core == 0, out_both[0], out_both[1]), jnp.where(core == 0, out_both[1], out_both[0])],
                axis=1,
            ),
            jnp.concatenate(xor_order(ff_all, dp), axis=1),
        ]

    small_rel = [part[drows:].reshape(-1) for part in first_z]
    small = jnp.stack(xor_order(small_rel, tensor))
    all_pairs = small[:, :n_pair].astype(jnp.int32).reshape(2, heads, blocks)
    my_pairs = jnp.where(core == 0, all_pairs[0], all_pairs[1])
    pair_slots = jnp.stack(xor_order([my_pairs[:, k] for k in range(blocks)], slot_mask), axis=1) ^ slot_mask
    pair_slots = jnp.stack([pair_slots[h] for h in order])
    all_qvb = small[:, n_pair : n_pair + n_qv].astype(F32).reshape(2, heads, lanes)
    my_qvb = jnp.where(core == 0, all_qvb[0], all_qvb[1])
    my_qvb = jnp.stack([my_qvb[h] for h in order])
    up_bias_rel = jnp.concatenate([s[n_pair + n_qv :][:units] for s in small_rel]).astype(F32)
    groups = heads // 2
    bias = jnp.concatenate(
        [
            my_qvb[:, :hs].reshape(groups, lanes),
            jnp.zeros((groups, lanes), F32),
            my_qvb[:, hs:].reshape(groups, lanes),
        ],
        axis=1,
    ).reshape(groups, 1, 3 * lanes)

    seg_rows = jnp.where(low == 0, segs[0], segs[1]).reshape(blocks, rows)
    seg_row = jnp.concatenate(xor_order([seg_rows[k] for k in range(blocks)], slot_mask))
    seg_col = seg_row.reshape(blocks * rows, 1)
    seg_row = seg_row.reshape(1, blocks * rows)

    x_parts = [x_mine, x_other]
    q, k, v, mixed, mixed_other, lse, w_all = attend(pair_slots, place, x_parts, qkv_pieces, bias, seg_row, seg_col, hs)
    if aligned:
        q, k, v, mixed, mixed_other, lse, w_all, fours, cot_a, cot_b = gate(
            q, k, v, mixed, mixed_other, lse, w_all, fours, cot_a, cot_b
        )
        out_mine, mixed_other = gate(out_mine, mixed_other)
        out_other = core_swap(out_mine)
        dense_pieces = [out_mine, out_other] + twos + fours + twos_swapped + [core_swap(four) for four in fours]
    other = core_swap(mixed_other)

    blank = jnp.zeros((width,), BF16)
    vec = jnp.stack(
        [out_bias, first_gain, first_shift, down_bias, second_gain, second_shift, blank, blank]
    ).astype(F32)
    (
        layer_a, layer_b, gm_mine, gm_other, active, middle_low, grad_branch, grad_upper, grad_attn, grad_one, sums,
    ) = dense(
        place, dense_pieces, x_mine, mixed, other, cot_a, cot_b, vec, up_bias_rel.reshape(1, nt * units), 256
    )
    gm_got = core_swap(gm_other)
    home_0 = lax.ppermute(layer_a, BOTH, column(0, 0, True))

    def total_of(parts):
        total = parts[0].astype(F32)
        for part in parts[1:]:
            total = total + part.astype(F32)
        return total

    class Plane:
        def __init__(self, first, keep, send, got=None):
            self.first, self.got = first, got
            self.keep, self.send = self.split(keep), self.split(send)

        def split(self, x):
            return [x[: self.first], x[self.first :]]

        def first_sends(self):
            if self.got is None:
                return self.send
            got = self.split(self.got)
            self.keep = [[keep, g[:, :2]] for keep, g in zip(self.keep, got)]
            return [total_of([send, g[:, 2:]]).astype(BF16) for send, g in zip(self.send, got)]

        def first_moves(self, sends):
            return [chip_step(sends[0], 1), chip_step(sends[1], 2)]

        def second_sends(self, moves):
            keep = [k if isinstance(k, list) else [k] for k in self.keep]
            own = [total_of([part[:, 0] for part in k] + [m[:, 0]]) for k, m in zip(keep, moves)]
            sends = [total_of([part[:, 1] for part in k] + [m[:, 1]]).astype(BF16) for k, m in zip(keep, moves)]
            return own, sends

        def second_moves(self, sends):
            return [chip_step(sends[0], 2), chip_step(sends[1], 1)]

        def sums(self, own, moves):
            return [total_of([o, m]) for o, m in zip(own, moves)]

    class SlowPlane(Plane):
        def __init__(self, first, keep, send, got=None):
            self.first, self.view = first, keep if got is None else keep + got.astype(F32)

        def first_sends(self):
            return []

        def first_moves(self, sends):
            return []

        def second_sends(self, moves):
            return [], []

        def second_moves(self, sends):
            return []

        def sums(self, own, moves):
            pick = lambda step: lax.dynamic_index_in_dim(self.view, chip ^ step, 0, keepdims=False)
            total = total_of([pick(0)] + [chip_step(pick(step).astype(BF16), step) for step in range(1, chips)])
            return self.split(total.transpose(1, 0, 2))

    fast = chips == 4 and aligned

    def grads_of(left, right, extra, first):
        if fast:
            return weight_grad(place, left, right, extra, drows, first)
        grads = mm_lt(left, right)
        if extra:
            near, far = mm_lt(extra[0], extra[1]), mm_lt(extra[0], extra[2])
            head = [jnp.where(core == 0, near, far), jnp.where(core == 0, far, near)]
            grads = jnp.concatenate(head + [grads], axis=1)
        view = grads.reshape(chips, 2, drows, grads.shape[1] // width, width)
        ours = lax.dynamic_index_in_dim(view, core, 1, keepdims=False)
        theirs = lax.dynamic_index_in_dim(view, 1 - core, 1, keepdims=False).astype(BF16)
        return ours, theirs, theirs

    plane_of = Plane if fast else SlowPlane
    down_keep, down_send, down_theirs = grads_of(grad_branch, active, [], 2)
    down_got = core_swap(down_theirs)
    middle_low, down_keep, down_send, down_theirs, gm_got = gate(
        middle_low, down_keep, down_send, down_theirs, gm_got
    )
    up_keep, up_send, up_theirs = grads_of(middle_low, grad_upper, [grad_attn, mixed, other], 3)
    up_keep, up_send, up_theirs, home_0 = gate(up_keep, up_send, up_theirs, home_0)
    up_got = core_swap(up_theirs)

    down = plane_of(2, down_keep, down_send, down_got)
    d_sends = down.first_sends()
    pairs_0, gm_got, d_sends, layer_b = gate(pair_slots, gm_got, d_sends, layer_b)
    d_moves = down.first_moves(d_sends)
    home_1 = lax.ppermute(layer_b, BOTH, column(1, 0, True))
    packed_0, sums_0 = attend_back(pairs_0, 0, q, k, v, gm_mine, gm_got, seg_row, seg_col, lse, hs)
    packed_0, sums_0, d_moves, up_got, home_1 = gate(packed_0, sums_0, d_moves, up_got, home_1)
    layer_out = at_home(home_0, home_1)
    d_own, d_sends = down.second_sends(d_moves)
    up = plane_of(3, up_keep, up_send, up_got)
    u_sends = up.first_sends()
    pairs_1, d_own, d_sends, u_sends = gate(pair_slots, d_own, d_sends, u_sends)
    d_moves = down.second_moves(d_sends)
    u_moves = up.first_moves(u_sends)
    packed_1, sums_1 = attend_back(pairs_1, 1, q, k, v, gm_mine, gm_got, seg_row, seg_col, lse, hs)
    packed_1, sums_1, d_moves = gate(packed_1, sums_1, d_moves)
    d_first, d_second = down.sums(d_own, d_moves)
    d_second = d_second.astype(BF16)
    pair_slots, packed_1, d_first, d_second = gate(pair_slots, packed_1, d_first, d_second)
    d_second = z_step(d_second, 2)
    packed_2, sums_2 = attend_back(pair_slots, 2, q, k, v, gm_mine, gm_got, seg_row, seg_col, lse, hs)
    packed_2, sums_2, u_moves, d_second = gate(packed_2, sums_2, u_moves, d_second)
    d_keep = total_of([d_first[0], d_second[0]])
    d_give = total_of([d_first[1], d_second[1]]).astype(BF16)
    u_own, u_sends = up.second_sends(u_moves)

    head_sums = jnp.concatenate([part[row] for row in range(2) for part in (sums_0, sums_1, sums_2)])[None]
    blank = jnp.zeros_like(head_sums)
    sums = jnp.concatenate(
        [
            sums[:12],
            jnp.where(core == 0, head_sums, blank),
            jnp.where(core == 0, blank, head_sums),
            jnp.zeros((2, width), F32),
        ]
    )
    packed_2, d_keep, d_give, u_own, u_sends, sums = gate(packed_2, d_keep, d_give, u_own, u_sends, sums)
    packed = [packed_0, packed_1, packed_2]
    d_give = z_step(d_give, 1)
    sums_got = z_step(sums, 1)
    in_other = in_grad(packed, w_all, True, [])
    in_other, sums_got, packed, d_give, u_sends = gate(in_other, sums_got, packed, d_give, u_sends)
    down_grad = (d_keep + d_give.astype(F32)).T
    in_got = core_swap(in_other)
    u_moves = up.second_moves(u_sends)
    sums = sums + sums_got
    sums_got = z_step(sums, 2)
    if fast:
        qkv_keep, qkv_send = qkv_grads(place, x_parts, packed, 2 * drows)
    else:
        parts = [mm_lt(jnp.concatenate(x_parts), packed[g]).reshape(chips, 2 * drows, 3 * lanes) for g in (0, 2, 1)]
        qkv_keep = qkv_send = jnp.stack(parts, axis=2)
    qkv_keep, qkv_send, packed, in_got, sums_got, u_moves = gate(qkv_keep, qkv_send, packed, in_got, sums_got, u_moves)
    sums = sums + sums_got
    qkv = plane_of(2, qkv_keep, qkv_send)
    a_sends = qkv.first_sends()
    u_first, u_second = up.sums(u_own, u_moves)
    out_near = jnp.where(half == 0, u_first[0, :, :cols], u_first[0, :, cols:])
    out_far = jnp.where(half == 0, u_first[0, :, cols:], u_first[0, :, :cols])
    u_first = u_first[1:]
    u_second = jnp.concatenate([u_second[0], u_second[1], out_far], axis=1).astype(BF16)
    packed, a_sends, sums, u_first, u_second, out_near = gate(packed, a_sends, sums, u_first, u_second, out_near)
    u_second = z_step(u_second, 2)
    a_moves = qkv.first_moves(a_sends)
    sums_got = core_swap(sums)
    in_first = in_grad(packed, w_all, False, [in_got, grad_one], 0)
    in_first, packed, sums_got, u_second = gate(in_first, packed, sums_got, u_second)
    sums = sums + sums_got
    home_a = lax.ppermute(in_first, BOTH, column(0, 0, True))
    in_second = in_grad(packed, w_all, False, [in_got, grad_one], 1)
    in_second, sums, a_moves, home_a = gate(in_second, sums, a_moves, home_a)
    homes = [home_a, lax.ppermute(in_second, BOTH, column(1, 0, True))]
    a_own, a_sends = qkv.second_sends(a_moves)
    u_keep, u_give = [total_of([u_first[j], u_second[:, units * j : units * (j + 1)]]) for j in range(2)]
    out_near = total_of([out_near, u_second[:, 2 * units :]])

    def out_unit(wanted_low):
        parts = [
            jnp.concatenate(
                [out_near[:, lanes * w : lanes * (w + 1)], out_near[:, 2 * lanes + hs * w : 2 * lanes + hs * (w + 1)]],
                axis=1,
            )
            for w in range(2)
        ]
        return jnp.where(wanted_low == 0, parts[0], parts[1])

    u_give = jnp.concatenate([u_give, out_unit(1 - low)], axis=1).astype(BF16)
    out_near = out_unit(low)
    a_moves = qkv.second_moves(a_sends)
    u_give = z_step(u_give, 1)
    up_grad = total_of([u_keep, u_give[:, :units]])
    out_grad = total_of([out_near, u_give[:, units:]]).T.reshape(lheads, hs, drows)
    for bit in range(chips.bit_length() - 1):
        sums = sums + chip_step(sums, 1 << bit)
    outb_grad, gain_one_grad, shift_one_grad, downb_grad, gain_two_grad, shift_two_grad = [
        sums[row] for row in range(6)
    ]
    upb_grad = lax.dynamic_index_in_dim(sums, 8 + tensor, 0, keepdims=False)
    head_row = jnp.where(half == 0, sums[12], sums[13]).reshape(2, 6, hs)
    qvb_grad = jnp.where(low == 0, head_row[:, [0, 1, 4]], head_row[:, [2, 3, 5]])
    qvb_grad = jnp.concatenate([qvb_grad[0], qvb_grad[1]], axis=1)

    homes, a_moves = gate(homes, a_moves)
    input_grad = at_home(*homes)
    sum_a, sum_b = qkv.sums(a_own, a_moves)
    sum_0, sum_2, sum_1 = [part.reshape(2, drows, 3 * lanes) for part in (sum_a[0], sum_a[1], sum_b[0])]
    sum_01 = [sum_0, sum_1]

    def share(c, u):
        third = [sum_2[c][:, lanes * k + hs * u : lanes * k + hs * (u + 1)] for k in range(3)]
        return jnp.concatenate([sum_01[u][c]] + third, axis=1)

    shares = [[share(c, u).astype(BF16) for u in range(2)] for c in range(2)]
    qkv_grad = jnp.zeros((drows, 3 * lheads * hs), F32)
    for flip in range(2):
        for step in range(2):
            by_core = [jnp.where((low ^ step) == 0, shares[c][0], shares[c][1]) for c in range(2)]
            sent = jnp.where((half ^ flip) == 0, by_core[0], by_core[1])
            qkv_grad = qkv_grad + lax.ppermute(sent, BOTH, column(step, flip, False)).astype(F32)
    pairs_part = qkv_grad[:, : 3 * lanes].reshape(drows, 3, 2, hs)
    third_part = qkv_grad[:, 3 * lanes :].reshape(drows, 3, 1, hs)
    qkv_grad = jnp.concatenate([pairs_part, third_part], axis=2).transpose(0, 2, 1, 3)
    qkv_grad = qkv_grad.reshape(drows, lheads, 3 * hs)
    return (
        layer_out,
        input_grad,
        qkv_grad,
        qvb_grad,
        out_grad,
        outb_grad,
        gain_one_grad,
        shift_one_grad,
        up_grad,
        upb_grad,
        down_grad,
        downb_grad,
        gain_two_grad,
        shift_two_grad,
    )


def solution(mesh):
    return jax.shard_map(
        per_device,
        mesh=mesh,
        in_specs=(
            P("dp", "tensor", None),
            P("dp", None),
            P("tensor", None),
            P("dp", "tensor", None),
            P("tensor", None),
            P("tensor", None, "dp"),
            P(),
            P(),
            P(),
            P("dp", "tensor"),
            P("tensor"),
            P("tensor", "dp"),
            P(),
            P(),
            P(),
            P("dp", "tensor", None),
        ),
        out_specs=(
            P("dp", "tensor", None),
            P("dp", "tensor", None),
            P("dp", "tensor", None),
            P("tensor", None),
            P("tensor", None, "dp"),
            P(),
            P(),
            P(),
            P("dp", "tensor"),
            P("tensor"),
            P("tensor", "dp"),
            P(),
            P(),
            P(),
        ),
        check_vma=False,
    )
```

```python
import functools

import jax
import jax.numpy as jnp
from jax import lax
from jax.experimental import pallas as pl
from jax.experimental.pallas import tpu as pltpu
from jax.sharding import PartitionSpec as P

EPS = 1e-06
NEG = -1e30
BOTH = ("dp", "tensor")
F32 = jnp.float32
BF16 = jnp.bfloat16
ANY = pl.BlockSpec(memory_space=pl.ANY)
LIMIT = 58 << 20
COST = pl.CostEstimate(flops=10**9, bytes_accessed=1 << 16, transcendentals=0)


def mm(left, right):
    return lax.dot_general(left, right, (((1,), (0,)), ((), ())), preferred_element_type=F32)


def mm_rt(left, right):
    return lax.dot_general(left, right, (((1,), (1,)), ((), ())), preferred_element_type=F32)


def mm_lt(left, right):
    return lax.dot_general(left, right, (((0,), (0,)), ((), ())), preferred_element_type=F32)


def head_lanes(shape, head, dim, head_size):
    place = lax.broadcasted_iota(jnp.int32, shape, dim)
    return (place < head_size) if head == 0 else (place >= head_size)


def fetches(pieces, offsets, target, dim, sems, first):
    copies = []
    for k, (piece, offset) in enumerate(zip(pieces, offsets)):
        count = piece.shape[dim]
        where = pl.ds(offset if isinstance(offset, int) else pl.multiple_of(offset, count), count)
        index = (slice(None),) * dim + (where,)
        copies.append(pltpu.make_async_copy(piece, target.at[index], sems.at[first + k]))
    return copies


def piece_rows(place, step, rows, count):
    if count == 1:
        return [0]
    return [(place ^ (k * step)) * rows for k in range(count)]


def attend_kernel(pair_ref, place_ref, *refs, rows, hs, blocks, n_w):
    x_refs, refs = refs[:2], refs[2:]
    w_refs, refs = refs[:n_w], refs[n_w:]
    bias_ref, segq_ref, segk_ref, q_out, k_out, v_out, o_mine, o_other, lse_ref, w_all, x_all, sems = refs
    group, block = pl.program_id(0), pl.program_id(1)
    lanes2 = 2 * hs

    @pl.when((group == 0) & (block == 0))
    def _():
        chip = place_ref[0] // 2
        w_parts = [piece.at[: w_all.shape[0]] for piece in w_refs]
        copies = fetches(
            w_parts, piece_rows(chip, 1, w_refs[0].shape[1], n_w), w_all, 1, sems, 0
        ) + fetches(x_refs, [0, x_refs[0].shape[0]], x_all, 0, sems, n_w)
        for copy in copies:
            copy.start()
        for copy in copies:
            copy.wait()

    @pl.when(block == 0)
    def _():
        weight = w_all[group]
        for k in range(blocks):
            part = pl.ds(k * rows, rows)
            out = (mm(x_all[part, :], weight) + bias_ref[0]).astype(BF16)
            q_out[part, :] = out[:, :lanes2] * (hs**-0.5)
            k_out[part, :] = out[:, lanes2 : 2 * lanes2]
            v_out[part, :] = out[:, 2 * lanes2 :]

    own = pl.ds(pl.multiple_of(block * rows, rows), rows)
    q2 = q_out[own, :]
    own_raw = (q2.astype(F32) * k_out[own, :].astype(F32)).T
    own_values = v_out[own, :].astype(F32).T
    segq = segq_ref[...]
    total = jnp.zeros((2 * hs, rows), F32)
    for head in range(2):
        target = pair_ref[2 * group + head, block]
        there = pl.ds(pl.multiple_of(target * rows, rows), rows)
        keys, values = k_out[there, :], v_out[there, :]
        lanes = head_lanes(q2.shape, head, 1, hs)
        scores = mm_rt(keys, jnp.where(lanes, q2, jnp.zeros_like(q2)))
        scores = jnp.where(segk_ref[there, :] == segq, scores, NEG)
        raw = jnp.sum(own_raw[head * hs : (head + 1) * hs], axis=0, keepdims=True)
        raw = jnp.where(target != block, raw, NEG)
        peak = jnp.maximum(jnp.max(scores, axis=0, keepdims=True), raw)
        expo = jnp.exp(scores - peak)
        own_expo = jnp.exp(raw - peak)
        denom = jnp.sum(expo, axis=0, keepdims=True) + own_expo
        masked_values = jnp.where(lanes, values, jnp.zeros_like(values))
        part = mm_lt(masked_values, expo.astype(BF16))
        low = own_expo.astype(BF16).astype(F32)
        mine = head_lanes(part.shape, head, 0, hs)
        part = part + jnp.where(mine, own_values * low, 0.0)
        total = total + part * (1.0 / denom)
        lse_ref[0, head : head + 1, :] = peak + jnp.log(denom)
    mixed = total.T.astype(BF16)

    @pl.when(block < blocks // 2)
    def _():
        o_mine[pl.ds(pl.multiple_of(block * rows, rows), rows), :] = mixed

    @pl.when(block >= blocks // 2)
    def _():
        o_other[pl.ds(pl.multiple_of((block - blocks // 2) * rows, rows), rows), :] = mixed


def attend(pairs, place, x_parts, w_pieces, bias, segq, segk, hs):
    heads, blocks = pairs.shape
    width = x_parts[0].shape[1]
    seq, groups, lanes = 2 * x_parts[0].shape[0], heads // 2, 2 * hs
    rows = seq // blocks
    kept = jax.ShapeDtypeStruct((seq, groups * lanes), BF16)
    flops = 2 * seq * width * 3 * groups * lanes + 4 * heads * seq * rows * 2 * lanes
    return pl.pallas_call(
        functools.partial(attend_kernel, rows=rows, hs=hs, blocks=blocks, n_w=len(w_pieces)),
        grid_spec=pltpu.PrefetchScalarGridSpec(
            num_scalar_prefetch=2,
            grid=(groups, blocks),
            in_specs=[ANY] * (2 + len(w_pieces))
            + [
                pl.BlockSpec((1, 1, 3 * lanes), lambda g, i, p, q: (g, 0, 0)),
                pl.BlockSpec((1, rows), lambda g, i, p, q: (0, i)),
                pl.BlockSpec((seq, 1), lambda g, i, p, q: (0, 0)),
            ],
            out_specs=[pl.BlockSpec((seq, lanes), lambda g, i, p, q: (0, g))] * 3
            + [
                pl.BlockSpec((seq // 2, lanes), lambda g, i, p, q: (0, g)),
                pl.BlockSpec((seq // 2, lanes), lambda g, i, p, q: (0, g)),
                pl.BlockSpec((1, 8, rows), lambda g, i, p, q: (g, 0, i)),
                pl.BlockSpec((groups, width, 3 * lanes), lambda g, i, p, q: (0, 0, 0)),
            ],
            scratch_shapes=[
                pltpu.VMEM((seq, width), BF16),
                pltpu.SemaphoreType.DMA((2 + len(w_pieces),)),
            ],
        ),
        out_shape=[kept] * 3
        + [jax.ShapeDtypeStruct((seq // 2, groups * lanes), BF16)] * 2
        + [
            jax.ShapeDtypeStruct((groups, 8, seq), F32),
            jax.ShapeDtypeStruct((groups, width, 3 * lanes), BF16),
        ],
        compiler_params=pltpu.CompilerParams(vmem_limit_bytes=58 << 20),
        cost_estimate=COST,
        name="attend",
    )(pairs, place, *x_parts, *w_pieces, bias, segq, segk)


def attend_back_kernel(
    pair_ref, group_ref, q_ref, k_ref, v_ref, do_a, do_b, segq_ref, segk_ref, lse_ref,
    packed_ref, sums_ref, dq_all, dk_acc, dv_acc, *, rows, hs, blocks,
):
    block = pl.program_id(0)

    @pl.when(block == 0)
    def _():
        dk_acc[...] = jnp.zeros_like(dk_acc)
        dv_acc[...] = jnp.zeros_like(dv_acc)
        sums_ref[...] = jnp.zeros_like(sums_ref)

    own = pl.ds(pl.multiple_of(block * rows, rows), rows)
    q2, do2 = q_ref[...], jnp.where(block < blocks // 2, do_a[...], do_b[...])
    qt, dot = q2.astype(F32).T, do2.astype(F32).T
    own_keys, own_values = k_ref[own, :].astype(F32).T, v_ref[own, :].astype(F32).T
    own_raw, own_dp = qt * own_keys, dot * own_values
    segq = segq_ref[...]
    dq = jnp.zeros((2 * hs, rows), F32)
    own_ds, own_low = [], []
    for head in range(2):
        target = pair_ref[2 * group_ref[0] + head, block]
        there = pl.ds(pl.multiple_of(target * rows, rows), rows)
        keys, values = k_ref[there, :], v_ref[there, :]
        lanes = head_lanes(q2.shape, head, 1, hs)
        zero = jnp.zeros_like(q2)
        qm, dom = jnp.where(lanes, q2, zero), jnp.where(lanes, do2, zero)
        lse = lse_ref[0, head : head + 1, :]
        scores = mm_rt(keys, qm)
        probs = jnp.exp(jnp.where(segk_ref[there, :] == segq, scores - lse, NEG))
        raw = jnp.sum(own_raw[head * hs : (head + 1) * hs], axis=0, keepdims=True)
        self_prob = jnp.exp(jnp.where(target != block, raw - lse, NEG))
        self_dp = jnp.sum(own_dp[head * hs : (head + 1) * hs], axis=0, keepdims=True)
        dv_acc[there, :] += mm(probs.astype(BF16), dom)
        dprobs = mm_rt(values, dom)
        delta = jnp.sum(probs * dprobs, axis=0, keepdims=True) + self_prob * self_dp
        dscores = (probs * (dprobs - delta)).astype(BF16)
        dk_acc[there, :] += mm(dscores, qm)
        dq = dq + mm_lt(jnp.where(lanes, keys, jnp.zeros_like(keys)), dscores)
        own_ds.append((self_prob * (self_dp - delta)).astype(BF16).astype(F32))
        own_low.append(self_prob.astype(BF16).astype(F32))
    first = head_lanes(dq.shape, 0, 0, hs)
    ds_rows = jnp.where(first, own_ds[0], own_ds[1])
    low_rows = jnp.where(first, own_low[0], own_low[1])
    dq = ((dq + ds_rows * own_keys) * (hs**-0.5)).T
    dq_all[own, :] = dq.astype(BF16)
    sums_ref[0:1, :] += jnp.sum(dq, axis=0, keepdims=True)
    dk_acc[own, :] += (ds_rows * qt).T
    dv_acc[own, :] += (low_rows * dot).T

    @pl.when(block == blocks - 1)
    def _():
        dv = dv_acc[...]
        sums_ref[1:2, :] = jnp.sum(dv, axis=0, keepdims=True)
        packed_ref[...] = jnp.concatenate(
            [dq_all[...], dk_acc[...].astype(BF16), dv.astype(BF16)], axis=1
        )


def attend_back(pairs, group, q, k, v, grad_a, grad_b, segq, segk, lse, hs):
    heads, blocks = pairs.shape
    seq, lanes = q.shape[0], 2 * hs
    rows, half = seq // blocks, blocks // 2
    return pl.pallas_call(
        functools.partial(attend_back_kernel, rows=rows, hs=hs, blocks=blocks),
        grid_spec=pltpu.PrefetchScalarGridSpec(
            num_scalar_prefetch=2,
            grid=(blocks,),
            in_specs=[
                pl.BlockSpec((rows, lanes), lambda i, p, g: (i, g[0])),
                pl.BlockSpec((seq, lanes), lambda i, p, g: (0, g[0])),
                pl.BlockSpec((seq, lanes), lambda i, p, g: (0, g[0])),
                pl.BlockSpec((rows, lanes), lambda i, p, g: (jnp.minimum(i, half - 1), g[0])),
                pl.BlockSpec((rows, lanes), lambda i, p, g: (jnp.maximum(i - half, 0), g[0])),
                pl.BlockSpec((1, rows), lambda i, p, g: (0, i)),
                pl.BlockSpec((seq, 1), lambda i, p, g: (0, 0)),
                pl.BlockSpec((1, 8, rows), lambda i, p, g: (g[0], 0, i)),
            ],
            out_specs=[
                pl.BlockSpec((seq, 3 * lanes), lambda i, p, g: (0, 0)),
                pl.BlockSpec((8, lanes), lambda i, p, g: (0, 0)),
            ],
            scratch_shapes=[
                pltpu.VMEM((seq, lanes), BF16),
                pltpu.VMEM((seq, lanes), F32),
                pltpu.VMEM((seq, lanes), F32),
            ],
        ),
        out_shape=[
            jax.ShapeDtypeStruct((seq, 3 * lanes), BF16),
            jax.ShapeDtypeStruct((8, lanes), F32),
        ],
        compiler_params=pltpu.CompilerParams(vmem_limit_bytes=12 << 20),
        cost_estimate=COST,
        name="attend_back",
    )(pairs, jnp.full((1,), group, jnp.int32), q, k, v, grad_a, grad_b, segq, segk, lse)


def qkv_grad_kernel(place_ref, *refs):
    packed_refs, xa_ref, xb_ref, keep_ref, send_a, send_b, packed, acc, sems = refs[:3], *refs[3:]
    half = xa_ref.shape[0]
    chip = place_ref[0] // 2
    rows = keep_ref.shape[2]
    step = pl.program_id(0)
    copies = [
        pltpu.make_async_copy(packed_refs[g], packed.at[j], sems.at[j]) for j, g in enumerate((0, 2, 1))
    ]

    @pl.when(step == 0)
    def _():
        for copy in copies:
            copy.start()

    for j, copy in enumerate(copies):

        @pl.when(step == j)
        def _(copy=copy):
            copy.wait()

    acc[...] = mm_lt(xa_ref[...], packed[step, :half, :]) + mm_lt(xb_ref[...], packed[step, half:, :])
    for k, away in enumerate(away_of(step == 2)):
        ours = acc[pl.ds(pl.multiple_of((chip ^ away) * rows, rows), rows), :]
        if k < 2:
            keep_ref[0, k] = ours
        else:
            ours = ours.astype(BF16)

            @pl.when(step < 2)
            def _(ours=ours, k=k):
                send_a[0, k - 2] = ours

            @pl.when(step == 2)
            def _(ours=ours, k=k):
                send_b[0, k - 2] = ours


def qkv_grads(place, x_parts, packed, rows):
    half, width = x_parts[0].shape
    cols = packed[0].shape[1]
    whole = lambda a, b: pl.BlockSpec((a, b), lambda i, p: (0, 0))
    return pl.pallas_call(
        qkv_grad_kernel,
        grid_spec=pltpu.PrefetchScalarGridSpec(
            num_scalar_prefetch=1,
            grid=(3,),
            in_specs=[ANY] * 3 + [whole(half, width)] * 2,
            out_specs=[
                pl.BlockSpec((1, 2, rows, cols), lambda i, p: (i, 0, 0, 0)),
                pl.BlockSpec((1, 2, rows, cols), lambda i, p: (jnp.minimum(i, 1), 0, 0, 0)),
                pl.BlockSpec((1, 2, rows, cols), lambda i, p: (0, 0, 0, 0)),
            ],
            scratch_shapes=[
                pltpu.VMEM((3, 2 * half, cols), BF16),
                pltpu.VMEM((width, cols), F32),
                pltpu.SemaphoreType.DMA((3,)),
            ],
        ),
        out_shape=[
            jax.ShapeDtypeStruct((3, 2, rows, cols), F32),
            jax.ShapeDtypeStruct((2, 2, rows, cols), BF16),
            jax.ShapeDtypeStruct((1, 2, rows, cols), BF16),
        ],
        compiler_params=pltpu.CompilerParams(vmem_limit_bytes=18 << 20),
        cost_estimate=COST,
        name="qkv_grads",
    )(place, *packed, *x_parts)


def in_grad_kernel(*refs, n, half):
    packed, w_ref, extra, mine_ref, other_ref = refs[:n], refs[n], *refs[n + 1 :]
    step = pl.program_id(0)
    total = mm_rt(packed[0][...], w_ref[0])
    for g in range(1, n):
        total = total + mm_rt(packed[g][...], w_ref[g])

    @pl.when(step < half)
    def _():
        other_ref[...] = total.astype(BF16)

    @pl.when(step >= half)
    def _():
        mine_ref[...] = total + extra[...]


def in_grad(packed, weight, extra):
    seq, cols = packed[0].shape
    n, width = weight.shape[:2]
    half = 2
    tile = seq // (2 * half)
    late = lambda i: (jnp.maximum(i - half, 0), 0)
    return pl.pallas_call(
        functools.partial(in_grad_kernel, n=n, half=half),
        grid=(2 * half,),
        in_specs=[pl.BlockSpec((tile, cols), lambda i: ((i + half) % (2 * half), 0))] * n
        + [pl.BlockSpec((n, width, cols), lambda i: (0, 0, 0)), pl.BlockSpec((tile, width), late)],
        out_specs=[
            pl.BlockSpec((tile, width), late),
            pl.BlockSpec((tile, width), lambda i: (jnp.minimum(i, half - 1), 0)),
        ],
        out_shape=[
            jax.ShapeDtypeStruct((seq // 2, width), F32),
            jax.ShapeDtypeStruct((seq // 2, width), BF16),
        ],
        compiler_params=pltpu.CompilerParams(vmem_limit_bytes=12 << 20),
        cost_estimate=COST,
        name="in_grad",
    )(*packed, weight, extra)


def norm(values):
    centred = values - jnp.mean(values, axis=-1, keepdims=True)
    scale = lax.rsqrt(jnp.mean(centred * centred, axis=-1, keepdims=True) + EPS)
    return centred * scale, scale


def norm_back(grad, unit, scale, gain):
    q = grad * gain
    mean_q = jnp.mean(q, axis=-1, keepdims=True)
    mean_qn = jnp.mean(q * unit, axis=-1, keepdims=True)
    return scale * (q - mean_q - unit * mean_qn)


def gelu_parts(u):
    dense = jnp.exp(-0.5 * u * u) * 0.3989422804014327
    t = 1.0 / (1.0 + 0.2316419 * jnp.abs(u))
    poly = t * (
        0.319381530
        + t * (-0.356563782 + t * (1.781477937 + t * (-1.821255978 + t * 1.330274429)))
    )
    tail = dense * poly
    phi = jnp.where(u >= 0, 1.0 - tail, tail)
    return u * phi, phi + u * dense


def dense_copies(place, pieces, wo, ww, sems):
    copies = []

    def add(source, target):
        copies.append(pltpu.make_async_copy(source, target, sems.at[len(copies)]))

    if len(pieces) == 2:
        add(pieces[0], wo)
        add(pieces[1], ww)
        return copies
    core, chip = place % 2, place // 2
    chips, rows, cols = pieces[0].shape
    for side in range(2):
        lanes = pl.ds(pl.multiple_of((core ^ side) * cols, cols), cols)
        for k in range(chips):
            add(pieces[side].at[k], wo.at[pl.ds(pl.multiple_of((chip ^ k) * rows, rows), rows), lanes])
    half, rows = pieces[2].shape[1:3]
    for k, piece in enumerate(pieces[2:]):
        away = ((0, 1), (0, 2), (2, 3), (1, 3))[k % 4]
        for j in range(2):
            base = (place ^ (2 * away[j] + k // 4)) * rows
            add(piece.at[j], ww.at[pl.ds((k % 2) * half, half), pl.ds(pl.multiple_of(base, rows), rows), :])
    return copies


def dense_kernel(place_ref, *refs, n_w, chunks):
    w_refs, refs = refs[:n_w], refs[n_w:]
    (
        x_ref, mine_ref, other_ref, cot_a, cot_b, vec_ref, upb_ref,
        layer_a, layer_b, gm_mine, gm_other, act_ref, mlow_ref, gb_ref, gul_ref, ga_ref, gone_ref, sums_ref,
        wo, ww, slope, layer, sems,
    ) = refs
    step = pl.program_id(0)
    core = place_ref[0] % 2
    cols = mine_ref.shape[1]
    width = x_ref.shape[1]
    units = ww.shape[2] // 2
    copies = dense_copies(place_ref[0], w_refs, wo, ww, sems)
    n_wo = 1 if len(w_refs) == 2 else 2 * w_refs[0].shape[0]

    @pl.when(step == 0)
    def _():
        for copy in copies:
            copy.start()
        for copy in copies[:n_wo]:
            copy.wait()
        sums_ref[...] = jnp.zeros_like(sums_ref)

    mine_cols = pl.ds(pl.multiple_of(core * cols, cols), cols)
    other_cols = pl.ds(pl.multiple_of((1 - core) * cols, cols), cols)
    early = step < pl.num_programs(0) // 2

    def add_sum(row, values):
        sums_ref[pl.ds(row, 1), :] += jnp.sum(values, axis=0, keepdims=True)

    def advance(at):
        attn = mm_rt(mine_ref[at, :], wo[:, mine_cols]) + mm_rt(other_ref[at, :], wo[:, other_cols])
        yield
        unit_one, scale_one = norm(x_ref[at, :].astype(F32) + attn + vec_ref[0:1, :])
        middle = unit_one * vec_ref[1:2, :] + vec_ref[2:3, :]
        low = middle.astype(BF16)
        mlow_ref[at, :] = low
        total = middle + vec_ref[3:4, :]

        @pl.when(step == 0)
        def _():
            for copy in copies[n_wo:]:
                copy.wait()

        yield
        for k in range(chunks):
            place = slice(k * units, (k + 1) * units)
            upper = mm(low, ww[k, :, :units]) + upb_ref[:, place]
            active, rise = gelu_parts(upper)
            active = active.astype(BF16)
            act_ref[at, place] = active
            slope[at, place] = rise.astype(BF16)
            total = total + mm_rt(active, ww[k, :, units:])
            yield
        unit_two, scale_two = norm(total)
        gain_two = vec_ref[4:5, :]
        layer[at, :] = (unit_two * gain_two + vec_ref[5:6, :]).astype(BF16)
        cot = jnp.where(early, cot_a[at, :], cot_b[at, :]).astype(F32)
        grad_two = norm_back(cot, unit_two, scale_two, gain_two)
        add_sum(4, cot * unit_two)
        add_sum(5, cot)
        add_sum(3, grad_two)
        low = grad_two.astype(BF16)
        gb_ref[at, :] = low
        total = grad_two
        yield
        for k in range(chunks):
            place = slice(k * units, (k + 1) * units)
            grad_upper = mm(low, ww[k, :, units:]) * slope[at, place].astype(F32)
            add_sum(8 + (k ^ place_ref[1]), grad_upper)
            grad_low = grad_upper.astype(BF16)
            gul_ref[at, place] = grad_low
            total = total + mm_rt(grad_low, ww[k, :, :units])
            yield
        add_sum(1, total * unit_one)
        add_sum(2, total)
        grad_one = norm_back(total, unit_one, scale_one, vec_ref[1:2, :])
        add_sum(0, grad_one)
        gone_ref[at, :] = grad_one
        grad_attn = grad_one.astype(BF16)
        ga_ref[at, :] = grad_attn
        yield
        gm_mine[at, :] = mm(grad_attn, wo[:, mine_cols]).astype(BF16)
        gm_other[at, :] = mm(grad_attn, wo[:, other_cols]).astype(BF16)
        yield

    part = x_ref.shape[0] // 1
    for _ in zip(*[advance(slice(part * k, part * (k + 1))) for k in range(1)]):
        pass

    @pl.when(early)
    def _():
        layer_a[...] = layer[...]

    @pl.when(jnp.logical_not(early))
    def _():
        layer_b[...] = layer[...]


def dense(place, w_pieces, x, mine, other, cot_a, cot_b, vec, upb, tile):
    count, width = x.shape
    cols = other.shape[1]
    units = w_pieces[-1].shape[-1] // 2
    chunks = upb.shape[1] // units
    steps = count // tile
    half = steps // 2
    n_copies = 2 if len(w_pieces) == 2 else 2 * w_pieces[0].shape[0] + 2 * (len(w_pieces) - 2)
    rows = lambda n: pl.BlockSpec((tile, n), lambda i, p: (i, 0))
    fixed = lambda a, b: pl.BlockSpec((a, b), lambda i, p: (0, 0))
    full = chunks * units
    shapes = [
        ((count // 2, width), BF16), ((count // 2, width), BF16),
        ((count, cols), BF16), ((count, cols), BF16), ((count, full), BF16),
        ((count, width), BF16), ((count, width), BF16), ((count, full), BF16), ((count, width), BF16),
        ((count, width), F32), ((16, width), F32),
    ]
    flops = 8 * count * width * full + 4 * count * width * 2 * cols
    return pl.pallas_call(
        functools.partial(dense_kernel, n_w=len(w_pieces), chunks=chunks),
        grid_spec=pltpu.PrefetchScalarGridSpec(
            num_scalar_prefetch=1,
            grid=(count // tile,),
            in_specs=[ANY] * len(w_pieces)
            + [rows(width), rows(cols), rows(cols)]
            + [
                pl.BlockSpec((tile, width), lambda i, p: (jnp.minimum(i, half - 1), 0)),
                pl.BlockSpec((tile, width), lambda i, p: (jnp.maximum(i - half, 0), 0)),
                fixed(8, width),
                fixed(1, full),
            ],
            out_specs=[
                pl.BlockSpec((tile, width), lambda i, p: (jnp.minimum(i, half - 1), 0)),
                pl.BlockSpec((tile, width), lambda i, p: (jnp.maximum(i - half, 0), 0)),
                rows(cols), rows(cols), rows(full), rows(width), rows(width), rows(full),
                rows(width), rows(width), fixed(16, width),
            ],
            scratch_shapes=[
                pltpu.VMEM((width, 2 * cols), BF16),
                pltpu.VMEM((chunks, width, 2 * units), BF16),
                pltpu.VMEM((tile, full), BF16),
                pltpu.VMEM((tile, width), BF16),
                pltpu.SemaphoreType.DMA((n_copies,)),
            ],
        ),
        out_shape=[jax.ShapeDtypeStruct(*s) for s in shapes],
        compiler_params=pltpu.CompilerParams(vmem_limit_bytes=27 << 20),
        cost_estimate=COST,
        name="dense",
    )(place, *w_pieces, x, mine, other, cot_a, cot_b, vec, upb)


def away_of(second):
    return [0, jnp.where(second, 1, 2), jnp.where(second, 2, 1), 3]


def grad_kernel(place_ref, *refs, n, steps, drows, first):
    left_ref, right_ref, refs = refs[0], refs[1], refs[2:]
    extra, (keep_ref, send_ref, theirs_ref, left_t, acc) = refs[: n - 2], refs[n - 2 :]
    core, chip = place_ref[0] % 2, place_ref[0] // 2
    step = pl.program_id(0)

    @pl.when(step == 0)
    def _():
        left_t[...] = left_ref[...].T

    @pl.when(step >= steps)
    def _():
        acc[...] = mm(left_t[...], right_ref[...])

    if extra:

        @pl.when(step < steps)
        def _():
            cols = extra[1].shape[1]
            mine_cols = pl.ds(pl.multiple_of(core * cols, cols), cols)
            other_cols = pl.ds(pl.multiple_of((1 - core) * cols, cols), cols)
            acc[:, mine_cols] = mm_lt(extra[0][...], extra[1][...])
            acc[:, other_cols] = mm_lt(extra[0][...], extra[2][...])

    for k, away in enumerate(away_of(step >= first)):
        base = 2 * (chip ^ away)
        ours = acc[pl.ds(pl.multiple_of((base + core) * drows, drows), drows), :]
        if k < 2:
            keep_ref[0, k] = ours
        else:
            send_ref[0, k - 2] = ours.astype(BF16)
        theirs_ref[0, k] = acc[pl.ds(pl.multiple_of((base + 1 - core) * drows, drows), drows), :].astype(BF16)


def weight_grad(place, left, right, extra, drows, first):
    count, width = left.shape
    tile = width
    steps = 1 if extra else 0
    chunks = right.shape[1] // tile + steps
    whole = lambda a, b: pl.BlockSpec((a, b), lambda i, p: (0, 0))
    shapes = [((chunks, 2, drows, tile), F32), ((chunks, 2, drows, tile), BF16), ((chunks, 4, drows, tile), BF16)]
    return pl.pallas_call(
        functools.partial(grad_kernel, n=2 + len(extra), steps=steps, drows=drows, first=first),
        grid_spec=pltpu.PrefetchScalarGridSpec(
            num_scalar_prefetch=1,
            grid=(chunks,),
            in_specs=[
                whole(count, width),
                pl.BlockSpec((count, tile), lambda i, p: (0, jnp.maximum(i - steps, 0))),
            ]
            + [whole(count, e.shape[1]) for e in extra],
            out_specs=[pl.BlockSpec((1,) + shape[1:], lambda i, p: (i, 0, 0, 0)) for shape, _ in shapes],
            scratch_shapes=[pltpu.VMEM((width, count), BF16), pltpu.VMEM((width, tile), F32)],
        ),
        out_shape=[jax.ShapeDtypeStruct(*shape) for shape in shapes],
        compiler_params=pltpu.CompilerParams(vmem_limit_bytes=15 << 20),
        cost_estimate=COST,
        name="weight_grad",
    )(place, left, right, *extra)


def xor_order(parts, index):
    parts = list(parts)
    bit = 1
    while bit < len(parts):
        odd = (index // bit) % 2 == 1
        parts = [jnp.where(odd, parts[k ^ bit], parts[k]) for k in range(len(parts))]
        bit *= 2
    return parts


def per_device(
    tokens,
    segments,
    pairing,
    qkv_weight,
    qv_bias,
    out_weight,
    out_bias,
    first_gain,
    first_shift,
    up_weight,
    up_bias,
    down_weight,
    down_bias,
    second_gain,
    second_shift,
    cotangent,
):
    width = tokens.shape[2]
    rows = tokens.shape[1]
    lheads, blocks = pairing.shape
    hs = qv_bias.shape[1] // 2
    lanes = 2 * hs
    units = up_weight.shape[1]
    ndp, nt = lax.axis_size("dp"), lax.axis_size("tensor")
    drows = width // ndp
    chips = ndp // 2
    dp, tensor = lax.axis_index("dp"), lax.axis_index("tensor")
    core, chip, half, low = dp % 2, dp // 2, tensor // 2, tensor % 2
    slot_mask = 2 * core + low
    heads = 2 * lheads
    cols = heads * hs
    aligned = drows % 8 == 0
    place = jnp.stack([dp, tensor]).astype(jnp.int32)
    order = [0, 1, 3, 4, 2, 5]

    core_pairs = [(i, i ^ 1) for i in range(ndp)]

    def core_swap(x):
        return lax.ppermute(x, "dp", core_pairs)

    def z_step(x, k):
        return lax.ppermute(x, "tensor", [(i, i ^ k) for i in range(nt)])

    def chip_step(x, k):
        return lax.ppermute(x, "dp", [(i, i ^ (2 * k)) for i in range(ndp)])

    def column(k, flip, back):
        steps = []
        for p in range(chips):
            for c in range(2):
                for a in range(2):
                    for b in range(2):
                        home = (2 * p + c) * nt + 2 * a + b
                        away = (2 * p + (a ^ flip)) * nt + 2 * c + (b ^ k)
                        steps.append((away, home) if back else (home, away))
        return steps

    def of_sequence(x, k):
        return lax.dynamic_index_in_dim(x, low ^ k, 0, keepdims=False)

    def to_sequence(part, k):
        return lax.ppermute(part, BOTH, column(k, 0, False))

    def at_home(first, second):
        return jnp.stack([jnp.where(low == 0, first, second), jnp.where(low == 0, second, first)])

    def z_all(x):
        return [x] + [z_step(x, k) for k in range(1, nt)]

    def chip_all(x):
        return [x] + [chip_step(x, k) for k in range(1, chips)]

    gate = lambda *trees: lax.optimization_barrier(trees)

    qkv_local = qkv_weight.reshape(drows, lheads, 3, hs).transpose(0, 2, 1, 3)
    qkv_local = jnp.concatenate(
        [
            qkv_local[:, :, :2].reshape(drows, 3 * lanes),
            qkv_local[:, :, 2].reshape(drows, 3 * hs),
            out_weight.reshape(lheads * hs, drows).T,
        ],
        axis=1,
    )
    small = jnp.concatenate([pairing.astype(BF16).reshape(-1), qv_bias.reshape(-1), up_bias])
    n_pair, n_qv = lheads * blocks, lheads * lanes
    extra_rows = 8
    small = jnp.pad(small, (0, extra_rows * qkv_local.shape[1] - small.shape[0]))
    first_z = z_all(jnp.concatenate([qkv_local, small.reshape(extra_rows, -1)]))
    segs = jnp.where(half == core, segments, core_swap(segments))
    ff_local = jnp.concatenate([up_weight, down_weight.T], axis=1)
    ff_local, first_z = gate(ff_local, first_z)
    ff_one = z_step(ff_local, 1)

    abs_z = xor_order([part[:drows] for part in first_z], tensor)
    qkv_cols = 3 * lheads * hs

    def regroup(first, second):
        left, right = first[:, 3 * lanes : qkv_cols], second[:, 3 * lanes : qkv_cols]
        both = [part[:, hs * k : hs * (k + 1)] for k in range(3) for part in (left, right)]
        return jnp.stack([first[:, : 3 * lanes], second[:, : 3 * lanes], jnp.concatenate(both, axis=1)])

    def with_out(first, second):
        left, right = first[:, qkv_cols:], second[:, qkv_cols:]
        out = jnp.concatenate([left[:, :lanes], right[:, :lanes], left[:, lanes:], right[:, lanes:]], axis=1)
        return jnp.concatenate([regroup(first, second), out[None]])

    zero_heads, one_heads = with_out(abs_z[0], abs_z[1]), with_out(abs_z[2], abs_z[3])
    keep = jnp.where(core == 0, zero_heads, one_heads)
    got = core_swap(jnp.where(core == 0, one_heads, zero_heads))
    chip_rows = jnp.where(
        core == 0, jnp.concatenate([keep, got], axis=1), jnp.concatenate([got, keep], axis=1)
    )
    ff_pair = jnp.stack([ff_local, ff_one])
    chip_rows, ff_pair = gate(chip_rows, ff_pair)
    qkv_pieces = chip_all(chip_rows)
    ff_middle = lax.ppermute(ff_pair, "tensor", [(1, 2), (2, 1)])

    tokens, ff_middle = gate(tokens, ff_middle)
    ff_end = lax.ppermute(ff_middle, "tensor", [(1, 0), (2, 3)])
    moved = [to_sequence(of_sequence(tokens, k), k) for k in range(2)]
    inner = (tensor == 1) | (tensor == 2)
    ff_other = jnp.where(inner, ff_middle[::-1], ff_end)
    qkv_pieces, ff_pair, ff_other, moved[0] = gate(qkv_pieces, ff_pair, ff_other, moved[0])
    out_mine = jnp.stack([piece[3] for piece in qkv_pieces])
    if aligned:
        firsts = [chip_step(ff_pair, 1), chip_step(ff_other, 2)]
        twos = [jnp.stack([ff_pair, firsts[0]]), jnp.stack([ff_other, firsts[1]])]
        cots = [of_sequence(cotangent, k) for k in range(2)]
        twos, moved, cots = gate(twos, moved, cots)
        fours = [chip_step(twos[0], 2), chip_step(twos[1], 1)]
        x_mine = jnp.concatenate(moved)
        x_other = core_swap(x_mine)
        twos_swapped = [core_swap(two) for two in twos]
        cots, x_mine, x_other, twos_swapped = gate(cots, x_mine, x_other, twos_swapped)
        cot_a, cot_b = [to_sequence(part, k) for k, part in enumerate(cots)]
    else:
        x_mine = jnp.concatenate(moved)
        x_other = core_swap(x_mine)
        cot_a, cot_b = [to_sequence(of_sequence(cotangent, k), k) for k in range(2)]
        out_other = core_swap(out_mine)
        ff_own = chip_all(jnp.concatenate([ff_pair, ff_other]))
        ff_all = [part for piece in ff_own for part in (piece, core_swap(piece))]
        qkv_pieces = [jnp.concatenate(xor_order(qkv_pieces, chip), axis=1)]
        out_both = [jnp.concatenate(xor_order(list(o), chip)) for o in (out_mine, out_other)]
        dense_pieces = [
            jnp.concatenate(
                [jnp.where(core == 0, out_both[0], out_both[1]), jnp.where(core == 0, out_both[1], out_both[0])],
                axis=1,
            ),
            jnp.concatenate(xor_order(ff_all, dp), axis=1),
        ]

    small_rel = [part[drows:].reshape(-1) for part in first_z]
    small = jnp.stack(xor_order(small_rel, tensor))
    all_pairs = small[:, :n_pair].astype(jnp.int32).reshape(2, heads, blocks)
    my_pairs = jnp.where(core == 0, all_pairs[0], all_pairs[1])
    pair_slots = jnp.stack(xor_order([my_pairs[:, k] for k in range(blocks)], slot_mask), axis=1) ^ slot_mask
    pair_slots = jnp.stack([pair_slots[h] for h in order])
    all_qvb = small[:, n_pair : n_pair + n_qv].astype(F32).reshape(2, heads, lanes)
    my_qvb = jnp.where(core == 0, all_qvb[0], all_qvb[1])
    my_qvb = jnp.stack([my_qvb[h] for h in order])
    up_bias_rel = jnp.concatenate([s[n_pair + n_qv :][:units] for s in small_rel]).astype(F32)
    groups = heads // 2
    bias = jnp.concatenate(
        [
            my_qvb[:, :hs].reshape(groups, lanes),
            jnp.zeros((groups, lanes), F32),
            my_qvb[:, hs:].reshape(groups, lanes),
        ],
        axis=1,
    ).reshape(groups, 1, 3 * lanes)

    seg_rows = jnp.where(low == 0, segs[0], segs[1]).reshape(blocks, rows)
    seg_row = jnp.concatenate(xor_order([seg_rows[k] for k in range(blocks)], slot_mask))
    seg_col = seg_row.reshape(blocks * rows, 1)
    seg_row = seg_row.reshape(1, blocks * rows)

    x_parts = [x_mine, x_other]
    q, k, v, mixed, mixed_other, lse, w_all = attend(pair_slots, place, x_parts, qkv_pieces, bias, seg_row, seg_col, hs)
    if aligned:
        q, k, v, mixed, mixed_other, lse, w_all, fours, cot_a, cot_b = gate(
            q, k, v, mixed, mixed_other, lse, w_all, fours, cot_a, cot_b
        )
        out_mine, mixed_other = gate(out_mine, mixed_other)
        out_other = core_swap(out_mine)
        dense_pieces = [out_mine, out_other] + twos + fours + twos_swapped + [core_swap(four) for four in fours]
    other = core_swap(mixed_other)

    blank = jnp.zeros((width,), BF16)
    vec = jnp.stack(
        [out_bias, first_gain, first_shift, down_bias, second_gain, second_shift, blank, blank]
    ).astype(F32)
    (
        layer_a, layer_b, gm_mine, gm_other, active, middle_low, grad_branch, grad_upper, grad_attn, grad_one, sums,
    ) = dense(
        place, dense_pieces, x_mine, mixed, other, cot_a, cot_b, vec, up_bias_rel.reshape(1, nt * units), 256
    )
    gm_got = core_swap(gm_other)
    home_0 = lax.ppermute(layer_a, BOTH, column(0, 0, True))

    def total_of(parts):
        total = parts[0].astype(F32)
        for part in parts[1:]:
            total = total + part.astype(F32)
        return total

    class Plane:
        def __init__(self, first, keep, send, got=None):
            self.first, self.got = first, got
            self.keep = self.split(keep)
            self.send = send if isinstance(send, list) else self.split(send)

        def split(self, x):
            return [x[: self.first], x[self.first :]]

        def first_sends(self):
            if self.got is None:
                return self.send
            got = self.split(self.got)
            self.keep = [[keep, g[:, :2]] for keep, g in zip(self.keep, got)]
            return [total_of([send, g[:, 2:]]).astype(BF16) for send, g in zip(self.send, got)]

        def first_moves(self, sends):
            return [chip_step(sends[0], 1), chip_step(sends[1], 2)]

        def second_sends(self, moves):
            keep = [k if isinstance(k, list) else [k] for k in self.keep]
            own = [total_of([part[:, 0] for part in k] + [m[:, 0]]) for k, m in zip(keep, moves)]
            sends = [total_of([part[:, 1] for part in k] + [m[:, 1]]).astype(BF16) for k, m in zip(keep, moves)]
            return own, sends

        def second_moves(self, sends):
            return [chip_step(sends[0], 2), chip_step(sends[1], 1)]

        def sums(self, own, moves):
            return [total_of([o, m]) for o, m in zip(own, moves)]

    class SlowPlane(Plane):
        def __init__(self, first, keep, send, got=None):
            self.first, self.view = first, keep if got is None else keep + got.astype(F32)

        def first_sends(self):
            return []

        def first_moves(self, sends):
            return []

        def second_sends(self, moves):
            return [], []

        def second_moves(self, sends):
            return []

        def sums(self, own, moves):
            pick = lambda step: lax.dynamic_index_in_dim(self.view, chip ^ step, 0, keepdims=False)
            total = total_of([pick(0)] + [chip_step(pick(step).astype(BF16), step) for step in range(1, chips)])
            return self.split(total.transpose(1, 0, 2))

    fast = chips == 4 and aligned

    def grads_of(left, right, extra, first):
        if fast:
            return weight_grad(place, left, right, extra, drows, first)
        grads = mm_lt(left, right)
        if extra:
            near, far = mm_lt(extra[0], extra[1]), mm_lt(extra[0], extra[2])
            head = [jnp.where(core == 0, near, far), jnp.where(core == 0, far, near)]
            grads = jnp.concatenate(head + [grads], axis=1)
        view = grads.reshape(chips, 2, drows, grads.shape[1] // width, width)
        ours = lax.dynamic_index_in_dim(view, core, 1, keepdims=False)
        theirs = lax.dynamic_index_in_dim(view, 1 - core, 1, keepdims=False).astype(BF16)
        return ours, theirs, theirs

    plane_of = Plane if fast else SlowPlane
    down_keep, down_send, down_theirs = grads_of(grad_branch, active, [], 2)
    down_got = core_swap(down_theirs)
    middle_low, down_keep, down_send, down_theirs, gm_got = gate(
        middle_low, down_keep, down_send, down_theirs, gm_got
    )
    up_keep, up_send, up_theirs = grads_of(middle_low, grad_upper, [grad_attn, mixed, other], 3)
    up_keep, up_send, up_theirs, home_0 = gate(up_keep, up_send, up_theirs, home_0)
    up_got = core_swap(up_theirs)

    down = plane_of(2, down_keep, down_send, down_got)
    d_sends = down.first_sends()
    pairs_0, gm_got, d_sends, layer_b = gate(pair_slots, gm_got, d_sends, layer_b)
    d_moves = down.first_moves(d_sends)
    home_1 = lax.ppermute(layer_b, BOTH, column(1, 0, True))
    packed_0, sums_0 = attend_back(pairs_0, 0, q, k, v, gm_mine, gm_got, seg_row, seg_col, lse, hs)
    packed_0, sums_0, d_moves, up_got, home_1 = gate(packed_0, sums_0, d_moves, up_got, home_1)
    layer_out = at_home(home_0, home_1)
    d_own, d_sends = down.second_sends(d_moves)
    up = plane_of(3, up_keep, up_send, up_got)
    u_sends = up.first_sends()
    pairs_1, d_own, d_sends, u_sends = gate(pair_slots, d_own, d_sends, u_sends)
    d_moves = down.second_moves(d_sends)
    u_moves = up.first_moves(u_sends)
    packed_1, sums_1 = attend_back(pairs_1, 1, q, k, v, gm_mine, gm_got, seg_row, seg_col, lse, hs)
    packed_1, sums_1, d_moves = gate(packed_1, sums_1, d_moves)
    d_first, d_second = down.sums(d_own, d_moves)
    d_second = d_second.astype(BF16)
    pair_slots, packed_1, d_first, d_second = gate(pair_slots, packed_1, d_first, d_second)
    d_second = z_step(d_second, 2)
    packed_2, sums_2 = attend_back(pair_slots, 2, q, k, v, gm_mine, gm_got, seg_row, seg_col, lse, hs)
    packed_2, sums_2, u_moves, d_second = gate(packed_2, sums_2, u_moves, d_second)
    d_keep = total_of([d_first[0], d_second[0]])
    d_give = total_of([d_first[1], d_second[1]]).astype(BF16)
    u_own, u_sends = up.second_sends(u_moves)

    head_sums = jnp.concatenate([part[row] for row in range(2) for part in (sums_0, sums_1, sums_2)])[None]
    blank = jnp.zeros_like(head_sums)
    sums = jnp.concatenate(
        [
            sums[:12],
            jnp.where(core == 0, head_sums, blank),
            jnp.where(core == 0, blank, head_sums),
            jnp.zeros((2, width), F32),
        ]
    )
    packed_2, d_keep, d_give, u_own, u_sends, sums = gate(packed_2, d_keep, d_give, u_own, u_sends, sums)
    packed = [packed_0, packed_1, packed_2]
    d_give = z_step(d_give, 1)
    sums_got = z_step(sums, 1)
    u_moves = up.second_moves(u_sends)
    in_mine, in_other = in_grad(packed, w_all, grad_one)
    in_mine, in_other, sums_got, packed, d_give, u_moves = gate(
        in_mine, in_other, sums_got, packed, d_give, u_moves
    )
    in_got = core_swap(in_other)
    down_grad = (d_keep + d_give.astype(F32)).T
    sums = sums + sums_got
    u_first, u_second = up.sums(u_own, u_moves)
    out_near = jnp.where(half == 0, u_first[0, :, :cols], u_first[0, :, cols:])
    out_far = jnp.where(half == 0, u_first[0, :, cols:], u_first[0, :, :cols])
    u_first = u_first[1:]
    u_second = jnp.concatenate([u_second[0], u_second[1], out_far], axis=1).astype(BF16)
    packed, sums, u_first, u_second, out_near = gate(packed, sums, u_first, u_second, out_near)
    u_second = z_step(u_second, 2)
    sums_got = z_step(sums, 2)
    if fast:
        qkv_keep, *qkv_send = qkv_grads(place, x_parts, packed, 2 * drows)
    else:
        parts = [mm_lt(jnp.concatenate(x_parts), packed[g]).reshape(chips, 2 * drows, 3 * lanes) for g in (0, 2, 1)]
        qkv_keep = qkv_send = jnp.stack(parts, axis=2)
    qkv_keep, qkv_send, packed, in_got, sums_got, u_second = gate(
        qkv_keep, qkv_send, packed, in_got, sums_got, u_second
    )
    sums = sums + sums_got
    qkv = plane_of(2, qkv_keep, qkv_send)
    a_sends = qkv.first_sends()
    u_keep, u_give = [total_of([u_first[j], u_second[:, units * j : units * (j + 1)]]) for j in range(2)]
    out_near = total_of([out_near, u_second[:, 2 * units :]])

    def out_unit(wanted_low):
        parts = [
            jnp.concatenate(
                [out_near[:, lanes * w : lanes * (w + 1)], out_near[:, 2 * lanes + hs * w : 2 * lanes + hs * (w + 1)]],
                axis=1,
            )
            for w in range(2)
        ]
        return jnp.where(wanted_low == 0, parts[0], parts[1])

    u_give = jnp.concatenate([u_give, out_unit(1 - low)], axis=1).astype(BF16)
    out_near = out_unit(low)
    a_moves = qkv.second_moves(a_sends)
    in_low = [total_of([part[rows * k : rows * (k + 1)] for part in (in_mine, in_got)]).astype(BF16) for k in range(2)]
    in_low, a_sends, sums, u_keep, u_give, out_near = gate(in_low, a_sends, sums, u_keep, u_give, out_near)
    homes = [lax.ppermute(part, BOTH, column(k, 0, True)) for k, part in enumerate(in_low)]
    a_moves = qkv.first_moves(a_sends)
    u_give = z_step(u_give, 1)
    a_own, a_sends = qkv.second_sends(a_moves)
    a_moves = qkv.second_moves(a_sends)
    up_grad = total_of([u_keep, u_give[:, :units]])
    out_grad = total_of([out_near, u_give[:, units:]]).T.reshape(lheads, hs, drows)
    homes, a_moves, sums = gate(homes, a_moves, sums)
    sums = sums + core_swap(sums)
    for bit in range(chips.bit_length() - 1):
        sums = sums + chip_step(sums, 1 << bit)
    outb_grad, gain_one_grad, shift_one_grad, downb_grad, gain_two_grad, shift_two_grad = [
        sums[row] for row in range(6)
    ]
    upb_grad = lax.dynamic_index_in_dim(sums, 8 + tensor, 0, keepdims=False)
    head_row = jnp.where(half == 0, sums[12], sums[13]).reshape(2, 6, hs)
    qvb_grad = jnp.where(low == 0, head_row[:, [0, 1, 4]], head_row[:, [2, 3, 5]])
    qvb_grad = jnp.concatenate([qvb_grad[0], qvb_grad[1]], axis=1)

    input_grad = at_home(*homes)
    sum_a, sum_b = qkv.sums(a_own, a_moves)
    sum_0, sum_2, sum_1 = [part.reshape(2, drows, 3 * lanes) for part in (sum_a[0], sum_a[1], sum_b[0])]
    sum_01 = [sum_0, sum_1]

    def share(c, u):
        third = [sum_2[c][:, lanes * k + hs * u : lanes * k + hs * (u + 1)] for k in range(3)]
        return jnp.concatenate([sum_01[u][c]] + third, axis=1)

    shares = [[share(c, u).astype(BF16) for u in range(2)] for c in range(2)]
    qkv_grad = jnp.zeros((drows, 3 * lheads * hs), F32)
    for flip in range(2):
        for step in range(2):
            by_core = [jnp.where((low ^ step) == 0, shares[c][0], shares[c][1]) for c in range(2)]
            sent = jnp.where((half ^ flip) == 0, by_core[0], by_core[1])
            qkv_grad = qkv_grad + lax.ppermute(sent, BOTH, column(step, flip, False)).astype(F32)
    pairs_part = qkv_grad[:, : 3 * lanes].reshape(drows, 3, 2, hs)
    third_part = qkv_grad[:, 3 * lanes :].reshape(drows, 3, 1, hs)
    qkv_grad = jnp.concatenate([pairs_part, third_part], axis=2).transpose(0, 2, 1, 3)
    qkv_grad = qkv_grad.reshape(drows, lheads, 3 * hs)
    return (
        layer_out,
        input_grad,
        qkv_grad,
        qvb_grad,
        out_grad,
        outb_grad,
        gain_one_grad,
        shift_one_grad,
        up_grad,
        upb_grad,
        down_grad,
        downb_grad,
        gain_two_grad,
        shift_two_grad,
    )


def solution(mesh):
    return jax.shard_map(
        per_device,
        mesh=mesh,
        in_specs=(
            P("dp", "tensor", None),
            P("dp", None),
            P("tensor", None),
            P("dp", "tensor", None),
            P("tensor", None),
            P("tensor", None, "dp"),
            P(),
            P(),
            P(),
            P("dp", "tensor"),
            P("tensor"),
            P("tensor", "dp"),
            P(),
            P(),
            P(),
            P("dp", "tensor", None),
        ),
        out_specs=(
            P("dp", "tensor", None),
            P("dp", "tensor", None),
            P("dp", "tensor", None),
            P("tensor", None),
            P("tensor", None, "dp"),
            P(),
            P(),
            P(),
            P("dp", "tensor"),
            P("tensor"),
            P("tensor", "dp"),
            P(),
            P(),
            P(),
        ),
        check_vma=False,
    )
```

```python
import functools

import jax
import jax.numpy as jnp
from jax import lax
from jax.experimental import pallas as pl
from jax.experimental.pallas import tpu as pltpu
from jax.sharding import PartitionSpec as P

EPS = 1e-06
NEG = -1e30
BOTH = ("dp", "tensor")
F32 = jnp.float32
BF16 = jnp.bfloat16
ANY = pl.BlockSpec(memory_space=pl.ANY)
LIMIT = 58 << 20
COST = pl.CostEstimate(flops=10**9, bytes_accessed=1 << 16, transcendentals=0)


def mm(left, right):
    return lax.dot_general(left, right, (((1,), (0,)), ((), ())), preferred_element_type=F32)


def mm_rt(left, right):
    return lax.dot_general(left, right, (((1,), (1,)), ((), ())), preferred_element_type=F32)


def mm_lt(left, right):
    return lax.dot_general(left, right, (((0,), (0,)), ((), ())), preferred_element_type=F32)


def head_lanes(shape, head, dim, head_size):
    place = lax.broadcasted_iota(jnp.int32, shape, dim)
    return (place < head_size) if head == 0 else (place >= head_size)


def fetches(pieces, offsets, target, dim, sems, first):
    copies = []
    for k, (piece, offset) in enumerate(zip(pieces, offsets)):
        count = piece.shape[dim]
        where = pl.ds(offset if isinstance(offset, int) else pl.multiple_of(offset, count), count)
        index = (slice(None),) * dim + (where,)
        copies.append(pltpu.make_async_copy(piece, target.at[index], sems.at[first + k]))
    return copies


def piece_rows(place, step, rows, count):
    if count == 1:
        return [0]
    return [(place ^ (k * step)) * rows for k in range(count)]


def attend_kernel(pair_ref, place_ref, *refs, rows, hs, blocks, n_w):
    x_refs, refs = refs[:2], refs[2:]
    w_refs, refs = refs[:n_w], refs[n_w:]
    bias_ref, segq_ref, segk_ref, q_out, k_out, v_out, o_mine, o_other, lse_ref, w_all, x_all, sems = refs
    group, block = pl.program_id(0), pl.program_id(1)
    lanes2 = 2 * hs

    @pl.when((group == 0) & (block == 0))
    def _():
        chip = place_ref[0] // 2
        w_parts = [piece.at[: w_all.shape[0]] for piece in w_refs]
        copies = fetches(
            w_parts, piece_rows(chip, 1, w_refs[0].shape[1], n_w), w_all, 1, sems, 0
        ) + fetches(x_refs, [0, x_refs[0].shape[0]], x_all, 0, sems, n_w)
        for copy in copies:
            copy.start()
        for copy in copies:
            copy.wait()

    @pl.when(block == 0)
    def _():
        weight = w_all[group]
        for k in range(blocks):
            part = pl.ds(k * rows, rows)
            out = (mm(x_all[part, :], weight) + bias_ref[0]).astype(BF16)
            q_out[part, :] = out[:, :lanes2] * (hs**-0.5)
            k_out[part, :] = out[:, lanes2 : 2 * lanes2]
            v_out[part, :] = out[:, 2 * lanes2 :]

    own = pl.ds(pl.multiple_of(block * rows, rows), rows)
    q2 = q_out[own, :]
    own_raw = (q2.astype(F32) * k_out[own, :].astype(F32)).T
    own_values = v_out[own, :].astype(F32).T
    segq = segq_ref[...]
    total = jnp.zeros((2 * hs, rows), F32)
    for head in range(2):
        target = pair_ref[2 * group + head, block]
        there = pl.ds(pl.multiple_of(target * rows, rows), rows)
        keys, values = k_out[there, :], v_out[there, :]
        lanes = head_lanes(q2.shape, head, 1, hs)
        scores = mm_rt(keys, jnp.where(lanes, q2, jnp.zeros_like(q2)))
        scores = jnp.where(segk_ref[there, :] == segq, scores, NEG)
        raw = jnp.sum(own_raw[head * hs : (head + 1) * hs], axis=0, keepdims=True)
        raw = jnp.where(target != block, raw, NEG)
        peak = jnp.maximum(jnp.max(scores, axis=0, keepdims=True), raw)
        expo = jnp.exp(scores - peak)
        own_expo = jnp.exp(raw - peak)
        denom = jnp.sum(expo, axis=0, keepdims=True) + own_expo
        masked_values = jnp.where(lanes, values, jnp.zeros_like(values))
        part = mm_lt(masked_values, expo.astype(BF16))
        low = own_expo.astype(BF16).astype(F32)
        mine = head_lanes(part.shape, head, 0, hs)
        part = part + jnp.where(mine, own_values * low, 0.0)
        total = total + part * (1.0 / denom)
        lse_ref[0, head : head + 1, :] = peak + jnp.log(denom)
    mixed = total.T.astype(BF16)

    @pl.when(block < blocks // 2)
    def _():
        o_mine[pl.ds(pl.multiple_of(block * rows, rows), rows), :] = mixed

    @pl.when(block >= blocks // 2)
    def _():
        o_other[pl.ds(pl.multiple_of((block - blocks // 2) * rows, rows), rows), :] = mixed


def attend(pairs, place, x_parts, w_pieces, bias, segq, segk, hs):
    heads, blocks = pairs.shape
    width = x_parts[0].shape[1]
    seq, groups, lanes = 2 * x_parts[0].shape[0], heads // 2, 2 * hs
    rows = seq // blocks
    kept = jax.ShapeDtypeStruct((seq, groups * lanes), BF16)
    flops = 2 * seq * width * 3 * groups * lanes + 4 * heads * seq * rows * 2 * lanes
    return pl.pallas_call(
        functools.partial(attend_kernel, rows=rows, hs=hs, blocks=blocks, n_w=len(w_pieces)),
        grid_spec=pltpu.PrefetchScalarGridSpec(
            num_scalar_prefetch=2,
            grid=(groups, blocks),
            in_specs=[ANY] * (2 + len(w_pieces))
            + [
                pl.BlockSpec((1, 1, 3 * lanes), lambda g, i, p, q: (g, 0, 0)),
                pl.BlockSpec((1, rows), lambda g, i, p, q: (0, i)),
                pl.BlockSpec((seq, 1), lambda g, i, p, q: (0, 0)),
            ],
            out_specs=[pl.BlockSpec((seq, lanes), lambda g, i, p, q: (0, g))] * 3
            + [
                pl.BlockSpec((seq // 2, lanes), lambda g, i, p, q: (0, g)),
                pl.BlockSpec((seq // 2, lanes), lambda g, i, p, q: (0, g)),
                pl.BlockSpec((1, 8, rows), lambda g, i, p, q: (g, 0, i)),
                pl.BlockSpec((groups, width, 3 * lanes), lambda g, i, p, q: (0, 0, 0)),
            ],
            scratch_shapes=[
                pltpu.VMEM((seq, width), BF16),
                pltpu.SemaphoreType.DMA((2 + len(w_pieces),)),
            ],
        ),
        out_shape=[kept] * 3
        + [jax.ShapeDtypeStruct((seq // 2, groups * lanes), BF16)] * 2
        + [
            jax.ShapeDtypeStruct((groups, 8, seq), F32),
            jax.ShapeDtypeStruct((groups, width, 3 * lanes), BF16),
        ],
        compiler_params=pltpu.CompilerParams(vmem_limit_bytes=58 << 20),
        cost_estimate=COST,
        name="attend",
    )(pairs, place, *x_parts, *w_pieces, bias, segq, segk)


def attend_back_kernel(
    pair_ref, group_ref, q_ref, k_ref, v_ref, do_a, do_b, segq_ref, segk_ref, lse_ref,
    packed_ref, sums_ref, dq_all, dk_acc, dv_acc, *, rows, hs, blocks,
):
    block = pl.program_id(0)

    @pl.when(block == 0)
    def _():
        dk_acc[...] = jnp.zeros_like(dk_acc)
        dv_acc[...] = jnp.zeros_like(dv_acc)
        sums_ref[...] = jnp.zeros_like(sums_ref)

    own = pl.ds(pl.multiple_of(block * rows, rows), rows)
    q2, do2 = q_ref[...], jnp.where(block < blocks // 2, do_a[...], do_b[...])
    qt, dot = q2.astype(F32).T, do2.astype(F32).T
    own_keys, own_values = k_ref[own, :].astype(F32).T, v_ref[own, :].astype(F32).T
    own_raw, own_dp = qt * own_keys, dot * own_values
    segq = segq_ref[...]
    dq = jnp.zeros((2 * hs, rows), F32)
    own_ds, own_low = [], []
    for head in range(2):
        target = pair_ref[2 * group_ref[0] + head, block]
        there = pl.ds(pl.multiple_of(target * rows, rows), rows)
        keys, values = k_ref[there, :], v_ref[there, :]
        lanes = head_lanes(q2.shape, head, 1, hs)
        zero = jnp.zeros_like(q2)
        qm, dom = jnp.where(lanes, q2, zero), jnp.where(lanes, do2, zero)
        lse = lse_ref[0, head : head + 1, :]
        scores = mm_rt(keys, qm)
        probs = jnp.exp(jnp.where(segk_ref[there, :] == segq, scores - lse, NEG))
        raw = jnp.sum(own_raw[head * hs : (head + 1) * hs], axis=0, keepdims=True)
        self_prob = jnp.exp(jnp.where(target != block, raw - lse, NEG))
        self_dp = jnp.sum(own_dp[head * hs : (head + 1) * hs], axis=0, keepdims=True)
        dv_acc[there, :] += mm(probs.astype(BF16), dom)
        dprobs = mm_rt(values, dom)
        delta = jnp.sum(probs * dprobs, axis=0, keepdims=True) + self_prob * self_dp
        dscores = (probs * (dprobs - delta)).astype(BF16)
        dk_acc[there, :] += mm(dscores, qm)
        dq = dq + mm_lt(jnp.where(lanes, keys, jnp.zeros_like(keys)), dscores)
        own_ds.append((self_prob * (self_dp - delta)).astype(BF16).astype(F32))
        own_low.append(self_prob.astype(BF16).astype(F32))
    first = head_lanes(dq.shape, 0, 0, hs)
    ds_rows = jnp.where(first, own_ds[0], own_ds[1])
    low_rows = jnp.where(first, own_low[0], own_low[1])
    dq = ((dq + ds_rows * own_keys) * (hs**-0.5)).T
    dq_all[own, :] = dq.astype(BF16)
    sums_ref[0:1, :] += jnp.sum(dq, axis=0, keepdims=True)
    dk_acc[own, :] += (ds_rows * qt).T
    dv_acc[own, :] += (low_rows * dot).T

    @pl.when(block == blocks - 1)
    def _():
        dv = dv_acc[...]
        sums_ref[1:2, :] = jnp.sum(dv, axis=0, keepdims=True)
        packed_ref[...] = jnp.concatenate(
            [dq_all[...], dk_acc[...].astype(BF16), dv.astype(BF16)], axis=1
        )


def attend_back(pairs, group, q, k, v, grad_a, grad_b, segq, segk, lse, hs):
    heads, blocks = pairs.shape
    seq, lanes = q.shape[0], 2 * hs
    rows, half = seq // blocks, blocks // 2
    return pl.pallas_call(
        functools.partial(attend_back_kernel, rows=rows, hs=hs, blocks=blocks),
        grid_spec=pltpu.PrefetchScalarGridSpec(
            num_scalar_prefetch=2,
            grid=(blocks,),
            in_specs=[
                pl.BlockSpec((rows, lanes), lambda i, p, g: (i, g[0])),
                pl.BlockSpec((seq, lanes), lambda i, p, g: (0, g[0])),
                pl.BlockSpec((seq, lanes), lambda i, p, g: (0, g[0])),
                pl.BlockSpec((rows, lanes), lambda i, p, g: (jnp.minimum(i, half - 1), g[0])),
                pl.BlockSpec((rows, lanes), lambda i, p, g: (jnp.maximum(i - half, 0), g[0])),
                pl.BlockSpec((1, rows), lambda i, p, g: (0, i)),
                pl.BlockSpec((seq, 1), lambda i, p, g: (0, 0)),
                pl.BlockSpec((1, 8, rows), lambda i, p, g: (g[0], 0, i)),
            ],
            out_specs=[
                pl.BlockSpec((seq, 3 * lanes), lambda i, p, g: (0, 0)),
                pl.BlockSpec((8, lanes), lambda i, p, g: (0, 0)),
            ],
            scratch_shapes=[
                pltpu.VMEM((seq, lanes), BF16),
                pltpu.VMEM((seq, lanes), F32),
                pltpu.VMEM((seq, lanes), F32),
            ],
        ),
        out_shape=[
            jax.ShapeDtypeStruct((seq, 3 * lanes), BF16),
            jax.ShapeDtypeStruct((8, lanes), F32),
        ],
        compiler_params=pltpu.CompilerParams(vmem_limit_bytes=12 << 20),
        cost_estimate=COST,
        name="attend_back",
    )(pairs, jnp.full((1,), group, jnp.int32), q, k, v, grad_a, grad_b, segq, segk, lse)


def qkv_grad_kernel(place_ref, *refs):
    packed_refs, xa_ref, xb_ref, keep_ref, send_a, send_b, packed, acc, sems = refs[:3], *refs[3:]
    half = xa_ref.shape[0]
    chip = place_ref[0] // 2
    rows = keep_ref.shape[2]
    step = pl.program_id(0)
    copies = [
        pltpu.make_async_copy(packed_refs[g], packed.at[j], sems.at[j]) for j, g in enumerate((0, 2, 1))
    ]

    @pl.when(step == 0)
    def _():
        for copy in copies:
            copy.start()

    for j, copy in enumerate(copies):

        @pl.when(step == j)
        def _(copy=copy):
            copy.wait()

    acc[...] = mm_lt(xa_ref[...], packed[step, :half, :]) + mm_lt(xb_ref[...], packed[step, half:, :])
    for k, away in enumerate(away_of(step == 2)):
        ours = acc[pl.ds(pl.multiple_of((chip ^ away) * rows, rows), rows), :]
        if k < 2:
            keep_ref[0, k] = ours
        else:
            ours = ours.astype(BF16)

            @pl.when(step < 2)
            def _(ours=ours, k=k):
                send_a[0, k - 2] = ours

            @pl.when(step == 2)
            def _(ours=ours, k=k):
                send_b[0, k - 2] = ours


def qkv_grads(place, x_parts, packed, rows):
    half, width = x_parts[0].shape
    cols = packed[0].shape[1]
    whole = lambda a, b: pl.BlockSpec((a, b), lambda i, p: (0, 0))
    return pl.pallas_call(
        qkv_grad_kernel,
        grid_spec=pltpu.PrefetchScalarGridSpec(
            num_scalar_prefetch=1,
            grid=(3,),
            in_specs=[ANY] * 3 + [whole(half, width)] * 2,
            out_specs=[
                pl.BlockSpec((1, 2, rows, cols), lambda i, p: (i, 0, 0, 0)),
                pl.BlockSpec((1, 2, rows, cols), lambda i, p: (jnp.minimum(i, 1), 0, 0, 0)),
                pl.BlockSpec((1, 2, rows, cols), lambda i, p: (0, 0, 0, 0)),
            ],
            scratch_shapes=[
                pltpu.VMEM((3, 2 * half, cols), BF16),
                pltpu.VMEM((width, cols), F32),
                pltpu.SemaphoreType.DMA((3,)),
            ],
        ),
        out_shape=[
            jax.ShapeDtypeStruct((3, 2, rows, cols), F32),
            jax.ShapeDtypeStruct((2, 2, rows, cols), BF16),
            jax.ShapeDtypeStruct((1, 2, rows, cols), BF16),
        ],
        compiler_params=pltpu.CompilerParams(vmem_limit_bytes=18 << 20),
        cost_estimate=COST,
        name="qkv_grads",
    )(place, *packed, *x_parts)


def in_grad_kernel(*refs, n, half):
    packed, w_ref, extra, mine_ref, other_ref = refs[:n], refs[n], *refs[n + 1 :]
    step = pl.program_id(0)
    total = mm_rt(packed[0][...], w_ref[0])
    for g in range(1, n):
        total = total + mm_rt(packed[g][...], w_ref[g])

    @pl.when(step < half)
    def _():
        other_ref[...] = total.astype(BF16)

    @pl.when(step >= half)
    def _():
        mine_ref[...] = total + extra[...]


def in_grad(packed, weight, extra):
    seq, cols = packed[0].shape
    n, width = weight.shape[:2]
    half = 2
    tile = seq // (2 * half)
    late = lambda i: (jnp.maximum(i - half, 0), 0)
    return pl.pallas_call(
        functools.partial(in_grad_kernel, n=n, half=half),
        grid=(2 * half,),
        in_specs=[pl.BlockSpec((tile, cols), lambda i: ((i + half) % (2 * half), 0))] * n
        + [pl.BlockSpec((n, width, cols), lambda i: (0, 0, 0)), pl.BlockSpec((tile, width), late)],
        out_specs=[
            pl.BlockSpec((tile, width), late),
            pl.BlockSpec((tile, width), lambda i: (jnp.minimum(i, half - 1), 0)),
        ],
        out_shape=[
            jax.ShapeDtypeStruct((seq // 2, width), F32),
            jax.ShapeDtypeStruct((seq // 2, width), BF16),
        ],
        compiler_params=pltpu.CompilerParams(vmem_limit_bytes=58 << 20),
        cost_estimate=COST,
        name="in_grad",
    )(*packed, weight, extra)


def norm(values):
    centred = values - jnp.mean(values, axis=-1, keepdims=True)
    scale = lax.rsqrt(jnp.mean(centred * centred, axis=-1, keepdims=True) + EPS)
    return centred * scale, scale


def norm_back(grad, unit, scale, gain):
    q = grad * gain
    mean_q = jnp.mean(q, axis=-1, keepdims=True)
    mean_qn = jnp.mean(q * unit, axis=-1, keepdims=True)
    return scale * (q - mean_q - unit * mean_qn)


def gelu_parts(u):
    dense = jnp.exp(-0.5 * u * u) * 0.3989422804014327
    t = 1.0 / (1.0 + 0.2316419 * jnp.abs(u))
    poly = t * (
        0.319381530
        + t * (-0.356563782 + t * (1.781477937 + t * (-1.821255978 + t * 1.330274429)))
    )
    tail = dense * poly
    phi = jnp.where(u >= 0, 1.0 - tail, tail)
    return u * phi, phi + u * dense


def dense_copies(place, pieces, wo, ww, sems):
    copies = []

    def add(source, target):
        copies.append(pltpu.make_async_copy(source, target, sems.at[len(copies)]))

    if len(pieces) == 2:
        add(pieces[0], wo)
        add(pieces[1], ww)
        return copies
    core, chip = place % 2, place // 2
    chips, rows, cols = pieces[0].shape
    for side in range(2):
        lanes = pl.ds(pl.multiple_of((core ^ side) * cols, cols), cols)
        for k in range(chips):
            add(pieces[side].at[k], wo.at[pl.ds(pl.multiple_of((chip ^ k) * rows, rows), rows), lanes])
    half, rows = pieces[2].shape[1:3]
    for k, piece in enumerate(pieces[2:]):
        away = ((0, 1), (0, 2), (2, 3), (1, 3))[k % 4]
        for j in range(2):
            base = (place ^ (2 * away[j] + k // 4)) * rows
            add(piece.at[j], ww.at[pl.ds((k % 2) * half, half), pl.ds(pl.multiple_of(base, rows), rows), :])
    return copies


def dense_kernel(place_ref, *refs, n_w, chunks):
    w_refs, refs = refs[:n_w], refs[n_w:]
    (
        x_ref, mine_ref, other_ref, cot_a, cot_b, vec_ref, upb_ref,
        layer_a, layer_b, gm_mine, gm_other, act_ref, mlow_ref, gb_ref, gul_ref, ga_ref, gone_ref, sums_ref,
        wo, ww, slope, layer, sems,
    ) = refs
    step = pl.program_id(0)
    core = place_ref[0] % 2
    cols = mine_ref.shape[1]
    width = x_ref.shape[1]
    units = ww.shape[2] // 2
    copies = dense_copies(place_ref[0], w_refs, wo, ww, sems)
    n_wo = 1 if len(w_refs) == 2 else 2 * w_refs[0].shape[0]

    @pl.when(step == 0)
    def _():
        for copy in copies:
            copy.start()
        for copy in copies[:n_wo]:
            copy.wait()
        sums_ref[...] = jnp.zeros_like(sums_ref)

    mine_cols = pl.ds(pl.multiple_of(core * cols, cols), cols)
    other_cols = pl.ds(pl.multiple_of((1 - core) * cols, cols), cols)
    early = step < pl.num_programs(0) // 2

    def add_sum(row, values):
        sums_ref[pl.ds(row, 1), :] += jnp.sum(values, axis=0, keepdims=True)

    def advance(at):
        attn = mm_rt(mine_ref[at, :], wo[:, mine_cols]) + mm_rt(other_ref[at, :], wo[:, other_cols])
        yield
        unit_one, scale_one = norm(x_ref[at, :].astype(F32) + attn + vec_ref[0:1, :])
        middle = unit_one * vec_ref[1:2, :] + vec_ref[2:3, :]
        low = middle.astype(BF16)
        mlow_ref[at, :] = low
        total = middle + vec_ref[3:4, :]

        @pl.when(step == 0)
        def _():
            for copy in copies[n_wo:]:
                copy.wait()

        yield
        for k in range(chunks):
            place = slice(k * units, (k + 1) * units)
            upper = mm(low, ww[k, :, :units]) + upb_ref[:, place]
            active, rise = gelu_parts(upper)
            active = active.astype(BF16)
            act_ref[at, place] = active
            slope[at, place] = rise.astype(BF16)
            total = total + mm_rt(active, ww[k, :, units:])
            yield
        unit_two, scale_two = norm(total)
        gain_two = vec_ref[4:5, :]
        layer[at, :] = (unit_two * gain_two + vec_ref[5:6, :]).astype(BF16)
        cot = jnp.where(early, cot_a[at, :], cot_b[at, :]).astype(F32)
        grad_two = norm_back(cot, unit_two, scale_two, gain_two)
        add_sum(4, cot * unit_two)
        add_sum(5, cot)
        add_sum(3, grad_two)
        low = grad_two.astype(BF16)
        gb_ref[at, :] = low
        total = grad_two
        yield
        for k in range(chunks):
            place = slice(k * units, (k + 1) * units)
            grad_upper = mm(low, ww[k, :, units:]) * slope[at, place].astype(F32)
            add_sum(8 + (k ^ place_ref[1]), grad_upper)
            grad_low = grad_upper.astype(BF16)
            gul_ref[at, place] = grad_low
            total = total + mm_rt(grad_low, ww[k, :, :units])
            yield
        add_sum(1, total * unit_one)
        add_sum(2, total)
        grad_one = norm_back(total, unit_one, scale_one, vec_ref[1:2, :])
        add_sum(0, grad_one)
        gone_ref[at, :] = grad_one
        grad_attn = grad_one.astype(BF16)
        ga_ref[at, :] = grad_attn
        yield
        gm_mine[at, :] = mm(grad_attn, wo[:, mine_cols]).astype(BF16)
        gm_other[at, :] = mm(grad_attn, wo[:, other_cols]).astype(BF16)
        yield

    part = x_ref.shape[0] // 1
    for _ in zip(*[advance(slice(part * k, part * (k + 1))) for k in range(1)]):
        pass

    @pl.when(early)
    def _():
        layer_a[...] = layer[...]

    @pl.when(jnp.logical_not(early))
    def _():
        layer_b[...] = layer[...]


def dense(place, w_pieces, x, mine, other, cot_a, cot_b, vec, upb, tile):
    count, width = x.shape
    cols = other.shape[1]
    units = w_pieces[-1].shape[-1] // 2
    chunks = upb.shape[1] // units
    steps = count // tile
    half = steps // 2
    n_copies = 2 if len(w_pieces) == 2 else 2 * w_pieces[0].shape[0] + 2 * (len(w_pieces) - 2)
    rows = lambda n: pl.BlockSpec((tile, n), lambda i, p: (i, 0))
    fixed = lambda a, b: pl.BlockSpec((a, b), lambda i, p: (0, 0))
    full = chunks * units
    shapes = [
        ((count // 2, width), BF16), ((count // 2, width), BF16),
        ((count, cols), BF16), ((count, cols), BF16), ((count, full), BF16),
        ((count, width), BF16), ((count, width), BF16), ((count, full), BF16), ((count, width), BF16),
        ((count, width), F32), ((16, width), F32),
    ]
    flops = 8 * count * width * full + 4 * count * width * 2 * cols
    return pl.pallas_call(
        functools.partial(dense_kernel, n_w=len(w_pieces), chunks=chunks),
        grid_spec=pltpu.PrefetchScalarGridSpec(
            num_scalar_prefetch=1,
            grid=(count // tile,),
            in_specs=[ANY] * len(w_pieces)
            + [rows(width), rows(cols), rows(cols)]
            + [
                pl.BlockSpec((tile, width), lambda i, p: (jnp.minimum(i, half - 1), 0)),
                pl.BlockSpec((tile, width), lambda i, p: (jnp.maximum(i - half, 0), 0)),
                fixed(8, width),
                fixed(1, full),
            ],
            out_specs=[
                pl.BlockSpec((tile, width), lambda i, p: (jnp.minimum(i, half - 1), 0)),
                pl.BlockSpec((tile, width), lambda i, p: (jnp.maximum(i - half, 0), 0)),
                rows(cols), rows(cols), rows(full), rows(width), rows(width), rows(full),
                rows(width), rows(width), fixed(16, width),
            ],
            scratch_shapes=[
                pltpu.VMEM((width, 2 * cols), BF16),
                pltpu.VMEM((chunks, width, 2 * units), BF16),
                pltpu.VMEM((tile, full), BF16),
                pltpu.VMEM((tile, width), BF16),
                pltpu.SemaphoreType.DMA((n_copies,)),
            ],
        ),
        out_shape=[jax.ShapeDtypeStruct(*s) for s in shapes],
        compiler_params=pltpu.CompilerParams(vmem_limit_bytes=58 << 20),
        cost_estimate=COST,
        name="dense",
    )(place, *w_pieces, x, mine, other, cot_a, cot_b, vec, upb)


def away_of(second):
    return [0, jnp.where(second, 1, 2), jnp.where(second, 2, 1), 3]


def grad_kernel(place_ref, *refs, n, steps, drows, first):
    left_ref, right_ref, refs = refs[0], refs[1], refs[2:]
    extra, (keep_ref, send_ref, theirs_ref, left_t, acc) = refs[: n - 2], refs[n - 2 :]
    core, chip = place_ref[0] % 2, place_ref[0] // 2
    step = pl.program_id(0)

    @pl.when(step == 0)
    def _():
        left_t[...] = left_ref[...].T

    @pl.when(step >= steps)
    def _():
        acc[...] = mm(left_t[...], right_ref[...])

    if extra:

        @pl.when(step < steps)
        def _():
            cols = extra[1].shape[1]
            mine_cols = pl.ds(pl.multiple_of(core * cols, cols), cols)
            other_cols = pl.ds(pl.multiple_of((1 - core) * cols, cols), cols)
            acc[:, mine_cols] = mm_lt(extra[0][...], extra[1][...])
            acc[:, other_cols] = mm_lt(extra[0][...], extra[2][...])

    for k, away in enumerate(away_of(step >= first)):
        base = 2 * (chip ^ away)
        ours = acc[pl.ds(pl.multiple_of((base + core) * drows, drows), drows), :]
        if k < 2:
            keep_ref[0, k] = ours
        else:
            send_ref[0, k - 2] = ours.astype(BF16)
        theirs_ref[0, k] = acc[pl.ds(pl.multiple_of((base + 1 - core) * drows, drows), drows), :].astype(BF16)


def weight_grad(place, left, right, extra, drows, first):
    count, width = left.shape
    tile = width
    steps = 1 if extra else 0
    chunks = right.shape[1] // tile + steps
    whole = lambda a, b: pl.BlockSpec((a, b), lambda i, p: (0, 0))
    shapes = [((chunks, 2, drows, tile), F32), ((chunks, 2, drows, tile), BF16), ((chunks, 4, drows, tile), BF16)]
    return pl.pallas_call(
        functools.partial(grad_kernel, n=2 + len(extra), steps=steps, drows=drows, first=first),
        grid_spec=pltpu.PrefetchScalarGridSpec(
            num_scalar_prefetch=1,
            grid=(chunks,),
            in_specs=[
                whole(count, width),
                pl.BlockSpec((count, tile), lambda i, p: (0, jnp.maximum(i - steps, 0))),
            ]
            + [whole(count, e.shape[1]) for e in extra],
            out_specs=[pl.BlockSpec((1,) + shape[1:], lambda i, p: (i, 0, 0, 0)) for shape, _ in shapes],
            scratch_shapes=[pltpu.VMEM((width, count), BF16), pltpu.VMEM((width, tile), F32)],
        ),
        out_shape=[jax.ShapeDtypeStruct(*shape) for shape in shapes],
        compiler_params=pltpu.CompilerParams(vmem_limit_bytes=15 << 20),
        cost_estimate=COST,
        name="weight_grad",
    )(place, left, right, *extra)


def xor_order(parts, index):
    parts = list(parts)
    bit = 1
    while bit < len(parts):
        odd = (index // bit) % 2 == 1
        parts = [jnp.where(odd, parts[k ^ bit], parts[k]) for k in range(len(parts))]
        bit *= 2
    return parts


def per_device(
    tokens,
    segments,
    pairing,
    qkv_weight,
    qv_bias,
    out_weight,
    out_bias,
    first_gain,
    first_shift,
    up_weight,
    up_bias,
    down_weight,
    down_bias,
    second_gain,
    second_shift,
    cotangent,
):
    width = tokens.shape[2]
    rows = tokens.shape[1]
    lheads, blocks = pairing.shape
    hs = qv_bias.shape[1] // 2
    lanes = 2 * hs
    units = up_weight.shape[1]
    ndp, nt = lax.axis_size("dp"), lax.axis_size("tensor")
    drows = width // ndp
    chips = ndp // 2
    dp, tensor = lax.axis_index("dp"), lax.axis_index("tensor")
    core, chip, half, low = dp % 2, dp // 2, tensor // 2, tensor % 2
    slot_mask = 2 * core + low
    heads = 2 * lheads
    cols = heads * hs
    aligned = drows % 8 == 0
    place = jnp.stack([dp, tensor]).astype(jnp.int32)
    order = [0, 1, 3, 4, 2, 5]

    core_pairs = [(i, i ^ 1) for i in range(ndp)]

    def core_swap(x):
        return lax.ppermute(x, "dp", core_pairs)

    def z_step(x, k):
        return lax.ppermute(x, "tensor", [(i, i ^ k) for i in range(nt)])

    def chip_step(x, k):
        return lax.ppermute(x, "dp", [(i, i ^ (2 * k)) for i in range(ndp)])

    def column(k, flip, back):
        steps = []
        for p in range(chips):
            for c in range(2):
                for a in range(2):
                    for b in range(2):
                        home = (2 * p + c) * nt + 2 * a + b
                        away = (2 * p + (a ^ flip)) * nt + 2 * c + (b ^ k)
                        steps.append((away, home) if back else (home, away))
        return steps

    def of_sequence(x, k):
        return lax.dynamic_index_in_dim(x, low ^ k, 0, keepdims=False)

    def to_sequence(part, k):
        return lax.ppermute(part, BOTH, column(k, 0, False))

    def at_home(first, second):
        return jnp.stack([jnp.where(low == 0, first, second), jnp.where(low == 0, second, first)])

    def z_all(x):
        return [x] + [z_step(x, k) for k in range(1, nt)]

    def chip_all(x):
        return [x] + [chip_step(x, k) for k in range(1, chips)]

    gate = lambda *trees: lax.optimization_barrier(trees)

    qkv_local = qkv_weight.reshape(drows, lheads, 3, hs).transpose(0, 2, 1, 3)
    qkv_local = jnp.concatenate(
        [
            qkv_local[:, :, :2].reshape(drows, 3 * lanes),
            qkv_local[:, :, 2].reshape(drows, 3 * hs),
            out_weight.reshape(lheads * hs, drows).T,
        ],
        axis=1,
    )
    small = jnp.concatenate([pairing.astype(BF16).reshape(-1), qv_bias.reshape(-1), up_bias])
    n_pair, n_qv = lheads * blocks, lheads * lanes
    extra_rows = 8
    small = jnp.pad(small, (0, extra_rows * qkv_local.shape[1] - small.shape[0]))
    first_z = z_all(jnp.concatenate([qkv_local, small.reshape(extra_rows, -1)]))
    segs = jnp.where(half == core, segments, core_swap(segments))
    ff_local = jnp.concatenate([up_weight, down_weight.T], axis=1)
    ff_local, first_z = gate(ff_local, first_z)
    ff_one = z_step(ff_local, 1)

    abs_z = xor_order([part[:drows] for part in first_z], tensor)
    qkv_cols = 3 * lheads * hs

    def regroup(first, second):
        left, right = first[:, 3 * lanes : qkv_cols], second[:, 3 * lanes : qkv_cols]
        both = [part[:, hs * k : hs * (k + 1)] for k in range(3) for part in (left, right)]
        return jnp.stack([first[:, : 3 * lanes], second[:, : 3 * lanes], jnp.concatenate(both, axis=1)])

    def with_out(first, second):
        left, right = first[:, qkv_cols:], second[:, qkv_cols:]
        out = jnp.concatenate([left[:, :lanes], right[:, :lanes], left[:, lanes:], right[:, lanes:]], axis=1)
        return jnp.concatenate([regroup(first, second), out[None]])

    zero_heads, one_heads = with_out(abs_z[0], abs_z[1]), with_out(abs_z[2], abs_z[3])
    keep = jnp.where(core == 0, zero_heads, one_heads)
    got = core_swap(jnp.where(core == 0, one_heads, zero_heads))
    chip_rows = jnp.where(
        core == 0, jnp.concatenate([keep, got], axis=1), jnp.concatenate([got, keep], axis=1)
    )
    ff_pair = jnp.stack([ff_local, ff_one])
    chip_rows, ff_pair = gate(chip_rows, ff_pair)
    qkv_pieces = chip_all(chip_rows)
    ff_middle = lax.ppermute(ff_pair, "tensor", [(1, 2), (2, 1)])

    tokens, ff_middle = gate(tokens, ff_middle)
    ff_end = lax.ppermute(ff_middle, "tensor", [(1, 0), (2, 3)])
    moved = [to_sequence(of_sequence(tokens, k), k) for k in range(2)]
    inner = (tensor == 1) | (tensor == 2)
    ff_other = jnp.where(inner, ff_middle[::-1], ff_end)
    qkv_pieces, ff_pair, ff_other, moved[0] = gate(qkv_pieces, ff_pair, ff_other, moved[0])
    out_mine = jnp.stack([piece[3] for piece in qkv_pieces])
    if aligned:
        firsts = [chip_step(ff_pair, 1), chip_step(ff_other, 2)]
        twos = [jnp.stack([ff_pair, firsts[0]]), jnp.stack([ff_other, firsts[1]])]
        cots = [of_sequence(cotangent, k) for k in range(2)]
        twos, moved, cots = gate(twos, moved, cots)
        fours = [chip_step(twos[0], 2), chip_step(twos[1], 1)]
        x_mine = jnp.concatenate(moved)
        x_other = core_swap(x_mine)
        twos_swapped = [core_swap(two) for two in twos]
        cots, x_mine, x_other, twos_swapped = gate(cots, x_mine, x_other, twos_swapped)
        cot_a, cot_b = [to_sequence(part, k) for k, part in enumerate(cots)]
    else:
        x_mine = jnp.concatenate(moved)
        x_other = core_swap(x_mine)
        cot_a, cot_b = [to_sequence(of_sequence(cotangent, k), k) for k in range(2)]
        out_other = core_swap(out_mine)
        ff_own = chip_all(jnp.concatenate([ff_pair, ff_other]))
        ff_all = [part for piece in ff_own for part in (piece, core_swap(piece))]
        qkv_pieces = [jnp.concatenate(xor_order(qkv_pieces, chip), axis=1)]
        out_both = [jnp.concatenate(xor_order(list(o), chip)) for o in (out_mine, out_other)]
        dense_pieces = [
            jnp.concatenate(
                [jnp.where(core == 0, out_both[0], out_both[1]), jnp.where(core == 0, out_both[1], out_both[0])],
                axis=1,
            ),
            jnp.concatenate(xor_order(ff_all, dp), axis=1),
        ]

    small_rel = [part[drows:].reshape(-1) for part in first_z]
    small = jnp.stack(xor_order(small_rel, tensor))
    all_pairs = small[:, :n_pair].astype(jnp.int32).reshape(2, heads, blocks)
    my_pairs = jnp.where(core == 0, all_pairs[0], all_pairs[1])
    pair_slots = jnp.stack(xor_order([my_pairs[:, k] for k in range(blocks)], slot_mask), axis=1) ^ slot_mask
    pair_slots = jnp.stack([pair_slots[h] for h in order])
    all_qvb = small[:, n_pair : n_pair + n_qv].astype(F32).reshape(2, heads, lanes)
    my_qvb = jnp.where(core == 0, all_qvb[0], all_qvb[1])
    my_qvb = jnp.stack([my_qvb[h] for h in order])
    up_bias_rel = jnp.concatenate([s[n_pair + n_qv :][:units] for s in small_rel]).astype(F32)
    groups = heads // 2
    bias = jnp.concatenate(
        [
            my_qvb[:, :hs].reshape(groups, lanes),
            jnp.zeros((groups, lanes), F32),
            my_qvb[:, hs:].reshape(groups, lanes),
        ],
        axis=1,
    ).reshape(groups, 1, 3 * lanes)

    seg_rows = jnp.where(low == 0, segs[0], segs[1]).reshape(blocks, rows)
    seg_row = jnp.concatenate(xor_order([seg_rows[k] for k in range(blocks)], slot_mask))
    seg_col = seg_row.reshape(blocks * rows, 1)
    seg_row = seg_row.reshape(1, blocks * rows)

    x_parts = [x_mine, x_other]
    q, k, v, mixed, mixed_other, lse, w_all = attend(pair_slots, place, x_parts, qkv_pieces, bias, seg_row, seg_col, hs)
    if aligned:
        q, k, v, mixed, mixed_other, lse, w_all, fours, cot_a, cot_b = gate(
            q, k, v, mixed, mixed_other, lse, w_all, fours, cot_a, cot_b
        )
        out_mine, mixed_other = gate(out_mine, mixed_other)
        out_other = core_swap(out_mine)
        dense_pieces = [out_mine, out_other] + twos + fours + twos_swapped + [core_swap(four) for four in fours]
    other = core_swap(mixed_other)

    blank = jnp.zeros((width,), BF16)
    vec = jnp.stack(
        [out_bias, first_gain, first_shift, down_bias, second_gain, second_shift, blank, blank]
    ).astype(F32)
    (
        layer_a, layer_b, gm_mine, gm_other, active, middle_low, grad_branch, grad_upper, grad_attn, grad_one, sums,
    ) = dense(
        place, dense_pieces, x_mine, mixed, other, cot_a, cot_b, vec, up_bias_rel.reshape(1, nt * units), 256
    )
    gm_got = core_swap(gm_other)
    home_0 = lax.ppermute(layer_a, BOTH, column(0, 0, True))

    def total_of(parts):
        total = parts[0].astype(F32)
        for part in parts[1:]:
            total = total + part.astype(F32)
        return total

    class Plane:
        def __init__(self, first, keep, send, got=None):
            self.first, self.got = first, got
            self.keep = self.split(keep)
            self.send = send if isinstance(send, list) else self.split(send)

        def split(self, x):
            return [x[: self.first], x[self.first :]]

        def first_sends(self):
            if self.got is None:
                return self.send
            got = self.split(self.got)
            self.keep = [[keep, g[:, :2]] for keep, g in zip(self.keep, got)]
            return [total_of([send, g[:, 2:]]).astype(BF16) for send, g in zip(self.send, got)]

        def first_moves(self, sends):
            return [chip_step(sends[0], 1), chip_step(sends[1], 2)]

        def second_sends(self, moves):
            keep = [k if isinstance(k, list) else [k] for k in self.keep]
            own = [total_of([part[:, 0] for part in k] + [m[:, 0]]) for k, m in zip(keep, moves)]
            sends = [total_of([part[:, 1] for part in k] + [m[:, 1]]).astype(BF16) for k, m in zip(keep, moves)]
            return own, sends

        def second_moves(self, sends):
            return [chip_step(sends[0], 2), chip_step(sends[1], 1)]

        def sums(self, own, moves):
            return [total_of([o, m]) for o, m in zip(own, moves)]

    class SlowPlane(Plane):
        def __init__(self, first, keep, send, got=None):
            self.first, self.view = first, keep if got is None else keep + got.astype(F32)

        def first_sends(self):
            return []

        def first_moves(self, sends):
            return []

        def second_sends(self, moves):
            return [], []

        def second_moves(self, sends):
            return []

        def sums(self, own, moves):
            pick = lambda step: lax.dynamic_index_in_dim(self.view, chip ^ step, 0, keepdims=False)
            total = total_of([pick(0)] + [chip_step(pick(step).astype(BF16), step) for step in range(1, chips)])
            return self.split(total.transpose(1, 0, 2))

    fast = chips == 4 and aligned

    def grads_of(left, right, extra, first):
        if fast:
            return weight_grad(place, left, right, extra, drows, first)
        grads = mm_lt(left, right)
        if extra:
            near, far = mm_lt(extra[0], extra[1]), mm_lt(extra[0], extra[2])
            head = [jnp.where(core == 0, near, far), jnp.where(core == 0, far, near)]
            grads = jnp.concatenate(head + [grads], axis=1)
        view = grads.reshape(chips, 2, drows, grads.shape[1] // width, width)
        ours = lax.dynamic_index_in_dim(view, core, 1, keepdims=False)
        theirs = lax.dynamic_index_in_dim(view, 1 - core, 1, keepdims=False).astype(BF16)
        return ours, theirs, theirs

    plane_of = Plane if fast else SlowPlane
    down_keep, down_send, down_theirs = grads_of(grad_branch, active, [], 2)
    down_got = core_swap(down_theirs)
    middle_low, down_keep, down_send, down_theirs, gm_got = gate(
        middle_low, down_keep, down_send, down_theirs, gm_got
    )
    up_keep, up_send, up_theirs = grads_of(middle_low, grad_upper, [grad_attn, mixed, other], 3)
    up_keep, up_send, up_theirs, home_0 = gate(up_keep, up_send, up_theirs, home_0)
    up_got = core_swap(up_theirs)

    down = plane_of(2, down_keep, down_send, down_got)
    d_sends = down.first_sends()
    pairs_0, gm_got, d_sends, layer_b = gate(pair_slots, gm_got, d_sends, layer_b)
    d_moves = down.first_moves(d_sends)
    home_1 = lax.ppermute(layer_b, BOTH, column(1, 0, True))
    packed_0, sums_0 = attend_back(pairs_0, 0, q, k, v, gm_mine, gm_got, seg_row, seg_col, lse, hs)
    packed_0, sums_0, d_moves, up_got = gate(packed_0, sums_0, d_moves, up_got)
    d_own, d_sends = down.second_sends(d_moves)
    up = plane_of(3, up_keep, up_send, up_got)
    u_sends = up.first_sends()
    pairs_1, d_own, d_sends, u_sends = gate(pair_slots, d_own, d_sends, u_sends)
    d_moves = down.second_moves(d_sends)
    u_moves = up.first_moves(u_sends)
    packed_1, sums_1 = attend_back(pairs_1, 1, q, k, v, gm_mine, gm_got, seg_row, seg_col, lse, hs)
    packed_1, sums_1, d_moves, home_1 = gate(packed_1, sums_1, d_moves, home_1)
    layer_out = at_home(home_0, home_1)
    d_first, d_second = down.sums(d_own, d_moves)
    d_second = d_second.astype(BF16)
    pair_slots, packed_1, d_first, d_second = gate(pair_slots, packed_1, d_first, d_second)
    d_second = z_step(d_second, 2)
    packed_2, sums_2 = attend_back(pair_slots, 2, q, k, v, gm_mine, gm_got, seg_row, seg_col, lse, hs)
    packed_2, sums_2, u_moves, d_second = gate(packed_2, sums_2, u_moves, d_second)
    d_keep = total_of([d_first[0], d_second[0]])
    d_give = total_of([d_first[1], d_second[1]]).astype(BF16)
    u_own, u_sends = up.second_sends(u_moves)

    head_sums = jnp.concatenate([part[row] for row in range(2) for part in (sums_0, sums_1, sums_2)])[None]
    blank = jnp.zeros_like(head_sums)
    sums = jnp.concatenate(
        [
            sums[:12],
            jnp.where(core == 0, head_sums, blank),
            jnp.where(core == 0, blank, head_sums),
            jnp.zeros((2, width), F32),
        ]
    )
    packed_2, d_keep, d_give, u_own, u_sends, sums = gate(packed_2, d_keep, d_give, u_own, u_sends, sums)
    packed = [packed_0, packed_1, packed_2]
    d_give = z_step(d_give, 1)
    sums_got = z_step(sums, 1)
    u_moves = up.second_moves(u_sends)
    in_mine, in_other = in_grad(packed, w_all, grad_one)
    in_mine, in_other, sums_got, packed, d_give, u_moves = gate(
        in_mine, in_other, sums_got, packed, d_give, u_moves
    )
    in_got = core_swap(in_other)
    down_grad = (d_keep + d_give.astype(F32)).T
    sums = sums + sums_got
    u_first, u_second = up.sums(u_own, u_moves)
    out_near = jnp.where(half == 0, u_first[0, :, :cols], u_first[0, :, cols:])
    out_far = jnp.where(half == 0, u_first[0, :, cols:], u_first[0, :, :cols])
    u_first = u_first[1:]
    u_second = jnp.concatenate([u_second[0], u_second[1], out_far], axis=1).astype(BF16)
    in_got, sums, u_first, u_second, out_near = gate(in_got, sums, u_first, u_second, out_near)
    u_second = z_step(u_second, 2)
    sums_got = z_step(sums, 2)
    in_low = [total_of([part[rows * k : rows * (k + 1)] for part in (in_mine, in_got)]).astype(BF16) for k in range(2)]
    packed, in_low = gate(packed, in_low)
    homes = [lax.ppermute(part, BOTH, column(k, 0, True)) for k, part in enumerate(in_low)]
    if fast:
        qkv_keep, *qkv_send = qkv_grads(place, x_parts, packed, 2 * drows)
    else:
        parts = [mm_lt(jnp.concatenate(x_parts), packed[g]).reshape(chips, 2 * drows, 3 * lanes) for g in (0, 2, 1)]
        qkv_keep = qkv_send = jnp.stack(parts, axis=2)
    qkv_keep, qkv_send, u_second, sums_got = gate(qkv_keep, qkv_send, u_second, sums_got)
    sums = sums + sums_got
    qkv = plane_of(2, qkv_keep, qkv_send)
    a_moves = qkv.first_moves(qkv.first_sends())
    u_keep, u_give = [total_of([u_first[j], u_second[:, units * j : units * (j + 1)]]) for j in range(2)]
    out_near = total_of([out_near, u_second[:, 2 * units :]])

    def out_unit(wanted_low):
        parts = [
            jnp.concatenate(
                [out_near[:, lanes * w : lanes * (w + 1)], out_near[:, 2 * lanes + hs * w : 2 * lanes + hs * (w + 1)]],
                axis=1,
            )
            for w in range(2)
        ]
        return jnp.where(wanted_low == 0, parts[0], parts[1])

    u_give = jnp.concatenate([u_give, out_unit(1 - low)], axis=1).astype(BF16)
    out_near = out_unit(low)
    u_give = z_step(u_give, 1)
    a_own, a_sends = qkv.second_sends(a_moves)
    a_moves = qkv.second_moves(a_sends)
    up_grad = total_of([u_keep, u_give[:, :units]])
    out_grad = total_of([out_near, u_give[:, units:]]).T.reshape(lheads, hs, drows)
    homes, a_moves, sums = gate(homes, a_moves, sums)
    sums = sums + core_swap(sums)
    for bit in range(chips.bit_length() - 1):
        sums = sums + chip_step(sums, 1 << bit)
    outb_grad, gain_one_grad, shift_one_grad, downb_grad, gain_two_grad, shift_two_grad = [
        sums[row] for row in range(6)
    ]
    upb_grad = lax.dynamic_index_in_dim(sums, 8 + tensor, 0, keepdims=False)
    head_row = jnp.where(half == 0, sums[12], sums[13]).reshape(2, 6, hs)
    qvb_grad = jnp.where(low == 0, head_row[:, [0, 1, 4]], head_row[:, [2, 3, 5]])
    qvb_grad = jnp.concatenate([qvb_grad[0], qvb_grad[1]], axis=1)

    input_grad = at_home(*homes)
    sum_a, sum_b = qkv.sums(a_own, a_moves)
    sum_0, sum_2, sum_1 = [part.reshape(2, drows, 3 * lanes) for part in (sum_a[0], sum_a[1], sum_b[0])]
    sum_01 = [sum_0, sum_1]

    def share(c, u):
        third = [sum_2[c][:, lanes * k + hs * u : lanes * k + hs * (u + 1)] for k in range(3)]
        return jnp.concatenate([sum_01[u][c]] + third, axis=1)

    shares = [[share(c, u).astype(BF16) for u in range(2)] for c in range(2)]
    qkv_grad = jnp.zeros((drows, 3 * lheads * hs), F32)
    for flip in range(2):
        for step in range(2):
            by_core = [jnp.where((low ^ step) == 0, shares[c][0], shares[c][1]) for c in range(2)]
            sent = jnp.where((half ^ flip) == 0, by_core[0], by_core[1])
            qkv_grad = qkv_grad + lax.ppermute(sent, BOTH, column(step, flip, False)).astype(F32)
    pairs_part = qkv_grad[:, : 3 * lanes].reshape(drows, 3, 2, hs)
    third_part = qkv_grad[:, 3 * lanes :].reshape(drows, 3, 1, hs)
    qkv_grad = jnp.concatenate([pairs_part, third_part], axis=2).transpose(0, 2, 1, 3)
    qkv_grad = qkv_grad.reshape(drows, lheads, 3 * hs)
    return (
        layer_out,
        input_grad,
        qkv_grad,
        qvb_grad,
        out_grad,
        outb_grad,
        gain_one_grad,
        shift_one_grad,
        up_grad,
        upb_grad,
        down_grad,
        downb_grad,
        gain_two_grad,
        shift_two_grad,
    )


def solution(mesh):
    return jax.shard_map(
        per_device,
        mesh=mesh,
        in_specs=(
            P("dp", "tensor", None),
            P("dp", None),
            P("tensor", None),
            P("dp", "tensor", None),
            P("tensor", None),
            P("tensor", None, "dp"),
            P(),
            P(),
            P(),
            P("dp", "tensor"),
            P("tensor"),
            P("tensor", "dp"),
            P(),
            P(),
            P(),
            P("dp", "tensor", None),
        ),
        out_specs=(
            P("dp", "tensor", None),
            P("dp", "tensor", None),
            P("dp", "tensor", None),
            P("tensor", None),
            P("tensor", None, "dp"),
            P(),
            P(),
            P(),
            P("dp", "tensor"),
            P("tensor"),
            P("tensor", "dp"),
            P(),
            P(),
            P(),
        ),
        check_vma=False,
    )
```

```python
import functools

import jax
import jax.numpy as jnp
from jax import lax
from jax.experimental import pallas as pl
from jax.experimental.pallas import tpu as pltpu
from jax.sharding import PartitionSpec as P

EPS = 1e-06
NEG = -1e30
BOTH = ("dp", "tensor")
F32 = jnp.float32
BF16 = jnp.bfloat16
ANY = pl.BlockSpec(memory_space=pl.ANY)
LIMIT = 58 << 20
COST = pl.CostEstimate(flops=10**9, bytes_accessed=1 << 16, transcendentals=0)


def mm(left, right):
    return lax.dot_general(left, right, (((1,), (0,)), ((), ())), preferred_element_type=F32)


def mm_rt(left, right):
    return lax.dot_general(left, right, (((1,), (1,)), ((), ())), preferred_element_type=F32)


def mm_lt(left, right):
    return lax.dot_general(left, right, (((0,), (0,)), ((), ())), preferred_element_type=F32)


def head_lanes(shape, head, dim, head_size):
    place = lax.broadcasted_iota(jnp.int32, shape, dim)
    return (place < head_size) if head == 0 else (place >= head_size)


def fetches(pieces, offsets, target, dim, sems, first):
    copies = []
    for k, (piece, offset) in enumerate(zip(pieces, offsets)):
        count = piece.shape[dim]
        where = pl.ds(offset if isinstance(offset, int) else pl.multiple_of(offset, count), count)
        index = (slice(None),) * dim + (where,)
        copies.append(pltpu.make_async_copy(piece, target.at[index], sems.at[first + k]))
    return copies


def piece_rows(place, step, rows, count):
    if count == 1:
        return [0]
    return [(place ^ (k * step)) * rows for k in range(count)]


def attend_kernel(pair_ref, place_ref, *refs, rows, hs, blocks, n_w):
    x_refs, refs = refs[:2], refs[2:]
    w_refs, refs = refs[:n_w], refs[n_w:]
    bias_ref, segq_ref, segk_ref, q_out, k_out, v_out, o_mine, o_other, lse_ref, w_all, x_all, sems = refs
    group, block = pl.program_id(0), pl.program_id(1)
    lanes2 = 2 * hs

    chip = place_ref[0] // 2
    w_parts = [piece.at[: w_all.shape[0]] for piece in w_refs]
    copies = fetches(x_refs, [0, x_refs[0].shape[0]], x_all, 0, sems, n_w) + fetches(
        w_parts, piece_rows(chip, 1, w_refs[0].shape[1], n_w), w_all, 1, sems, 0
    )
    late = copies.pop(1)

    @pl.when((group == 0) & (block == 0))
    def _():
        for copy in copies:
            copy.start()
        late.start()
        for copy in copies:
            copy.wait()

    @pl.when(block == 0)
    def _():
        weight = w_all[group]
        for k in range(blocks):
            if k == blocks // 2:

                @pl.when(group == 0)
                def _():
                    late.wait()

            part = pl.ds(k * rows, rows)
            out = (mm(x_all[part, :], weight) + bias_ref[0]).astype(BF16)
            q_out[part, :] = out[:, :lanes2] * (hs**-0.5)
            k_out[part, :] = out[:, lanes2 : 2 * lanes2]
            v_out[part, :] = out[:, 2 * lanes2 :]

    own = pl.ds(pl.multiple_of(block * rows, rows), rows)
    q2 = q_out[own, :]
    own_raw = (q2.astype(F32) * k_out[own, :].astype(F32)).T
    own_values = v_out[own, :].astype(F32).T
    segq = segq_ref[...]
    total = jnp.zeros((2 * hs, rows), F32)
    for head in range(2):
        target = pair_ref[2 * group + head, block]
        there = pl.ds(pl.multiple_of(target * rows, rows), rows)
        keys, values = k_out[there, :], v_out[there, :]
        lanes = head_lanes(q2.shape, head, 1, hs)
        scores = mm_rt(keys, jnp.where(lanes, q2, jnp.zeros_like(q2)))
        scores = jnp.where(segk_ref[there, :] == segq, scores, NEG)
        raw = jnp.sum(own_raw[head * hs : (head + 1) * hs], axis=0, keepdims=True)
        raw = jnp.where(target != block, raw, NEG)
        peak = jnp.maximum(jnp.max(scores, axis=0, keepdims=True), raw)
        expo = jnp.exp(scores - peak)
        own_expo = jnp.exp(raw - peak)
        denom = jnp.sum(expo, axis=0, keepdims=True) + own_expo
        masked_values = jnp.where(lanes, values, jnp.zeros_like(values))
        part = mm_lt(masked_values, expo.astype(BF16))
        low = own_expo.astype(BF16).astype(F32)
        mine = head_lanes(part.shape, head, 0, hs)
        part = part + jnp.where(mine, own_values * low, 0.0)
        total = total + part * (1.0 / denom)
        lse_ref[0, head : head + 1, :] = peak + jnp.log(denom)
    mixed = total.T.astype(BF16)

    @pl.when(block < blocks // 2)
    def _():
        o_mine[pl.ds(pl.multiple_of(block * rows, rows), rows), :] = mixed

    @pl.when(block >= blocks // 2)
    def _():
        o_other[pl.ds(pl.multiple_of((block - blocks // 2) * rows, rows), rows), :] = mixed


def attend(pairs, place, x_parts, w_pieces, bias, segq, segk, hs):
    heads, blocks = pairs.shape
    width = x_parts[0].shape[1]
    seq, groups, lanes = 2 * x_parts[0].shape[0], heads // 2, 2 * hs
    rows = seq // blocks
    kept = jax.ShapeDtypeStruct((seq, groups * lanes), BF16)
    flops = 2 * seq * width * 3 * groups * lanes + 4 * heads * seq * rows * 2 * lanes
    return pl.pallas_call(
        functools.partial(attend_kernel, rows=rows, hs=hs, blocks=blocks, n_w=len(w_pieces)),
        grid_spec=pltpu.PrefetchScalarGridSpec(
            num_scalar_prefetch=2,
            grid=(groups, blocks),
            in_specs=[ANY] * (2 + len(w_pieces))
            + [
                pl.BlockSpec((1, 1, 3 * lanes), lambda g, i, p, q: (g, 0, 0)),
                pl.BlockSpec((1, rows), lambda g, i, p, q: (0, i)),
                pl.BlockSpec((seq, 1), lambda g, i, p, q: (0, 0)),
            ],
            out_specs=[pl.BlockSpec((seq, lanes), lambda g, i, p, q: (0, g))] * 3
            + [
                pl.BlockSpec((seq // 2, lanes), lambda g, i, p, q: (0, g)),
                pl.BlockSpec((seq // 2, lanes), lambda g, i, p, q: (0, g)),
                pl.BlockSpec((1, 8, rows), lambda g, i, p, q: (g, 0, i)),
                pl.BlockSpec((groups, width, 3 * lanes), lambda g, i, p, q: (0, 0, 0)),
            ],
            scratch_shapes=[
                pltpu.VMEM((seq, width), BF16),
                pltpu.SemaphoreType.DMA((2 + len(w_pieces),)),
            ],
        ),
        out_shape=[kept] * 3
        + [jax.ShapeDtypeStruct((seq // 2, groups * lanes), BF16)] * 2
        + [
            jax.ShapeDtypeStruct((groups, 8, seq), F32),
            jax.ShapeDtypeStruct((groups, width, 3 * lanes), BF16),
        ],
        compiler_params=pltpu.CompilerParams(vmem_limit_bytes=58 << 20),
        cost_estimate=COST,
        name="attend",
    )(pairs, place, *x_parts, *w_pieces, bias, segq, segk)


def attend_back_kernel(
    pair_ref, group_ref, q_ref, k_ref, v_ref, do_a, do_b, segq_ref, segk_ref, lse_ref,
    packed_ref, sums_ref, dq_all, dk_acc, dv_acc, *, rows, hs, blocks,
):
    block = pl.program_id(0)

    @pl.when(block == 0)
    def _():
        dk_acc[...] = jnp.zeros_like(dk_acc)
        dv_acc[...] = jnp.zeros_like(dv_acc)
        sums_ref[...] = jnp.zeros_like(sums_ref)

    own = pl.ds(pl.multiple_of(block * rows, rows), rows)
    q2, do2 = q_ref[...], jnp.where(block < blocks // 2, do_a[...], do_b[...])
    qt, dot = q2.astype(F32).T, do2.astype(F32).T
    own_keys, own_values = k_ref[own, :].astype(F32).T, v_ref[own, :].astype(F32).T
    own_raw, own_dp = qt * own_keys, dot * own_values
    segq = segq_ref[...]
    dq = jnp.zeros((2 * hs, rows), F32)
    own_ds, own_low = [], []
    for head in range(2):
        target = pair_ref[2 * group_ref[0] + head, block]
        there = pl.ds(pl.multiple_of(target * rows, rows), rows)
        keys, values = k_ref[there, :], v_ref[there, :]
        lanes = head_lanes(q2.shape, head, 1, hs)
        zero = jnp.zeros_like(q2)
        qm, dom = jnp.where(lanes, q2, zero), jnp.where(lanes, do2, zero)
        lse = lse_ref[0, head : head + 1, :]
        scores = mm_rt(keys, qm)
        probs = jnp.exp(jnp.where(segk_ref[there, :] == segq, scores - lse, NEG))
        raw = jnp.sum(own_raw[head * hs : (head + 1) * hs], axis=0, keepdims=True)
        self_prob = jnp.exp(jnp.where(target != block, raw - lse, NEG))
        self_dp = jnp.sum(own_dp[head * hs : (head + 1) * hs], axis=0, keepdims=True)
        dv_acc[there, :] += mm(probs.astype(BF16), dom)
        dprobs = mm_rt(values, dom)
        delta = jnp.sum(probs * dprobs, axis=0, keepdims=True) + self_prob * self_dp
        dscores = (probs * (dprobs - delta)).astype(BF16)
        dk_acc[there, :] += mm(dscores, qm)
        dq = dq + mm_lt(jnp.where(lanes, keys, jnp.zeros_like(keys)), dscores)
        own_ds.append((self_prob * (self_dp - delta)).astype(BF16).astype(F32))
        own_low.append(self_prob.astype(BF16).astype(F32))
    first = head_lanes(dq.shape, 0, 0, hs)
    ds_rows = jnp.where(first, own_ds[0], own_ds[1])
    low_rows = jnp.where(first, own_low[0], own_low[1])
    dq = ((dq + ds_rows * own_keys) * (hs**-0.5)).T
    dq_all[own, :] = dq.astype(BF16)
    sums_ref[0:1, :] += jnp.sum(dq, axis=0, keepdims=True)
    dk_acc[own, :] += (ds_rows * qt).T
    dv_acc[own, :] += (low_rows * dot).T

    @pl.when(block == blocks - 1)
    def _():
        dv = dv_acc[...]
        sums_ref[1:2, :] = jnp.sum(dv, axis=0, keepdims=True)
        packed_ref[...] = jnp.concatenate(
            [dq_all[...], dk_acc[...].astype(BF16), dv.astype(BF16)], axis=1
        )


def attend_back(pairs, group, q, k, v, grad_a, grad_b, segq, segk, lse, hs):
    heads, blocks = pairs.shape
    seq, lanes = q.shape[0], 2 * hs
    rows, half = seq // blocks, blocks // 2
    return pl.pallas_call(
        functools.partial(attend_back_kernel, rows=rows, hs=hs, blocks=blocks),
        grid_spec=pltpu.PrefetchScalarGridSpec(
            num_scalar_prefetch=2,
            grid=(blocks,),
            in_specs=[
                pl.BlockSpec((rows, lanes), lambda i, p, g: (i, g[0])),
                pl.BlockSpec((seq, lanes), lambda i, p, g: (0, g[0])),
                pl.BlockSpec((seq, lanes), lambda i, p, g: (0, g[0])),
                pl.BlockSpec((rows, lanes), lambda i, p, g: (jnp.minimum(i, half - 1), g[0])),
                pl.BlockSpec((rows, lanes), lambda i, p, g: (jnp.maximum(i - half, 0), g[0])),
                pl.BlockSpec((1, rows), lambda i, p, g: (0, i)),
                pl.BlockSpec((seq, 1), lambda i, p, g: (0, 0)),
                pl.BlockSpec((1, 8, rows), lambda i, p, g: (g[0], 0, i)),
            ],
            out_specs=[
                pl.BlockSpec((seq, 3 * lanes), lambda i, p, g: (0, 0)),
                pl.BlockSpec((8, lanes), lambda i, p, g: (0, 0)),
            ],
            scratch_shapes=[
                pltpu.VMEM((seq, lanes), BF16),
                pltpu.VMEM((seq, lanes), F32),
                pltpu.VMEM((seq, lanes), F32),
            ],
        ),
        out_shape=[
            jax.ShapeDtypeStruct((seq, 3 * lanes), BF16),
            jax.ShapeDtypeStruct((8, lanes), F32),
        ],
        compiler_params=pltpu.CompilerParams(vmem_limit_bytes=12 << 20),
        cost_estimate=COST,
        name="attend_back",
    )(pairs, jnp.full((1,), group, jnp.int32), q, k, v, grad_a, grad_b, segq, segk, lse)


def qkv_grad_kernel(place_ref, *refs):
    packed_refs, xa_ref, xb_ref, keep_ref, send_a, send_b, packed, acc, sems = refs[:3], *refs[3:]
    half = xa_ref.shape[0]
    chip = place_ref[0] // 2
    rows = keep_ref.shape[2]
    step = pl.program_id(0)
    copies = [
        pltpu.make_async_copy(packed_refs[g], packed.at[j], sems.at[j]) for j, g in enumerate((0, 2, 1))
    ]

    @pl.when(step == 0)
    def _():
        for copy in copies:
            copy.start()

    for j, copy in enumerate(copies):

        @pl.when(step == j)
        def _(copy=copy):
            copy.wait()

    acc[...] = mm_lt(xa_ref[...], packed[step, :half, :]) + mm_lt(xb_ref[...], packed[step, half:, :])
    for k, away in enumerate(away_of(step == 2)):
        ours = acc[pl.ds(pl.multiple_of((chip ^ away) * rows, rows), rows), :]
        if k < 2:
            keep_ref[0, k] = ours
        else:
            ours = ours.astype(BF16)

            @pl.when(step < 2)
            def _(ours=ours, k=k):
                send_a[0, k - 2] = ours

            @pl.when(step == 2)
            def _(ours=ours, k=k):
                send_b[0, k - 2] = ours


def qkv_grads(place, x_parts, packed, rows):
    half, width = x_parts[0].shape
    cols = packed[0].shape[1]
    whole = lambda a, b: pl.BlockSpec((a, b), lambda i, p: (0, 0))
    return pl.pallas_call(
        qkv_grad_kernel,
        grid_spec=pltpu.PrefetchScalarGridSpec(
            num_scalar_prefetch=1,
            grid=(3,),
            in_specs=[ANY] * 3 + [whole(half, width)] * 2,
            out_specs=[
                pl.BlockSpec((1, 2, rows, cols), lambda i, p: (i, 0, 0, 0)),
                pl.BlockSpec((1, 2, rows, cols), lambda i, p: (jnp.minimum(i, 1), 0, 0, 0)),
                pl.BlockSpec((1, 2, rows, cols), lambda i, p: (0, 0, 0, 0)),
            ],
            scratch_shapes=[
                pltpu.VMEM((3, 2 * half, cols), BF16),
                pltpu.VMEM((width, cols), F32),
                pltpu.SemaphoreType.DMA((3,)),
            ],
        ),
        out_shape=[
            jax.ShapeDtypeStruct((3, 2, rows, cols), F32),
            jax.ShapeDtypeStruct((2, 2, rows, cols), BF16),
            jax.ShapeDtypeStruct((1, 2, rows, cols), BF16),
        ],
        compiler_params=pltpu.CompilerParams(vmem_limit_bytes=18 << 20),
        cost_estimate=COST,
        name="qkv_grads",
    )(place, *packed, *x_parts)


def in_grad_kernel(*refs, n, half):
    packed, w_ref, extra, mine_ref, other_ref = refs[:n], refs[n], *refs[n + 1 :]
    step = pl.program_id(0)
    total = mm_rt(packed[0][...], w_ref[0])
    for g in range(1, n):
        total = total + mm_rt(packed[g][...], w_ref[g])

    @pl.when(step < half)
    def _():
        other_ref[...] = total.astype(BF16)

    @pl.when(step >= half)
    def _():
        mine_ref[...] = total + extra[...]


def in_grad(packed, weight, extra):
    seq, cols = packed[0].shape
    n, width = weight.shape[:2]
    half = 2
    tile = seq // (2 * half)
    late = lambda i: (jnp.maximum(i - half, 0), 0)
    return pl.pallas_call(
        functools.partial(in_grad_kernel, n=n, half=half),
        grid=(2 * half,),
        in_specs=[pl.BlockSpec((tile, cols), lambda i: ((i + half) % (2 * half), 0))] * n
        + [pl.BlockSpec((n, width, cols), lambda i: (0, 0, 0)), pl.BlockSpec((tile, width), late)],
        out_specs=[
            pl.BlockSpec((tile, width), late),
            pl.BlockSpec((tile, width), lambda i: (jnp.minimum(i, half - 1), 0)),
        ],
        out_shape=[
            jax.ShapeDtypeStruct((seq // 2, width), F32),
            jax.ShapeDtypeStruct((seq // 2, width), BF16),
        ],
        compiler_params=pltpu.CompilerParams(vmem_limit_bytes=58 << 20),
        cost_estimate=COST,
        name="in_grad",
    )(*packed, weight, extra)


def norm(values):
    centred = values - jnp.mean(values, axis=-1, keepdims=True)
    scale = lax.rsqrt(jnp.mean(centred * centred, axis=-1, keepdims=True) + EPS)
    return centred * scale, scale


def norm_back(grad, unit, scale, gain):
    q = grad * gain
    mean_q = jnp.mean(q, axis=-1, keepdims=True)
    mean_qn = jnp.mean(q * unit, axis=-1, keepdims=True)
    return scale * (q - mean_q - unit * mean_qn)


def gelu_parts(u):
    dense = jnp.exp(-0.5 * u * u) * 0.3989422804014327
    t = 1.0 / (1.0 + 0.2316419 * jnp.abs(u))
    poly = t * (
        0.319381530
        + t * (-0.356563782 + t * (1.781477937 + t * (-1.821255978 + t * 1.330274429)))
    )
    tail = dense * poly
    phi = jnp.where(u >= 0, 1.0 - tail, tail)
    return u * phi, phi + u * dense


def dense_copies(place, pieces, wo, ww, sems):
    copies = []

    def add(source, target):
        copies.append(pltpu.make_async_copy(source, target, sems.at[len(copies)]))

    if len(pieces) == 2:
        add(pieces[0], wo)
        add(pieces[1], ww)
        return copies
    core, chip = place % 2, place // 2
    chips, rows, cols = pieces[0].shape
    for side in range(2):
        lanes = pl.ds(pl.multiple_of((core ^ side) * cols, cols), cols)
        for k in range(chips):
            add(pieces[side].at[k], wo.at[pl.ds(pl.multiple_of((chip ^ k) * rows, rows), rows), lanes])
    half, rows = pieces[2].shape[1:3]
    for k, piece in enumerate(pieces[2:]):
        away = ((0, 1), (0, 2), (2, 3), (1, 3))[k % 4]
        for j in range(2):
            base = (place ^ (2 * away[j] + k // 4)) * rows
            add(piece.at[j], ww.at[pl.ds((k % 2) * half, half), pl.ds(pl.multiple_of(base, rows), rows), :])
    return copies


def dense_kernel(place_ref, *refs, n_w, chunks):
    w_refs, refs = refs[:n_w], refs[n_w:]
    (
        x_ref, mine_ref, other_ref, cot_a, cot_b, vec_ref, upb_ref,
        layer_a, layer_b, gm_mine, gm_other, act_ref, mlow_ref, gb_ref, gul_ref, ga_ref, gone_ref, sums_ref,
        wo, ww, slope, layer, sems,
    ) = refs
    step = pl.program_id(0)
    core = place_ref[0] % 2
    cols = mine_ref.shape[1]
    width = x_ref.shape[1]
    units = ww.shape[2] // 2
    copies = dense_copies(place_ref[0], w_refs, wo, ww, sems)
    n_wo = 1 if len(w_refs) == 2 else 2 * w_refs[0].shape[0]

    @pl.when(step == 0)
    def _():
        for copy in copies:
            copy.start()
        for copy in copies[:n_wo]:
            copy.wait()
        sums_ref[...] = jnp.zeros_like(sums_ref)

    mine_cols = pl.ds(pl.multiple_of(core * cols, cols), cols)
    other_cols = pl.ds(pl.multiple_of((1 - core) * cols, cols), cols)
    early = step < pl.num_programs(0) // 2

    def add_sum(row, values):
        sums_ref[pl.ds(row, 1), :] += jnp.sum(values, axis=0, keepdims=True)

    def advance(at):
        attn = mm_rt(mine_ref[at, :], wo[:, mine_cols]) + mm_rt(other_ref[at, :], wo[:, other_cols])
        yield
        unit_one, scale_one = norm(x_ref[at, :].astype(F32) + attn + vec_ref[0:1, :])
        middle = unit_one * vec_ref[1:2, :] + vec_ref[2:3, :]
        low = middle.astype(BF16)
        mlow_ref[at, :] = low
        total = middle + vec_ref[3:4, :]

        @pl.when(step == 0)
        def _():
            for copy in copies[n_wo:]:
                copy.wait()

        yield
        for k in range(chunks):
            place = slice(k * units, (k + 1) * units)
            upper = mm(low, ww[k, :, :units]) + upb_ref[:, place]
            active, rise = gelu_parts(upper)
            active = active.astype(BF16)
            act_ref[at, place] = active
            slope[at, place] = rise.astype(BF16)
            total = total + mm_rt(active, ww[k, :, units:])
            yield
        unit_two, scale_two = norm(total)
        gain_two = vec_ref[4:5, :]
        layer[at, :] = (unit_two * gain_two + vec_ref[5:6, :]).astype(BF16)
        cot = jnp.where(early, cot_a[at, :], cot_b[at, :]).astype(F32)
        grad_two = norm_back(cot, unit_two, scale_two, gain_two)
        add_sum(4, cot * unit_two)
        add_sum(5, cot)
        add_sum(3, grad_two)
        low = grad_two.astype(BF16)
        gb_ref[at, :] = low
        total = grad_two
        yield
        for k in range(chunks):
            place = slice(k * units, (k + 1) * units)
            grad_upper = mm(low, ww[k, :, units:]) * slope[at, place].astype(F32)
            add_sum(8 + (k ^ place_ref[1]), grad_upper)
            grad_low = grad_upper.astype(BF16)
            gul_ref[at, place] = grad_low
            total = total + mm_rt(grad_low, ww[k, :, :units])
            yield
        add_sum(1, total * unit_one)
        add_sum(2, total)
        grad_one = norm_back(total, unit_one, scale_one, vec_ref[1:2, :])
        add_sum(0, grad_one)
        gone_ref[at, :] = grad_one
        grad_attn = grad_one.astype(BF16)
        ga_ref[at, :] = grad_attn
        yield
        gm_mine[at, :] = mm(grad_attn, wo[:, mine_cols]).astype(BF16)
        gm_other[at, :] = mm(grad_attn, wo[:, other_cols]).astype(BF16)
        yield

    part = x_ref.shape[0] // 1
    for _ in zip(*[advance(slice(part * k, part * (k + 1))) for k in range(1)]):
        pass

    @pl.when(early)
    def _():
        layer_a[...] = layer[...]

    @pl.when(jnp.logical_not(early))
    def _():
        layer_b[...] = layer[...]


def dense(place, w_pieces, x, mine, other, cot_a, cot_b, vec, upb, tile):
    count, width = x.shape
    cols = other.shape[1]
    units = w_pieces[-1].shape[-1] // 2
    chunks = upb.shape[1] // units
    steps = count // tile
    half = steps // 2
    n_copies = 2 if len(w_pieces) == 2 else 2 * w_pieces[0].shape[0] + 2 * (len(w_pieces) - 2)
    rows = lambda n: pl.BlockSpec((tile, n), lambda i, p: (i, 0))
    fixed = lambda a, b: pl.BlockSpec((a, b), lambda i, p: (0, 0))
    full = chunks * units
    shapes = [
        ((count // 2, width), BF16), ((count // 2, width), BF16),
        ((count, cols), BF16), ((count, cols), BF16), ((count, full), BF16),
        ((count, width), BF16), ((count, width), BF16), ((count, full), BF16), ((count, width), BF16),
        ((count, width), F32), ((16, width), F32),
    ]
    flops = 8 * count * width * full + 4 * count * width * 2 * cols
    return pl.pallas_call(
        functools.partial(dense_kernel, n_w=len(w_pieces), chunks=chunks),
        grid_spec=pltpu.PrefetchScalarGridSpec(
            num_scalar_prefetch=1,
            grid=(count // tile,),
            in_specs=[ANY] * len(w_pieces)
            + [rows(width), rows(cols), rows(cols)]
            + [
                pl.BlockSpec((tile, width), lambda i, p: (jnp.minimum(i, half - 1), 0)),
                pl.BlockSpec((tile, width), lambda i, p: (jnp.maximum(i - half, 0), 0)),
                fixed(8, width),
                fixed(1, full),
            ],
            out_specs=[
                pl.BlockSpec((tile, width), lambda i, p: (jnp.minimum(i, half - 1), 0)),
                pl.BlockSpec((tile, width), lambda i, p: (jnp.maximum(i - half, 0), 0)),
                rows(cols), rows(cols), rows(full), rows(width), rows(width), rows(full),
                rows(width), rows(width), fixed(16, width),
            ],
            scratch_shapes=[
                pltpu.VMEM((width, 2 * cols), BF16),
                pltpu.VMEM((chunks, width, 2 * units), BF16),
                pltpu.VMEM((tile, full), BF16),
                pltpu.VMEM((tile, width), BF16),
                pltpu.SemaphoreType.DMA((n_copies,)),
            ],
        ),
        out_shape=[jax.ShapeDtypeStruct(*s) for s in shapes],
        compiler_params=pltpu.CompilerParams(vmem_limit_bytes=58 << 20),
        cost_estimate=COST,
        name="dense",
    )(place, *w_pieces, x, mine, other, cot_a, cot_b, vec, upb)


def away_of(second):
    return [0, jnp.where(second, 1, 2), jnp.where(second, 2, 1), 3]


def grad_kernel(place_ref, *refs, n, steps, drows, first):
    left_ref, right_ref, refs = refs[0], refs[1], refs[2:]
    extra, (keep_ref, send_ref, theirs_ref, left_t, acc) = refs[: n - 2], refs[n - 2 :]
    core, chip = place_ref[0] % 2, place_ref[0] // 2
    step = pl.program_id(0)

    @pl.when(step == 0)
    def _():
        left_t[...] = left_ref[...].T

    @pl.when(step >= steps)
    def _():
        acc[...] = mm(left_t[...], right_ref[...])

    if extra:

        @pl.when(step < steps)
        def _():
            cols = extra[1].shape[1]
            mine_cols = pl.ds(pl.multiple_of(core * cols, cols), cols)
            other_cols = pl.ds(pl.multiple_of((1 - core) * cols, cols), cols)
            acc[:, mine_cols] = mm_lt(extra[0][...], extra[1][...])
            acc[:, other_cols] = mm_lt(extra[0][...], extra[2][...])

    for k, away in enumerate(away_of(step >= first)):
        base = 2 * (chip ^ away)
        ours = acc[pl.ds(pl.multiple_of((base + core) * drows, drows), drows), :]
        if k < 2:
            keep_ref[0, k] = ours
        else:
            send_ref[0, k - 2] = ours.astype(BF16)
        theirs_ref[0, k] = acc[pl.ds(pl.multiple_of((base + 1 - core) * drows, drows), drows), :].astype(BF16)


def weight_grad(place, left, right, extra, drows, first):
    count, width = left.shape
    tile = width
    steps = 1 if extra else 0
    chunks = right.shape[1] // tile + steps
    whole = lambda a, b: pl.BlockSpec((a, b), lambda i, p: (0, 0))
    shapes = [((chunks, 2, drows, tile), F32), ((chunks, 2, drows, tile), BF16), ((chunks, 4, drows, tile), BF16)]
    return pl.pallas_call(
        functools.partial(grad_kernel, n=2 + len(extra), steps=steps, drows=drows, first=first),
        grid_spec=pltpu.PrefetchScalarGridSpec(
            num_scalar_prefetch=1,
            grid=(chunks,),
            in_specs=[
                whole(count, width),
                pl.BlockSpec((count, tile), lambda i, p: (0, jnp.maximum(i - steps, 0))),
            ]
            + [whole(count, e.shape[1]) for e in extra],
            out_specs=[pl.BlockSpec((1,) + shape[1:], lambda i, p: (i, 0, 0, 0)) for shape, _ in shapes],
            scratch_shapes=[pltpu.VMEM((width, count), BF16), pltpu.VMEM((width, tile), F32)],
        ),
        out_shape=[jax.ShapeDtypeStruct(*shape) for shape in shapes],
        compiler_params=pltpu.CompilerParams(vmem_limit_bytes=15 << 20),
        cost_estimate=COST,
        name="weight_grad",
    )(place, left, right, *extra)


def xor_order(parts, index):
    parts = list(parts)
    bit = 1
    while bit < len(parts):
        odd = (index // bit) % 2 == 1
        parts = [jnp.where(odd, parts[k ^ bit], parts[k]) for k in range(len(parts))]
        bit *= 2
    return parts


def per_device(
    tokens,
    segments,
    pairing,
    qkv_weight,
    qv_bias,
    out_weight,
    out_bias,
    first_gain,
    first_shift,
    up_weight,
    up_bias,
    down_weight,
    down_bias,
    second_gain,
    second_shift,
    cotangent,
):
    width = tokens.shape[2]
    rows = tokens.shape[1]
    lheads, blocks = pairing.shape
    hs = qv_bias.shape[1] // 2
    lanes = 2 * hs
    units = up_weight.shape[1]
    ndp, nt = lax.axis_size("dp"), lax.axis_size("tensor")
    drows = width // ndp
    chips = ndp // 2
    dp, tensor = lax.axis_index("dp"), lax.axis_index("tensor")
    core, chip, half, low = dp % 2, dp // 2, tensor // 2, tensor % 2
    slot_mask = 2 * core + low
    heads = 2 * lheads
    cols = heads * hs
    aligned = drows % 8 == 0
    place = jnp.stack([dp, tensor]).astype(jnp.int32)
    order = [0, 1, 3, 4, 2, 5]

    core_pairs = [(i, i ^ 1) for i in range(ndp)]

    def core_swap(x):
        return lax.ppermute(x, "dp", core_pairs)

    def z_step(x, k):
        return lax.ppermute(x, "tensor", [(i, i ^ k) for i in range(nt)])

    def chip_step(x, k):
        return lax.ppermute(x, "dp", [(i, i ^ (2 * k)) for i in range(ndp)])

    def column(k, flip, back):
        steps = []
        for p in range(chips):
            for c in range(2):
                for a in range(2):
                    for b in range(2):
                        home = (2 * p + c) * nt + 2 * a + b
                        away = (2 * p + (a ^ flip)) * nt + 2 * c + (b ^ k)
                        steps.append((away, home) if back else (home, away))
        return steps

    def of_sequence(x, k):
        return lax.dynamic_index_in_dim(x, low ^ k, 0, keepdims=False)

    def to_sequence(part, k):
        return lax.ppermute(part, BOTH, column(k, 0, False))

    def at_home(first, second):
        return jnp.stack([jnp.where(low == 0, first, second), jnp.where(low == 0, second, first)])

    def z_all(x):
        return [x] + [z_step(x, k) for k in range(1, nt)]

    def chip_all(x):
        return [x] + [chip_step(x, k) for k in range(1, chips)]

    gate = lambda *trees: lax.optimization_barrier(trees)

    qkv_local = qkv_weight.reshape(drows, lheads, 3, hs).transpose(0, 2, 1, 3)
    qkv_local = jnp.concatenate(
        [
            qkv_local[:, :, :2].reshape(drows, 3 * lanes),
            qkv_local[:, :, 2].reshape(drows, 3 * hs),
            out_weight.reshape(lheads * hs, drows).T,
        ],
        axis=1,
    )
    small = jnp.concatenate([pairing.astype(BF16).reshape(-1), qv_bias.reshape(-1), up_bias])
    n_pair, n_qv = lheads * blocks, lheads * lanes
    extra_rows = 8
    small = jnp.pad(small, (0, extra_rows * qkv_local.shape[1] - small.shape[0]))
    first_z = z_all(jnp.concatenate([qkv_local, small.reshape(extra_rows, -1)]))
    segs = jnp.where(half == core, segments, core_swap(segments))
    ff_local = jnp.concatenate([up_weight, down_weight.T], axis=1)
    ff_local, first_z = gate(ff_local, first_z)
    ff_one = z_step(ff_local, 1)

    abs_z = xor_order([part[:drows] for part in first_z], tensor)
    qkv_cols = 3 * lheads * hs

    def regroup(first, second):
        left, right = first[:, 3 * lanes : qkv_cols], second[:, 3 * lanes : qkv_cols]
        both = [part[:, hs * k : hs * (k + 1)] for k in range(3) for part in (left, right)]
        return jnp.stack([first[:, : 3 * lanes], second[:, : 3 * lanes], jnp.concatenate(both, axis=1)])

    def with_out(first, second):
        left, right = first[:, qkv_cols:], second[:, qkv_cols:]
        out = jnp.concatenate([left[:, :lanes], right[:, :lanes], left[:, lanes:], right[:, lanes:]], axis=1)
        return jnp.concatenate([regroup(first, second), out[None]])

    zero_heads, one_heads = with_out(abs_z[0], abs_z[1]), with_out(abs_z[2], abs_z[3])
    keep = jnp.where(core == 0, zero_heads, one_heads)
    got = core_swap(jnp.where(core == 0, one_heads, zero_heads))
    chip_rows = jnp.where(
        core == 0, jnp.concatenate([keep, got], axis=1), jnp.concatenate([got, keep], axis=1)
    )
    ff_pair = jnp.stack([ff_local, ff_one])
    chip_rows, ff_pair = gate(chip_rows, ff_pair)
    qkv_pieces = chip_all(chip_rows)
    ff_middle = lax.ppermute(ff_pair, "tensor", [(1, 2), (2, 1)])

    tokens, ff_middle = gate(tokens, ff_middle)
    ff_end = lax.ppermute(ff_middle, "tensor", [(1, 0), (2, 3)])
    moved = [to_sequence(of_sequence(tokens, k), k) for k in range(2)]
    inner = (tensor == 1) | (tensor == 2)
    ff_other = jnp.where(inner, ff_middle[::-1], ff_end)
    qkv_pieces, ff_pair, ff_other, moved[0] = gate(qkv_pieces, ff_pair, ff_other, moved[0])
    out_mine = jnp.stack([piece[3] for piece in qkv_pieces])
    if aligned:
        firsts = [chip_step(ff_pair, 1), chip_step(ff_other, 2)]
        twos = [jnp.stack([ff_pair, firsts[0]]), jnp.stack([ff_other, firsts[1]])]
        cots = [of_sequence(cotangent, k) for k in range(2)]
        twos, moved, cots = gate(twos, moved, cots)
        fours = [chip_step(twos[0], 2), chip_step(twos[1], 1)]
        x_mine = jnp.concatenate(moved)
        x_other = core_swap(x_mine)
        twos_swapped = [core_swap(two) for two in twos]
        cots, x_mine, x_other, twos_swapped = gate(cots, x_mine, x_other, twos_swapped)
        cot_a, cot_b = [to_sequence(part, k) for k, part in enumerate(cots)]
    else:
        x_mine = jnp.concatenate(moved)
        x_other = core_swap(x_mine)
        cot_a, cot_b = [to_sequence(of_sequence(cotangent, k), k) for k in range(2)]
        out_other = core_swap(out_mine)
        ff_own = chip_all(jnp.concatenate([ff_pair, ff_other]))
        ff_all = [part for piece in ff_own for part in (piece, core_swap(piece))]
        qkv_pieces = [jnp.concatenate(xor_order(qkv_pieces, chip), axis=1)]
        out_both = [jnp.concatenate(xor_order(list(o), chip)) for o in (out_mine, out_other)]
        dense_pieces = [
            jnp.concatenate(
                [jnp.where(core == 0, out_both[0], out_both[1]), jnp.where(core == 0, out_both[1], out_both[0])],
                axis=1,
            ),
            jnp.concatenate(xor_order(ff_all, dp), axis=1),
        ]

    small_rel = [part[drows:].reshape(-1) for part in first_z]
    small = jnp.stack(xor_order(small_rel, tensor))
    all_pairs = small[:, :n_pair].astype(jnp.int32).reshape(2, heads, blocks)
    my_pairs = jnp.where(core == 0, all_pairs[0], all_pairs[1])
    pair_slots = jnp.stack(xor_order([my_pairs[:, k] for k in range(blocks)], slot_mask), axis=1) ^ slot_mask
    pair_slots = jnp.stack([pair_slots[h] for h in order])
    all_qvb = small[:, n_pair : n_pair + n_qv].astype(F32).reshape(2, heads, lanes)
    my_qvb = jnp.where(core == 0, all_qvb[0], all_qvb[1])
    my_qvb = jnp.stack([my_qvb[h] for h in order])
    up_bias_rel = jnp.concatenate([s[n_pair + n_qv :][:units] for s in small_rel]).astype(F32)
    groups = heads // 2
    bias = jnp.concatenate(
        [
            my_qvb[:, :hs].reshape(groups, lanes),
            jnp.zeros((groups, lanes), F32),
            my_qvb[:, hs:].reshape(groups, lanes),
        ],
        axis=1,
    ).reshape(groups, 1, 3 * lanes)

    seg_rows = jnp.where(low == 0, segs[0], segs[1]).reshape(blocks, rows)
    seg_row = jnp.concatenate(xor_order([seg_rows[k] for k in range(blocks)], slot_mask))
    seg_col = seg_row.reshape(blocks * rows, 1)
    seg_row = seg_row.reshape(1, blocks * rows)

    x_parts = [x_mine, x_other]
    q, k, v, mixed, mixed_other, lse, w_all = attend(pair_slots, place, x_parts, qkv_pieces, bias, seg_row, seg_col, hs)
    if aligned:
        q, k, v, mixed, mixed_other, lse, w_all, fours, cot_a, cot_b = gate(
            q, k, v, mixed, mixed_other, lse, w_all, fours, cot_a, cot_b
        )
        out_mine, mixed_other = gate(out_mine, mixed_other)
        out_other = core_swap(out_mine)
        dense_pieces = [out_mine, out_other] + twos + fours + twos_swapped + [core_swap(four) for four in fours]
    other = core_swap(mixed_other)

    blank = jnp.zeros((width,), BF16)
    vec = jnp.stack(
        [out_bias, first_gain, first_shift, down_bias, second_gain, second_shift, blank, blank]
    ).astype(F32)
    (
        layer_a, layer_b, gm_mine, gm_other, active, middle_low, grad_branch, grad_upper, grad_attn, grad_one, sums,
    ) = dense(
        place, dense_pieces, x_mine, mixed, other, cot_a, cot_b, vec, up_bias_rel.reshape(1, nt * units), 256
    )
    gm_got = core_swap(gm_other)
    home_0 = lax.ppermute(layer_a, BOTH, column(0, 0, True))

    def total_of(parts):
        total = parts[0].astype(F32)
        for part in parts[1:]:
            total = total + part.astype(F32)
        return total

    class Plane:
        def __init__(self, first, keep, send, got=None):
            self.first, self.got = first, got
            self.keep = self.split(keep)
            self.send = send if isinstance(send, list) else self.split(send)

        def split(self, x):
            return [x[: self.first], x[self.first :]]

        def first_sends(self):
            if self.got is None:
                return self.send
            got = self.split(self.got)
            self.keep = [[keep, g[:, :2]] for keep, g in zip(self.keep, got)]
            return [total_of([send, g[:, 2:]]).astype(BF16) for send, g in zip(self.send, got)]

        def first_moves(self, sends):
            return [chip_step(sends[0], 1), chip_step(sends[1], 2)]

        def second_sends(self, moves):
            keep = [k if isinstance(k, list) else [k] for k in self.keep]
            own = [total_of([part[:, 0] for part in k] + [m[:, 0]]) for k, m in zip(keep, moves)]
            sends = [total_of([part[:, 1] for part in k] + [m[:, 1]]).astype(BF16) for k, m in zip(keep, moves)]
            return own, sends

        def second_moves(self, sends):
            return [chip_step(sends[0], 2), chip_step(sends[1], 1)]

        def sums(self, own, moves):
            return [total_of([o, m]) for o, m in zip(own, moves)]

    class SlowPlane(Plane):
        def __init__(self, first, keep, send, got=None):
            self.first, self.view = first, keep if got is None else keep + got.astype(F32)

        def first_sends(self):
            return []

        def first_moves(self, sends):
            return []

        def second_sends(self, moves):
            return [], []

        def second_moves(self, sends):
            return []

        def sums(self, own, moves):
            pick = lambda step: lax.dynamic_index_in_dim(self.view, chip ^ step, 0, keepdims=False)
            total = total_of([pick(0)] + [chip_step(pick(step).astype(BF16), step) for step in range(1, chips)])
            return self.split(total.transpose(1, 0, 2))

    fast = chips == 4 and aligned

    def grads_of(left, right, extra, first):
        if fast:
            return weight_grad(place, left, right, extra, drows, first)
        grads = mm_lt(left, right)
        if extra:
            near, far = mm_lt(extra[0], extra[1]), mm_lt(extra[0], extra[2])
            head = [jnp.where(core == 0, near, far), jnp.where(core == 0, far, near)]
            grads = jnp.concatenate(head + [grads], axis=1)
        view = grads.reshape(chips, 2, drows, grads.shape[1] // width, width)
        ours = lax.dynamic_index_in_dim(view, core, 1, keepdims=False)
        theirs = lax.dynamic_index_in_dim(view, 1 - core, 1, keepdims=False).astype(BF16)
        return ours, theirs, theirs

    plane_of = Plane if fast else SlowPlane
    down_keep, down_send, down_theirs = grads_of(grad_branch, active, [], 2)
    down_got = core_swap(down_theirs)
    middle_low, down_keep, down_send, down_theirs, gm_got = gate(
        middle_low, down_keep, down_send, down_theirs, gm_got
    )
    up_keep, up_send, up_theirs = grads_of(middle_low, grad_upper, [grad_attn, mixed, other], 3)
    up_keep, up_send, up_theirs, home_0 = gate(up_keep, up_send, up_theirs, home_0)
    up_got = core_swap(up_theirs)

    down = plane_of(2, down_keep, down_send, down_got)
    d_sends = down.first_sends()
    pairs_0, gm_got, d_sends, layer_b = gate(pair_slots, gm_got, d_sends, layer_b)
    d_moves = down.first_moves(d_sends)
    home_1 = lax.ppermute(layer_b, BOTH, column(1, 0, True))
    packed_0, sums_0 = attend_back(pairs_0, 0, q, k, v, gm_mine, gm_got, seg_row, seg_col, lse, hs)
    packed_0, sums_0, d_moves, up_got = gate(packed_0, sums_0, d_moves, up_got)
    d_own, d_sends = down.second_sends(d_moves)
    up = plane_of(3, up_keep, up_send, up_got)
    u_sends = up.first_sends()
    pairs_1, d_own, d_sends, u_sends = gate(pair_slots, d_own, d_sends, u_sends)
    d_moves = down.second_moves(d_sends)
    u_moves = up.first_moves(u_sends)
    packed_1, sums_1 = attend_back(pairs_1, 1, q, k, v, gm_mine, gm_got, seg_row, seg_col, lse, hs)
    packed_1, sums_1, d_moves, home_1 = gate(packed_1, sums_1, d_moves, home_1)
    layer_out = at_home(home_0, home_1)
    d_first, d_second = down.sums(d_own, d_moves)
    d_second = d_second.astype(BF16)
    pair_slots, packed_1, d_first, d_second = gate(pair_slots, packed_1, d_first, d_second)
    d_second = z_step(d_second, 2)
    packed_2, sums_2 = attend_back(pair_slots, 2, q, k, v, gm_mine, gm_got, seg_row, seg_col, lse, hs)
    packed_2, sums_2, u_moves, d_second = gate(packed_2, sums_2, u_moves, d_second)
    d_keep = total_of([d_first[0], d_second[0]])
    d_give = total_of([d_first[1], d_second[1]]).astype(BF16)
    u_own, u_sends = up.second_sends(u_moves)

    head_sums = jnp.concatenate([part[row] for row in range(2) for part in (sums_0, sums_1, sums_2)])[None]
    blank = jnp.zeros_like(head_sums)
    sums = jnp.concatenate(
        [
            sums[:12],
            jnp.where(core == 0, head_sums, blank),
            jnp.where(core == 0, blank, head_sums),
            jnp.zeros((2, width), F32),
        ]
    )
    packed_2, d_keep, d_give, u_own, u_sends, sums = gate(packed_2, d_keep, d_give, u_own, u_sends, sums)
    packed = [packed_0, packed_1, packed_2]
    d_give = z_step(d_give, 1)
    sums_got = z_step(sums, 1)
    u_moves = up.second_moves(u_sends)
    in_mine, in_other = in_grad(packed, w_all, grad_one)
    in_mine, in_other, sums_got, packed, d_give, u_moves = gate(
        in_mine, in_other, sums_got, packed, d_give, u_moves
    )
    in_got = core_swap(in_other)
    down_grad = (d_keep + d_give.astype(F32)).T
    sums = sums + sums_got
    u_first, u_second = up.sums(u_own, u_moves)
    out_near = jnp.where(half == 0, u_first[0, :, :cols], u_first[0, :, cols:])
    out_far = jnp.where(half == 0, u_first[0, :, cols:], u_first[0, :, :cols])
    u_first = u_first[1:]
    u_second = jnp.concatenate([u_second[0], u_second[1], out_far], axis=1).astype(BF16)
    in_got, sums, u_first, u_second, out_near = gate(in_got, sums, u_first, u_second, out_near)
    u_second = z_step(u_second, 2)
    sums_got = z_step(sums, 2)
    in_low = [total_of([part[rows * k : rows * (k + 1)] for part in (in_mine, in_got)]).astype(BF16) for k in range(2)]
    packed, in_low = gate(packed, in_low)
    homes = [lax.ppermute(part, BOTH, column(k, 0, True)) for k, part in enumerate(in_low)]
    if fast:
        qkv_keep, *qkv_send = qkv_grads(place, x_parts, packed, 2 * drows)
    else:
        parts = [mm_lt(jnp.concatenate(x_parts), packed[g]).reshape(chips, 2 * drows, 3 * lanes) for g in (0, 2, 1)]
        qkv_keep = qkv_send = jnp.stack(parts, axis=2)
    qkv_keep, qkv_send, u_second, sums_got = gate(qkv_keep, qkv_send, u_second, sums_got)
    sums = sums + sums_got
    qkv = plane_of(2, qkv_keep, qkv_send)
    a_moves = qkv.first_moves(qkv.first_sends())
    u_keep, u_give = [total_of([u_first[j], u_second[:, units * j : units * (j + 1)]]) for j in range(2)]
    out_near = total_of([out_near, u_second[:, 2 * units :]])

    def out_unit(wanted_low):
        parts = [
            jnp.concatenate(
                [out_near[:, lanes * w : lanes * (w + 1)], out_near[:, 2 * lanes + hs * w : 2 * lanes + hs * (w + 1)]],
                axis=1,
            )
            for w in range(2)
        ]
        return jnp.where(wanted_low == 0, parts[0], parts[1])

    u_give = jnp.concatenate([u_give, out_unit(1 - low)], axis=1).astype(BF16)
    out_near = out_unit(low)
    u_give = z_step(u_give, 1)
    a_own, a_sends = qkv.second_sends(a_moves)
    a_moves = qkv.second_moves(a_sends)
    up_grad = total_of([u_keep, u_give[:, :units]])
    out_grad = total_of([out_near, u_give[:, units:]]).T.reshape(lheads, hs, drows)
    homes, a_moves, sums = gate(homes, a_moves, sums)
    sums = sums + core_swap(sums)
    for bit in range(chips.bit_length() - 1):
        sums = sums + chip_step(sums, 1 << bit)
    outb_grad, gain_one_grad, shift_one_grad, downb_grad, gain_two_grad, shift_two_grad = [
        sums[row] for row in range(6)
    ]
    upb_grad = lax.dynamic_index_in_dim(sums, 8 + tensor, 0, keepdims=False)
    head_row = jnp.where(half == 0, sums[12], sums[13]).reshape(2, 6, hs)
    qvb_grad = jnp.where(low == 0, head_row[:, [0, 1, 4]], head_row[:, [2, 3, 5]])
    qvb_grad = jnp.concatenate([qvb_grad[0], qvb_grad[1]], axis=1)

    input_grad = at_home(*homes)
    sum_a, sum_b = qkv.sums(a_own, a_moves)
    sum_0, sum_2, sum_1 = [part.reshape(2, drows, 3 * lanes) for part in (sum_a[0], sum_a[1], sum_b[0])]
    sum_01 = [sum_0, sum_1]

    def share(c, u):
        third = [sum_2[c][:, lanes * k + hs * u : lanes * k + hs * (u + 1)] for k in range(3)]
        return jnp.concatenate([sum_01[u][c]] + third, axis=1)

    shares = [[share(c, u).astype(BF16) for u in range(2)] for c in range(2)]
    qkv_grad = jnp.zeros((drows, 3 * lheads * hs), F32)
    for flip in range(2):
        for step in range(2):
            by_core = [jnp.where((low ^ step) == 0, shares[c][0], shares[c][1]) for c in range(2)]
            sent = jnp.where((half ^ flip) == 0, by_core[0], by_core[1])
            qkv_grad = qkv_grad + lax.ppermute(sent, BOTH, column(step, flip, False)).astype(F32)
    pairs_part = qkv_grad[:, : 3 * lanes].reshape(drows, 3, 2, hs)
    third_part = qkv_grad[:, 3 * lanes :].reshape(drows, 3, 1, hs)
    qkv_grad = jnp.concatenate([pairs_part, third_part], axis=2).transpose(0, 2, 1, 3)
    qkv_grad = qkv_grad.reshape(drows, lheads, 3 * hs)
    return (
        layer_out,
        input_grad,
        qkv_grad,
        qvb_grad,
        out_grad,
        outb_grad,
        gain_one_grad,
        shift_one_grad,
        up_grad,
        upb_grad,
        down_grad,
        downb_grad,
        gain_two_grad,
        shift_two_grad,
    )


def solution(mesh):
    return jax.shard_map(
        per_device,
        mesh=mesh,
        in_specs=(
            P("dp", "tensor", None),
            P("dp", None),
            P("tensor", None),
            P("dp", "tensor", None),
            P("tensor", None),
            P("tensor", None, "dp"),
            P(),
            P(),
            P(),
            P("dp", "tensor"),
            P("tensor"),
            P("tensor", "dp"),
            P(),
            P(),
            P(),
            P("dp", "tensor", None),
        ),
        out_specs=(
            P("dp", "tensor", None),
            P("dp", "tensor", None),
            P("dp", "tensor", None),
            P("tensor", None),
            P("tensor", None, "dp"),
            P(),
            P(),
            P(),
            P("dp", "tensor"),
            P("tensor"),
            P("tensor", "dp"),
            P(),
            P(),
            P(),
        ),
        check_vma=False,
    )
```
